32 devices in a mesh: groups: 2 (over x), tm: 8 (over z, y), mp: 2 (over core).
Axes of the slice: x: 2, y: 2, z: 4, core: 2. Of those that a mesh axis runs over, the one named last changes fastest.
Arguments:
- frames: bfloat16 [8192, 1024], P(('groups', 'tm')), parts along dimension 0, may hold values from -6 to 6
- weight_qkv: bfloat16 [1024, 3, 1024], P(None, None, 'mp'), as said below
- weight_out: bfloat16 [1024, 1024], P('mp'), may hold values from -0.1875 to 0.1875
- proj_in: bfloat16 [1024, 8192], P('tm', 'mp'), may hold values from -0.1875 to 0.1875
- norm_gain: float32 [8192], P('mp'), may hold values from 0.28 to 2.8, as said below
- proj_kv: bfloat16 [8192, 2048], P(('mp', 'tm')), may hold values from -0.0625 to 0.0625
- shifts: int32 [256], replicated, may hold values from 0 to 255, each once
- route: int32 [8, 8], replicated, may hold values from 0 to 7, each once within a row
- d_kv: bfloat16 [2048, 2048], P(('groups', 'tm'), 'mp'), parts along dimension 0, may hold values from -3 to 3
Outputs:
- kv: bfloat16 [2048, 2048], P(('groups', 'tm'), 'mp'), parts along dimension 0
- grad_qkv: float32 [2048, 3, 1024], P(('groups', 'tm'), None, 'mp'), parts along dimension 0
- grad_out: float32 [2048, 1024], P(('groups', 'mp', 'tm')), parts along dimension 0
The draws below stay inside these ranges and needn't reach their ends.
There are 2 independent parts, one for each index of `groups`. The reference program is written for one: setup_inputs(seed, part) draws one part's arguments, and reference() takes and returns one part's arrays. A program takes and returns all parts, laid end to end along the dimension named above; an argument that names none is the same for every part. Nothing has to cross between parts.
Inputs may be any that keep to these rules, and one draw needn't show every extreme that they name: Row d of route is a permutation: it names each owner for exactly one piece of source d. shifts is a permutation of the whole numbers 0 to 255. `weight_qkv`: entries of order 1024**-0.5 times a few. `norm_gain`: positive gains.
All inputs are finite; a program needn't handle non-finite values.
Results may differ from the reference program's by a relative error of at most 0.02.
Values may be sent and summed in bfloat16 or wider, within the bound.
No kernel may reach another device: no remote copies, remote signals or barrier semaphores. Data moves between devices by JAX's collectives and lax.ppermute only.
A program may use at most 128 MiB of HBM per device.

```python
import jax
import jax.numpy as jnp
from jax import lax

D_ENC = 1024
HEADS = 16
HEAD = 64
WINDOW = 256
POOL = 4
LLM_D = 8192
KV_WIDTH = 2048
FRAMES = 4096
TOKENS = 1024
SOURCES = 8
PIECE = 16


def draw_weight_qkv(key, part):
    base = jax.random.normal(key, (D_ENC, 3, D_ENC), jnp.float32) * D_ENC ** (-0.5)
    return base.astype(jnp.bfloat16)


def draw_norm_gain(key, part):
    place = jnp.arange(LLM_D, dtype=jnp.float32) / (LLM_D - 1)
    fresh = jax.random.fold_in(key, 4243)
    low_end = 0.5
    high_end = 1.5
    rough = jax.random.uniform(fresh, (LLM_D,), jnp.float32, 0.8, 1.25)
    trend = jnp.exp(jnp.log(low_end) + place * (jnp.log(high_end) - jnp.log(low_end)))
    return trend * rough


def spiked(drawn, rng, source, target, shards_of, factor):
    owner, partner = [(jnp.arange(drawn.shape[axis_at]) // (drawn.shape[axis_at] // shards_of)).reshape([-1 if axis == axis_at else 1 for axis in range(drawn.ndim)]) for axis_at in (source, target)]
    chosen = jax.random.permutation(rng, shards_of)[partner]
    strong = (owner == chosen) | (owner == (partner + shards_of // 2) % shards_of)
    return jnp.where(strong, factor * drawn, drawn)


def block_levels(key, extent, split, smallest, top_value):
    gain = 1.0
    for axis_at, blocks in split:
        steps = jax.random.uniform(jax.random.fold_in(jax.random.fold_in(key, 6), axis_at), (blocks,), jnp.float32, smallest / len(split), top_value / len(split))
        gain = gain * jnp.repeat(jnp.exp(steps), extent[axis_at] // blocks).reshape((-1,) + (1,) * (len(extent) - 1 - axis_at))
    return gain


def bell_draw(key, dims, width, bound, shards=(), kind=jnp.bfloat16):
    entries = width * jax.random.normal(key, dims, jnp.float32)
    if shards:
        entries = entries * block_levels(key, dims, shards, -0.22, 0.18)
    return jnp.clip(entries, -bound, bound).astype(kind)


def noise_with(key, extent, scale, reach, split, heavy, held_as=jnp.bfloat16):
    values = scale * jax.random.normal(key, extent, jnp.float32)
    if split:
        values = values * block_levels(key, extent, split, -0.22, 0.18)
    return jnp.clip(spiked(values, jax.random.fold_in(key, 3), *heavy), -reach, reach).astype(held_as)


def setup_inputs(seed: int = 0, part: int = 0) -> dict:
    keys = jax.random.split(jax.random.key(seed), 10)
    part_keys = jax.random.split(jax.random.fold_in(keys[9], part), 10)
    frames = noise_with(part_keys[0], (FRAMES, D_ENC), 1.0, 6.0, ((0, 8),), (0, 1, 8, 2.0))
    weight_qkv = draw_weight_qkv(jax.random.fold_in(keys[9], 71), part)
    weight_out = bell_draw(keys[2], (D_ENC, D_ENC), D_ENC ** -0.5, 0.1875, ((0, 2),))
    proj_in = bell_draw(keys[3], (D_ENC, LLM_D), D_ENC ** -0.5, 0.1875, ((0, 8), (1, 2)))
    norm_gain = draw_norm_gain(jax.random.fold_in(keys[9], 71), part)
    proj_kv = bell_draw(keys[5], (LLM_D, KV_WIDTH), LLM_D ** -0.5, 0.0625, ((0, 16),))
    shifts = jax.random.permutation(keys[6], WINDOW).astype(jnp.int32)
    route = jax.vmap(lambda own: jax.random.permutation(own, SOURCES))(jax.random.split(keys[7], SOURCES)).reshape((SOURCES, SOURCES)).astype(jnp.int32)
    d_kv = bell_draw(part_keys[8], (TOKENS, KV_WIDTH), 0.2, 3.0, ((0, 8), (1, 2)))
    return {"frames": frames, "weight_qkv": weight_qkv, "weight_out": weight_out, "proj_in": proj_in, "norm_gain": norm_gain, "proj_kv": proj_kv, "shifts": shifts, "route": route, "d_kv": d_kv}


def rms_normed(values):
    return values * lax.rsqrt(lax.optimization_barrier(jnp.mean(values * values, axis=-1, keepdims=True)) + 1e-05)

def window_forward(block, row_label):
    queries = block[:, 0].astype(jnp.float32)
    keys_part = block[:, 1].astype(jnp.float32)
    values_part = block[:, 2].astype(jnp.float32)
    scores = jnp.einsum('qhd,khd->hqk', queries, keys_part) * HEAD ** (-0.5)
    allowed = row_label[:, None] == row_label[None, :]
    scores = jnp.where(allowed[None], scores, -1e+30)
    top_score = lax.optimization_barrier(jnp.max(scores, axis=-1, keepdims=True))
    exponent_terms = jnp.exp(scores - top_score)
    softmax_probs = exponent_terms / lax.optimization_barrier(jnp.sum(exponent_terms, axis=-1, keepdims=True))
    weights_low = softmax_probs.astype(jnp.bfloat16)
    attended = jnp.einsum('hqk,khd->qhd', weights_low.astype(jnp.float32), values_part)
    return (attended.astype(jnp.bfloat16), softmax_probs, weights_low)

def window_backward(block, softmax_probs, weights_low, grads_in):
    queries = block[:, 0].astype(jnp.float32)
    keys_part = block[:, 1].astype(jnp.float32)
    values_part = block[:, 2].astype(jnp.float32)
    grads_out = grads_in.astype(jnp.float32)
    d_weights = jnp.einsum('qhd,khd->hqk', grads_out, values_part)
    d_values = jnp.einsum('hqk,qhd->khd', weights_low.astype(jnp.float32), grads_out).astype(jnp.bfloat16)
    centre = lax.optimization_barrier(jnp.sum(softmax_probs * d_weights, axis=-1, keepdims=True))
    d_scores = (softmax_probs * (d_weights - centre) * HEAD ** (-0.5)).astype(jnp.bfloat16)
    d_queries = jnp.einsum('hqk,khd->qhd', d_scores.astype(jnp.float32), keys_part).astype(jnp.bfloat16)
    d_keys = jnp.einsum('hqk,qhd->khd', d_scores.astype(jnp.float32), queries).astype(jnp.bfloat16)
    return jnp.stack([d_queries, d_keys, d_values], axis=1)

def reference(frames, weight_qkv, weight_out, proj_in, norm_gain, proj_kv, shifts, route, d_kv):
    shift_rows = shifts[0]
    x_full = frames.astype(jnp.float32)
    normed = rms_normed(x_full).astype(jnp.bfloat16)
    qkv = jnp.dot(normed, weight_qkv.reshape(D_ENC, 3 * D_ENC), preferred_element_type=jnp.float32).astype(jnp.bfloat16)
    rolled = jnp.roll(qkv, -shift_rows, axis=0)
    wrapped = (jnp.arange(FRAMES, dtype=jnp.int32) >= FRAMES - shift_rows).astype(jnp.int32)
    blocks = rolled.reshape(FRAMES // WINDOW, WINDOW, 3, HEADS, HEAD)
    labels = wrapped.reshape(FRAMES // WINDOW, WINDOW)

    def forward_one(pair):
        attended, probs_unused, weights_unused = window_forward(pair[0], pair[1])
        return attended
    rolled_attn = lax.map(forward_one, (blocks, labels)).reshape(FRAMES, D_ENC)
    attn = jnp.roll(rolled_attn, shift_rows, axis=0)
    encoded = (x_full + jnp.dot(attn, weight_out, preferred_element_type=jnp.float32)).astype(jnp.bfloat16)
    pooled = encoded.astype(jnp.float32).reshape(FRAMES // POOL, POOL, D_ENC).mean(axis=1).astype(jnp.bfloat16)
    sources = pooled.reshape(SOURCES, SOURCES, PIECE, D_ENC)
    inverse = jnp.argsort(route, axis=1).astype(jnp.int32)
    source_ids = jnp.arange(SOURCES, dtype=jnp.int32)
    tokens = sources[source_ids[None, :], inverse.T].reshape(TOKENS, D_ENC)
    lifted = jnp.dot(tokens, proj_in, preferred_element_type=jnp.float32)
    inv_rms = lax.rsqrt(lax.optimization_barrier(jnp.mean(lifted * lifted, axis=-1, keepdims=True)) + 1e-05)
    llm_normed = (lifted * inv_rms * norm_gain).astype(jnp.bfloat16)
    kv = jnp.dot(llm_normed, proj_kv, preferred_element_type=jnp.float32).astype(jnp.bfloat16)
    d_kv_total = (kv.astype(jnp.float32) + d_kv.astype(jnp.float32)).astype(jnp.bfloat16)
    d_normed = jnp.dot(d_kv_total, proj_kv.T, preferred_element_type=jnp.float32)
    inner = lax.optimization_barrier(jnp.sum(lifted * norm_gain * d_normed, axis=-1, keepdims=True))
    d_lifted = (inv_rms * norm_gain * d_normed - lifted * inv_rms ** 3 * inner / LLM_D).astype(jnp.bfloat16)
    d_tokens = jnp.dot(d_lifted, proj_in.T, preferred_element_type=jnp.float32).astype(jnp.bfloat16)
    d_tokens = d_tokens.reshape(SOURCES, SOURCES, PIECE, D_ENC)
    d_sources = d_tokens[route, source_ids[:, None]]
    d_pooled = d_sources.reshape(FRAMES // POOL, D_ENC)
    d_encoded = (jnp.repeat(d_pooled, POOL, axis=0).astype(jnp.float32) * (1.0 / POOL)).astype(jnp.bfloat16)
    grad_out = jnp.dot(attn.T, d_encoded, preferred_element_type=jnp.float32)
    d_attn = jnp.dot(d_encoded, weight_out.T, preferred_element_type=jnp.float32).astype(jnp.bfloat16)
    d_rolled = jnp.roll(d_attn, -shift_rows, axis=0).reshape(FRAMES // WINDOW, WINDOW, HEADS, HEAD)

    def backward_one(triple):
        attended, softmax_probs, weights_low = window_forward(triple[0], triple[1])
        return window_backward(triple[0], softmax_probs, weights_low, triple[2])
    d_rolled_qkv = lax.map(backward_one, (blocks, labels, d_rolled)).reshape(FRAMES, 3 * D_ENC)
    d_qkv = jnp.roll(d_rolled_qkv, shift_rows, axis=0)
    grad_qkv = jnp.dot(normed.T, d_qkv, preferred_element_type=jnp.float32).reshape(D_ENC, 3, D_ENC)
    return (kv, grad_qkv, grad_out)
```

```python
import jax
import jax.numpy as jnp
from jax import lax
from jax.sharding import PartitionSpec as P

HEAD = 64
WINDOW = 256
POOL = 4
LLM_D = 8192
BF = jnp.bfloat16
F32 = jnp.float32


def dot(a, b):
    return jnp.dot(a, b, preferred_element_type=F32)


def dot_nt(a, b):
    return lax.dot_general(a, b, (((1,), (1,)), ((), ())), preferred_element_type=F32)


def dot_tn(a, b):
    return lax.dot_general(a, b, (((0,), (0,)), ((), ())), preferred_element_type=F32)


def swap_tm(block, mask):
    n = lax.axis_size("tm")
    return lax.ppermute(block, "tm", [(i, i ^ mask) for i in range(n)])


def swap_mp(block):
    n = lax.axis_size("mp")
    return lax.ppermute(block, "mp", [(i, n - 1 - i) for i in range(n)])


def to_tm(block, step, cross):
    n, m = lax.axis_size("tm"), lax.axis_size("mp")
    pairs = []
    for i in range(n):
        for c in range(m):
            pairs.append((i * m + c, (i + step) % n * m + (m - 1 - c if cross else c)))
    return lax.ppermute(block, ("tm", "mp"), pairs)


def gather_xor(block):
    n = lax.axis_size("tm")
    parts = [None] * n
    parts[0] = block
    for k in range(2, n, 2):
        parts[k] = swap_tm(block, k)
    parts[1] = swap_tm(block, 1)
    for k in range(2, n, 2):
        parts[k + 1] = swap_tm(parts[k], 1)
    return parts


def scatter_xor(even, odd):
    got = swap_tm(odd, 1)
    half = even.astype(F32) + got.astype(F32)
    low = half.astype(BF)
    total = half[0]
    for j in range(1, even.shape[0]):
        total = total + swap_tm(low[j], 2 * j).astype(F32)
    return total


def scatter_natural(blocks, me):
    n = blocks.shape[0]
    rest = blocks.shape[1:]
    paired = blocks.reshape((n // 2, 2) + rest)
    low_bit = me % 2
    keep = lax.dynamic_index_in_dim(paired, low_bit, 1, keepdims=False)
    send = lax.dynamic_index_in_dim(paired, 1 - low_bit, 1, keepdims=False)
    half = (keep.astype(F32) + swap_tm(send, 1).astype(F32)).astype(BF)
    high = me // 2
    total = lax.dynamic_index_in_dim(half, high, 0, keepdims=False).astype(F32)
    for j in range(1, n // 2):
        piece = lax.dynamic_index_in_dim(half, high ^ j, 0, keepdims=False)
        total = total + swap_tm(piece, 2 * j).astype(F32)
    return total


def small_scatter(rows):
    total = rows + swap_mp(rows)
    n = rows.shape[0]
    while n > 1:
        n //= 2
        total = total[:n] + swap_tm(total[n:], n)
    return total


def small_gather(row):
    n = 1
    while n < lax.axis_size("tm"):
        row = jnp.concatenate([row, swap_tm(row, n)], axis=0)
        n *= 2
    return row


def split_heads(rolled):
    rows = rolled.shape[0]
    heads = rolled.shape[1] // (3 * HEAD)
    split = rolled.reshape(rows // WINDOW, WINDOW, 3, heads, HEAD)
    return split[:, :, 0], split[:, :, 1], split[:, :, 2]


def window_forward(rolled, row_label):
    rows = rolled.shape[0]
    queries, keys_part, values_part = split_heads(rolled)
    scores = jnp.einsum(
        "wqhd,wkhd->whqk", queries, keys_part, preferred_element_type=F32
    ) * HEAD ** (-0.5)
    labels = row_label.reshape(rows // WINDOW, WINDOW)
    allowed = labels[:, :, None] == labels[:, None, :]
    scores = jnp.where(allowed[:, None], scores, -1e30)
    top_score = jnp.max(scores, axis=-1, keepdims=True)
    exponent_terms = jnp.exp(scores - top_score)
    probs = exponent_terms / jnp.sum(exponent_terms, axis=-1, keepdims=True)
    weights_low = probs.astype(BF)
    attended = jnp.einsum("whqk,wkhd->wqhd", weights_low, values_part, preferred_element_type=F32)
    return attended.astype(BF).reshape(rows, -1), probs, weights_low


def window_backward(rolled, probs, weights_low, d_rolled):
    rows = rolled.shape[0]
    queries, keys_part, values_part = split_heads(rolled)
    grads_out = d_rolled.reshape(queries.shape)
    d_weights = jnp.einsum("wqhd,wkhd->whqk", grads_out, values_part, preferred_element_type=F32)
    d_values = jnp.einsum("whqk,wqhd->wkhd", weights_low, grads_out, preferred_element_type=F32)
    centre = jnp.sum(probs * d_weights, axis=-1, keepdims=True)
    d_scores = (probs * (d_weights - centre) * HEAD ** (-0.5)).astype(BF)
    d_queries = jnp.einsum("whqk,wkhd->wqhd", d_scores, keys_part, preferred_element_type=F32)
    d_keys = jnp.einsum("whqk,wqhd->wkhd", d_scores, queries, preferred_element_type=F32)
    return jnp.stack([d_queries, d_keys, d_values], axis=2).reshape(rows, -1)


def on_device(frames, weight_qkv, weight_out, proj_in, norm_gain, proj_kv, shifts, route, d_kv):
    n = lax.axis_size("tm")
    me = lax.axis_index("tm")
    core = lax.axis_index("mp")
    rows, width = frames.shape
    half_w = width // 2
    shift = shifts[0]
    own_tok = rows // POOL
    tail_tok = WINDOW // POOL
    ext_tok = own_tok + tail_tok
    feats = proj_kv.shape[0]
    kv_half = proj_kv.shape[1] // 2
    piece = own_tok // n

    part = lax.dynamic_slice_in_dim(frames, core * (WINDOW // 2), WINDOW // 2, 0)
    mine = to_tm(part, -1, False)
    other = swap_mp(mine)
    halo = jnp.where(
        core == 0, jnp.concatenate([mine, other], 0), jnp.concatenate([other, mine], 0)
    )
    x_roll = lax.dynamic_slice_in_dim(jnp.concatenate([frames, halo], 0), shift, rows, 0)

    blocks = [lax.dynamic_slice_in_dim(proj_in, me * feats, feats, 1)]
    for k in range(1, n):
        blocks.append(swap_tm(lax.dynamic_slice_in_dim(proj_in, (me ^ k) * feats, feats, 1), k))
    lift_w = jnp.take(jnp.stack(blocks), me ^ jnp.arange(n, dtype=jnp.int32), axis=0)
    lift_w = lift_w.reshape(width, feats)
    gain = lax.dynamic_slice_in_dim(norm_gain, me * feats, feats, 0)

    w_t = jnp.transpose(weight_qkv, (1, 2, 0)).reshape(-1, width)
    x32 = x_roll.astype(F32)
    scale = lax.rsqrt(jnp.mean(x32 * x32, axis=-1, keepdims=True) + 1e-05)
    rolled = (dot_nt(x_roll, w_t) * scale).astype(BF)
    position = me * rows + jnp.arange(rows, dtype=jnp.int32)
    row_label = (position >= rows * n - shift).astype(jnp.int32)
    rolled_attn, probs, weights_low = window_forward(rolled, row_label)

    tok_of = (shift + jnp.arange(rows, dtype=jnp.int32)) // POOL
    member = tok_of[None, :] == jnp.arange(ext_tok, dtype=jnp.int32)[:, None]
    pool = member.astype(BF) * (1.0 / POOL)
    pooled_attn = dot(pool, rolled_attn).astype(BF)
    out_part = dot(pooled_attn, weight_out)
    out_low = out_part.astype(BF)
    low_own = lax.dynamic_slice_in_dim(out_low, core * half_w, half_w, 1)
    low_other = lax.dynamic_slice_in_dim(out_low, (1 - core) * half_w, half_w, 1)
    from_core = swap_mp(low_other[:own_tok])
    tail_a = to_tm(low_own[own_tok:], 1, False)
    tail_b = to_tm(low_other[own_tok:], 1, True)
    own_pool = (
        jnp.arange(rows, dtype=jnp.int32)[None, :] // POOL
        == jnp.arange(own_tok, dtype=jnp.int32)[:, None]
    ).astype(BF) * (1.0 / POOL)
    x_mean = dot(own_pool, lax.dynamic_slice_in_dim(frames, core * half_w, half_w, 1))
    pooled = (
        x_mean
        + lax.dynamic_slice_in_dim(out_part, core * half_w, half_w, 1)[:own_tok]
        + from_core.astype(F32)
    )
    tail = tail_a.astype(F32) + tail_b.astype(F32)
    pooled = jnp.concatenate([pooled[:tail_tok] + tail, pooled[tail_tok:]], 0).astype(BF)

    tok_half = jnp.concatenate(gather_xor(pooled), 0)
    tok_other = swap_mp(tok_half)
    inverse = jnp.argsort(route, axis=1).astype(jnp.int32)
    owners = me ^ jnp.arange(n, dtype=jnp.int32)
    sources = jnp.arange(n, dtype=jnp.int32)
    piece_at = (sources[None, :] ^ me) * n + inverse.T[owners]
    row_at = (piece_at[:, :, None] * piece + jnp.arange(piece, dtype=jnp.int32)).reshape(-1)
    tok = jnp.concatenate([tok_half, tok_other], 1)
    tok = jnp.take(tok, row_at, axis=0)
    lift_own = jnp.concatenate(
        [
            lax.dynamic_slice_in_dim(lift_w, core * half_w, half_w, 0),
            lax.dynamic_slice_in_dim(lift_w, (1 - core) * half_w, half_w, 0),
        ],
        0,
    )
    lifted = dot(tok, lift_own)
    squares = jnp.sum(lifted * lifted, axis=-1).reshape(n, own_tok)
    square_sum = small_scatter(squares)
    inv_rms = lax.rsqrt(square_sum / LLM_D + 1e-05)
    scaled = (lifted * gain).astype(BF)
    kv_w_own = lax.dynamic_slice_in_dim(proj_kv, core * kv_half, kv_half, 1)
    kv_w_other = lax.dynamic_slice_in_dim(proj_kv, (1 - core) * kv_half, kv_half, 1)
    from_core = swap_mp(dot(scaled, kv_w_other).astype(BF))
    kv_part = (dot(scaled, kv_w_own) + from_core.astype(F32)).astype(BF)
    kv_part = kv_part.reshape(n // 2, 2, own_tok, kv_half)
    kv_sum = scatter_xor(kv_part[:, 0], kv_part[:, 1])
    kv = (kv_sum * inv_rms.reshape(own_tok, 1)).astype(BF)
    total_cot = (kv.astype(F32) + d_kv.astype(F32)).astype(BF)
    inner = jnp.sum(total_cot.astype(F32) * kv_sum, axis=-1).reshape(1, own_tok)
    inner = inner + swap_mp(inner)
    stats = small_gather(jnp.stack([inv_rms, inner], axis=1))
    inv_all = stats[:, 0].reshape(-1, 1)
    inner_all = stats[:, 1].reshape(-1, 1)
    cot_half = jnp.concatenate(gather_xor(total_cot), 0)
    cot_other = swap_mp(cot_half)
    d_normed = dot_nt(cot_half, kv_w_own) + dot_nt(cot_other, kv_w_other)
    d_lifted = (inv_all * gain * d_normed - lifted * (inv_all**3 * inner_all / LLM_D)).astype(BF)
    d_tok = dot_nt(d_lifted, lift_own).astype(BF)
    slot_of = (
        jnp.arange(n, dtype=jnp.int32)[None, :] * 0
        + (route[sources ^ me] ^ me) * n
        + (sources ^ me)[:, None]
    )
    back_at = (slot_of[:, :, None] * piece + jnp.arange(piece, dtype=jnp.int32)).reshape(-1)
    d_tok = jnp.take(d_tok, back_at, axis=0)
    from_core = swap_mp(d_tok[:, half_w:])
    d_part = (d_tok[:, :half_w].astype(F32) + from_core.astype(F32)).astype(BF)
    d_part = d_part.reshape(n // 2, 2, own_tok, half_w)
    d_half = scatter_xor(d_part[:, 0], d_part[:, 1]).astype(BF)

    d_other = swap_mp(d_half)
    next_a = to_tm(d_half[:tail_tok], -1, False)
    next_b = to_tm(d_half[:tail_tok], -1, True)
    left = jnp.concatenate([d_half, next_a], 0)
    right = jnp.concatenate([d_other, next_b], 0)
    d_ext = jnp.where(
        core == 0, jnp.concatenate([left, right], 1), jnp.concatenate([right, left], 1)
    )
    grad_out = scatter_natural(
        dot_tn(pooled_attn, d_ext).astype(BF).reshape(n, -1, width), me
    )
    d_attn = (dot_nt(d_ext, weight_out) * (1.0 / POOL)).astype(BF)
    d_rolled_attn = dot_tn(member.astype(BF), d_attn).astype(BF)
    d_rolled = (window_backward(rolled, probs, weights_low, d_rolled_attn) * scale).astype(BF)
    grad_qkv = scatter_natural(
        dot_tn(x_roll, d_rolled).astype(BF).reshape(n, width // n, -1), me
    )
    return kv, grad_qkv.reshape(width // n, 3, -1), grad_out


def solution(mesh):
    in_specs = (
        P(("groups", "tm"), None),
        P(None, None, "mp"),
        P("mp", None),
        P("tm", "mp"),
        P("mp"),
        P(("mp", "tm"), None),
        P(),
        P(),
        P(("groups", "tm"), "mp"),
    )
    out_specs = (
        P(("groups", "tm"), "mp"),
        P(("groups", "tm"), None, "mp"),
        P(("groups", "mp", "tm"), None),
    )
    return jax.shard_map(
        on_device, mesh=mesh, in_specs=in_specs, out_specs=out_specs, check_vma=False
    )
```

```python
import functools

import jax
import jax.numpy as jnp
from jax import lax
from jax.experimental import pallas as pl
from jax.experimental.pallas import tpu as pltpu
from jax.sharding import PartitionSpec as P

HEAD = 64
WINDOW = 256
POOL = 4
LLM_D = 8192
BF = jnp.bfloat16
F32 = jnp.float32
VMEM_LIMIT = 48 << 20


def dot(a, b):
    return jnp.dot(a, b, preferred_element_type=F32)


def dot_nt(a, b):
    return lax.dot_general(a, b, (((1,), (1,)), ((), ())), preferred_element_type=F32)


def dot_tn(a, b):
    return lax.dot_general(a, b, (((0,), (0,)), ((), ())), preferred_element_type=F32)


def swap_tm(block, mask):
    n = lax.axis_size("tm")
    return lax.ppermute(block, "tm", [(i, i ^ mask) for i in range(n)])


def swap_mp(block):
    n = lax.axis_size("mp")
    return lax.ppermute(block, "mp", [(i, n - 1 - i) for i in range(n)])


def to_tm(block, step, cross):
    n, m = lax.axis_size("tm"), lax.axis_size("mp")
    pairs = []
    for i in range(n):
        for c in range(m):
            pairs.append((i * m + c, (i + step) % n * m + (m - 1 - c if cross else c)))
    return lax.ppermute(block, ("tm", "mp"), pairs)


def gather_xor(block):
    n = lax.axis_size("tm")
    parts = [None] * n
    parts[0] = block
    for k in range(2, n, 2):
        parts[k] = swap_tm(block, k)
    parts[1] = swap_tm(block, 1)
    for k in range(2, n, 2):
        parts[k + 1] = swap_tm(parts[k], 1)
    return parts


def scatter_xor(even, odd):
    got = swap_tm(odd, 1)
    half = even.astype(F32) + got.astype(F32)
    low = half.astype(BF)
    total = half[0]
    for j in range(1, even.shape[0]):
        total = total + swap_tm(low[j], 2 * j).astype(F32)
    return total


def halving_order(n):
    order, bit = [0], n // 2
    while bit > 1:
        order = order + [k | bit for k in order]
        bit //= 2
    return order


def scatter_halving(even, odd):
    n = lax.axis_size("tm")
    total = even.astype(F32) + swap_tm(odd, 1).astype(F32)
    mask = 2
    while mask < n:
        low = total.astype(BF)
        half = low.shape[0] // 2
        total = low[:half].astype(F32) + swap_tm(low[half:], mask).astype(F32)
        mask *= 2
    return total[0]


def small_scatter(rows):
    total = rows + swap_mp(rows)
    n = rows.shape[0]
    while n > 1:
        n //= 2
        total = total[:n] + swap_tm(total[n:], n)
    return total


def small_gather(row):
    n = 1
    while n < lax.axis_size("tm"):
        row = jnp.concatenate([row, swap_tm(row, n)], axis=0)
        n *= 2
    return row


def head_mask(shape, head):
    return lax.broadcasted_iota(jnp.int32, shape, 1) // HEAD == head


def forward_kernel(at, x_ref, wq_ref, wk_ref, wv_ref, wo_ref, normed, qkv, probs, pooled, out, attn):
    shift, border = at[0], at[1]
    rows = x_ref.shape[0]
    cols = wq_ref.shape[0]

    @pl.when(pl.program_id(0) == 0)
    def _():
        x = x_ref[...].astype(F32)
        scale = lax.rsqrt(jnp.mean(x * x, axis=-1, keepdims=True) + 1e-05)
        normed[...] = (x * scale).astype(BF)
        out[...] = jnp.zeros_like(out)

    base = normed[...]
    for i, w_ref in enumerate((wq_ref, wk_ref, wv_ref)):
        qkv[i] = dot_nt(base, w_ref[...]).astype(BF)
    for w in range(rows // WINDOW):
        span = pl.ds(w * WINDOW, WINDOW)
        q, k, v = qkv[0, span, :], qkv[1, span, :], qkv[2, span, :]
        square = (WINDOW, WINDOW)
        key_at = lax.broadcasted_iota(jnp.int32, square, 0) + w * WINDOW
        query_at = lax.broadcasted_iota(jnp.int32, square, 1) + w * WINDOW
        allowed = (key_at >= border) == (query_at >= border)
        attended = None
        for h in range(cols // HEAD):
            own = head_mask(k.shape, h)
            scores = dot_nt(jnp.where(own, k, jnp.zeros_like(k)), q) * HEAD ** (-0.5)
            scores = jnp.where(allowed, scores, -1e30)
            terms = jnp.exp(scores - jnp.max(scores, axis=0, keepdims=True))
            low = (terms * (1.0 / jnp.sum(terms, axis=0, keepdims=True))).astype(BF)
            probs[0, w, h] = low
            part = dot_tn(low, v)
            attended = part if attended is None else jnp.where(own, part, attended)
        attn[span, :] = attended.astype(BF)
    tok_shape = (pooled.shape[0], rows)
    tok_of = (lax.broadcasted_iota(jnp.int32, tok_shape, 1) + shift) // POOL
    member = tok_of == lax.broadcasted_iota(jnp.int32, tok_shape, 0)
    pool = jnp.where(member, 1.0 / POOL, 0.0).astype(BF)
    low = dot(pool, attn[...]).astype(BF)
    pooled[...] = low
    out[...] += dot(low, wo_ref[...])


def encoder_forward(x_roll, w_t, weight_out, at, ext_tok):
    rows, width = x_roll.shape
    heads_w = weight_out.shape[0]
    cols = 2 * HEAD
    pairs = heads_w // cols
    windows = rows // WINDOW
    weight = lambda i: pl.BlockSpec((cols, width), lambda p, at: (i * pairs + p, 0))
    return pl.pallas_call(
        forward_kernel,
        grid_spec=pltpu.PrefetchScalarGridSpec(
            num_scalar_prefetch=1,
            grid=(pairs,),
            in_specs=[
                pl.BlockSpec((rows, width), lambda p, at: (0, 0)),
                weight(0),
                weight(1),
                weight(2),
                weight(0),
            ],
            out_specs=[
                pl.BlockSpec((rows, width), lambda p, at: (0, 0)),
                pl.BlockSpec((3, rows, cols), lambda p, at: (0, 0, p)),
                pl.BlockSpec((1, windows, 2, WINDOW, WINDOW), lambda p, at: (p, 0, 0, 0, 0)),
                pl.BlockSpec((ext_tok, cols), lambda p, at: (0, p)),
                pl.BlockSpec((ext_tok, width), lambda p, at: (0, 0)),
            ],
            scratch_shapes=[pltpu.VMEM((rows, cols), BF)],
        ),
        out_shape=[
            jax.ShapeDtypeStruct((rows, width), BF),
            jax.ShapeDtypeStruct((3, rows, heads_w), BF),
            jax.ShapeDtypeStruct((pairs, windows, 2, WINDOW, WINDOW), BF),
            jax.ShapeDtypeStruct((ext_tok, heads_w), BF),
            jax.ShapeDtypeStruct((ext_tok, width), F32),
        ],
        compiler_params=pltpu.CompilerParams(vmem_limit_bytes=VMEM_LIMIT),
        name="encoder_forward",
    )(at, x_roll, w_t, w_t, w_t, weight_out)


def out_grad_kernel(n, at, d_ref, wo_ref, pa_ref, d_attn, even, odd, turned):
    me = at[2]
    block = even.shape[1]
    d_ext = d_ref[...]
    d_attn[...] = (dot_nt(d_ext, wo_ref[...]) * (1.0 / POOL)).astype(BF)
    turned[...] = pa_ref[...].T
    for bit, ref in enumerate((even, odd)):
        for j, k in enumerate(halving_order(n)):
            start = pl.multiple_of((me ^ (k | bit)) * block, block)
            ref[j] = dot(turned[pl.ds(start, block), :], d_ext).astype(BF)


def out_grad(d_ext, weight_out, pooled_attn, at, n):
    heads_w, width = weight_out.shape
    blocks = jax.ShapeDtypeStruct((n // 2, heads_w // n, width), BF)
    whole = pl.BlockSpec(memory_space=pltpu.VMEM)
    return pl.pallas_call(
        functools.partial(out_grad_kernel, n),
        in_specs=[pl.BlockSpec(memory_space=pltpu.SMEM), whole, whole, whole],
        out_specs=[whole] * 3,
        out_shape=[jax.ShapeDtypeStruct(pooled_attn.shape, BF), blocks, blocks],
        scratch_shapes=[pltpu.VMEM((heads_w, pooled_attn.shape[0]), BF)],
        compiler_params=pltpu.CompilerParams(vmem_limit_bytes=VMEM_LIMIT),
        name="out_grad",
    )(at, d_ext, weight_out, pooled_attn)


def backward_kernel(n, at, n_ref, qkv, probs, d_ref, even, odd, turned, grads):
    shift, me = at[0], at[2]
    rows = n_ref.shape[0]
    cols = d_ref.shape[1]
    block = even.shape[2]

    @pl.when(pl.program_id(0) == 0)
    def _():
        turned[...] = n_ref[...].T

    tok_shape = (rows, d_ref.shape[0])
    tok_of = (lax.broadcasted_iota(jnp.int32, tok_shape, 0) + shift) // POOL
    member = tok_of == lax.broadcasted_iota(jnp.int32, tok_shape, 1)
    d_rows = dot(jnp.where(member, 1.0, 0.0).astype(BF), d_ref[...]).astype(BF)
    for w in range(rows // WINDOW):
        span = pl.ds(w * WINDOW, WINDOW)
        q, k, v = qkv[0, span, :], qkv[1, span, :], qkv[2, span, :]
        d_out = d_rows[w * WINDOW : (w + 1) * WINDOW]
        none = jnp.zeros_like(q)
        sums = [0.0, 0.0, 0.0]
        for h in range(cols // HEAD):
            own = head_mask(q.shape, h)
            low = probs[0, w, h]
            weight = low.astype(F32)
            d_weight = dot_nt(jnp.where(own, v, none), d_out)
            centre = jnp.sum(weight * d_weight, axis=0, keepdims=True)
            d_score = (weight * (d_weight - centre) * HEAD ** (-0.5)).astype(BF)
            sums[0] += dot_tn(d_score, jnp.where(own, k, none))
            sums[1] += dot(d_score, jnp.where(own, q, none))
            sums[2] += dot(low, jnp.where(own, d_out, none))
        for i in range(3):
            grads[span, i * cols : (i + 1) * cols] = sums[i].astype(BF)
    d_all = grads[...]
    for bit, ref in enumerate((even, odd)):
        for j, k in enumerate(halving_order(n)):
            start = pl.multiple_of((me ^ (k | bit)) * block, block)
            term = dot(turned[pl.ds(start, block), :], d_all).astype(BF)
            for i in range(3):
                ref[j, i] = term[:, i * cols : (i + 1) * cols]


def encoder_backward(normed, qkv, probs, d_attn, at, n, first, count):
    rows, width = normed.shape
    cols = 2 * HEAD
    windows = rows // WINDOW
    block = width // n
    out = pl.BlockSpec((n // 2, 3, block, cols), lambda p, at: (0, 0, 0, p))
    shape = jax.ShapeDtypeStruct((n // 2, 3, block, cols * count), BF)
    return pl.pallas_call(
        functools.partial(backward_kernel, n),
        grid_spec=pltpu.PrefetchScalarGridSpec(
            num_scalar_prefetch=1,
            grid=(count,),
            in_specs=[
                pl.BlockSpec((rows, width), lambda p, at: (0, 0)),
                pl.BlockSpec((3, rows, cols), lambda p, at: (0, 0, p + first)),
                pl.BlockSpec(
                    (1, windows, 2, WINDOW, WINDOW), lambda p, at: (p + first, 0, 0, 0, 0)
                ),
                pl.BlockSpec((d_attn.shape[0], cols), lambda p, at: (0, p + first)),
            ],
            out_specs=[out, out],
            scratch_shapes=[pltpu.VMEM((width, rows), BF), pltpu.VMEM((rows, 3 * cols), BF)],
        ),
        out_shape=[shape, shape],
        compiler_params=pltpu.CompilerParams(vmem_limit_bytes=VMEM_LIMIT),
        name="encoder_backward",
    )(at, normed, qkv, probs, d_attn)


def on_device(frames, weight_qkv, weight_out, proj_in, norm_gain, proj_kv, shifts, route, d_kv):
    n = lax.axis_size("tm")
    me = lax.axis_index("tm")
    core = lax.axis_index("mp")
    rows, width = frames.shape
    half_w = width // 2
    shift = shifts[0]
    own_tok = rows // POOL
    tail_tok = WINDOW // POOL
    ext_tok = own_tok + tail_tok
    feats = proj_kv.shape[0]
    kv_half = proj_kv.shape[1] // 2
    piece = own_tok // n

    part = lax.dynamic_slice_in_dim(frames, core * (WINDOW // 2), WINDOW // 2, 0)
    mine = to_tm(part, -1, False)
    other = swap_mp(mine)
    halo = jnp.where(
        core == 0, jnp.concatenate([mine, other], 0), jnp.concatenate([other, mine], 0)
    )
    x_roll = lax.dynamic_slice_in_dim(jnp.concatenate([frames, halo], 0), shift, rows, 0)

    proj_in, x_roll = lax.optimization_barrier((proj_in, x_roll))
    blocks = [lax.dynamic_slice_in_dim(proj_in, me * feats, feats, 1)]
    for k in range(1, n):
        blocks.append(swap_tm(lax.dynamic_slice_in_dim(proj_in, (me ^ k) * feats, feats, 1), k))
    lift_w = jnp.take(jnp.stack(blocks), me ^ jnp.arange(n, dtype=jnp.int32), axis=0)
    lift_w = lift_w.reshape(width, feats)
    gain = lax.dynamic_slice_in_dim(norm_gain, me * feats, feats, 0)

    w_t = jnp.transpose(weight_qkv, (1, 2, 0)).reshape(-1, width)
    at = jnp.stack([shift, rows * n - shift - me * rows, me]).astype(jnp.int32)
    normed, qkv, probs, pooled_attn, out_part = encoder_forward(
        x_roll, w_t, weight_out, at, ext_tok
    )
    out_low = out_part.astype(BF)
    low_own = lax.dynamic_slice_in_dim(out_low, core * half_w, half_w, 1)
    low_other = lax.dynamic_slice_in_dim(out_low, (1 - core) * half_w, half_w, 1)
    from_core = swap_mp(low_other[:own_tok])
    tail_a = to_tm(low_own[own_tok:], 1, False)
    tail_b = to_tm(low_other[own_tok:], 1, True)
    own_pool = (
        jnp.arange(rows, dtype=jnp.int32)[None, :] // POOL
        == jnp.arange(own_tok, dtype=jnp.int32)[:, None]
    ).astype(BF) * (1.0 / POOL)
    x_mean = dot(own_pool, lax.dynamic_slice_in_dim(frames, core * half_w, half_w, 1))
    pooled = (
        x_mean
        + lax.dynamic_slice_in_dim(out_part, core * half_w, half_w, 1)[:own_tok]
        + from_core.astype(F32)
    )
    tail = tail_a.astype(F32) + tail_b.astype(F32)
    pooled = jnp.concatenate([pooled[:tail_tok] + tail, pooled[tail_tok:]], 0).astype(BF)

    tok_half = jnp.concatenate(gather_xor(pooled), 0)
    tok_other = swap_mp(tok_half)
    inverse = jnp.argsort(route, axis=1).astype(jnp.int32)
    owners = me ^ jnp.arange(n, dtype=jnp.int32)
    sources = jnp.arange(n, dtype=jnp.int32)
    piece_at = (sources[None, :] ^ me) * n + inverse.T[owners]
    row_at = (piece_at[:, :, None] * piece + jnp.arange(piece, dtype=jnp.int32)).reshape(-1)
    tok = jnp.concatenate([tok_half, tok_other], 1)
    tok = jnp.take(tok, row_at, axis=0)
    lift_own = jnp.concatenate(
        [
            lax.dynamic_slice_in_dim(lift_w, core * half_w, half_w, 0),
            lax.dynamic_slice_in_dim(lift_w, (1 - core) * half_w, half_w, 0),
        ],
        0,
    )
    lifted = dot(tok, lift_own)
    squares = jnp.sum(lifted * lifted, axis=-1).reshape(n, own_tok)
    square_sum = small_scatter(squares)
    inv_rms = lax.rsqrt(square_sum / LLM_D + 1e-05)
    scaled = (lifted * gain).astype(BF)
    kv_w_own = lax.dynamic_slice_in_dim(proj_kv, core * kv_half, kv_half, 1)
    kv_w_other = lax.dynamic_slice_in_dim(proj_kv, (1 - core) * kv_half, kv_half, 1)
    from_core = swap_mp(dot(scaled, kv_w_other).astype(BF))
    kv_part = (dot(scaled, kv_w_own) + from_core.astype(F32)).astype(BF)
    kv_part = kv_part.reshape(n // 2, 2, own_tok, kv_half)
    kv_sum = scatter_xor(kv_part[:, 0], kv_part[:, 1])
    kv = (kv_sum * inv_rms.reshape(own_tok, 1)).astype(BF)
    total_cot = (kv.astype(F32) + d_kv.astype(F32)).astype(BF)
    inner = jnp.sum(total_cot.astype(F32) * kv_sum, axis=-1).reshape(1, own_tok)
    inner = inner + swap_mp(inner)
    stats = small_gather(jnp.stack([inv_rms, inner], axis=1))
    inv_all = stats[:, 0].reshape(-1, 1)
    inner_all = stats[:, 1].reshape(-1, 1)
    cot_half = jnp.concatenate(gather_xor(total_cot), 0)
    cot_other = swap_mp(cot_half)
    d_normed = dot_nt(cot_half, kv_w_own) + dot_nt(cot_other, kv_w_other)
    d_lifted = (inv_all * gain * d_normed - lifted * (inv_all**3 * inner_all / LLM_D)).astype(BF)
    d_tok = dot_nt(d_lifted, lift_own).astype(BF)
    slot_of = (
        jnp.arange(n, dtype=jnp.int32)[None, :] * 0
        + (route[sources ^ me] ^ me) * n
        + (sources ^ me)[:, None]
    )
    back_at = (slot_of[:, :, None] * piece + jnp.arange(piece, dtype=jnp.int32)).reshape(-1)
    d_tok = jnp.take(d_tok, back_at, axis=0)
    from_core = swap_mp(d_tok[:, half_w:])
    d_part = (d_tok[:, :half_w].astype(F32) + from_core.astype(F32)).astype(BF)
    d_part = d_part.reshape(n // 2, 2, own_tok, half_w)
    d_half = scatter_xor(d_part[:, 0], d_part[:, 1]).astype(BF)

    d_other = swap_mp(d_half)
    next_a = to_tm(d_half[:tail_tok], -1, False)
    next_b = to_tm(d_half[:tail_tok], -1, True)
    left = jnp.concatenate([d_half, next_a], 0)
    right = jnp.concatenate([d_other, next_b], 0)
    d_ext = jnp.where(
        core == 0, jnp.concatenate([left, right], 1), jnp.concatenate([right, left], 1)
    )
    d_attn, out_even, out_odd = out_grad(d_ext, weight_out, pooled_attn, at, n)
    grad_out = scatter_halving(out_even, out_odd)
    chunks, count = [], weight_out.shape[0] // (4 * HEAD)
    for first in range(0, 2 * count, count):
        even, odd = encoder_backward(normed, qkv, probs, d_attn, at, n, first, count)
        chunks.append(scatter_halving(even, odd))
    grad_qkv = jnp.transpose(jnp.concatenate(chunks, axis=-1), (1, 0, 2))
    return kv, grad_qkv, grad_out


def solution(mesh):
    in_specs = (
        P(("groups", "tm"), None),
        P(None, None, "mp"),
        P("mp", None),
        P("tm", "mp"),
        P("mp"),
        P(("mp", "tm"), None),
        P(),
        P(),
        P(("groups", "tm"), "mp"),
    )
    out_specs = (
        P(("groups", "tm"), "mp"),
        P(("groups", "tm"), None, "mp"),
        P(("groups", "mp", "tm"), None),
    )
    return jax.shard_map(
        on_device, mesh=mesh, in_specs=in_specs, out_specs=out_specs, check_vma=False
    )
```

```python
import functools

import jax
import jax.numpy as jnp
import numpy as np
from jax import lax
from jax.experimental import pallas as pl
from jax.experimental.pallas import tpu as pltpu
from jax.sharding import PartitionSpec as P

HEAD = 64
WINDOW = 256
POOL = 4
LLM_D = 8192
BF = jnp.bfloat16
F32 = jnp.float32
VMEM_LIMIT = 48 << 20
SPLIT = 1
CHUNK = 512


def dot(a, b):
    return jnp.dot(a, b, preferred_element_type=F32)


def dot_nt(a, b):
    return lax.dot_general(a, b, (((1,), (1,)), ((), ())), preferred_element_type=F32)


def dot_tn(a, b):
    return lax.dot_general(a, b, (((0,), (0,)), ((), ())), preferred_element_type=F32)


def swap_tm(block, mask):
    n = lax.axis_size("tm")
    return lax.ppermute(block, "tm", [(i, i ^ mask) for i in range(n)])


def swap_mp(block):
    n = lax.axis_size("mp")
    return lax.ppermute(block, "mp", [(i, n - 1 - i) for i in range(n)])


def to_tm(block, step, cross):
    n, m = lax.axis_size("tm"), lax.axis_size("mp")
    pairs = []
    for i in range(n):
        for c in range(m):
            pairs.append((i * m + c, (i + step) % n * m + (m - 1 - c if cross else c)))
    return lax.ppermute(block, ("tm", "mp"), pairs)


def offsets(masks):
    order = [0]
    for mask in reversed(masks):
        order = order + [k | mask for k in order]
    return order


def tm_bits():
    n = lax.axis_size("tm")
    return [1 << i for i in range(n.bit_length() - 1)]


def group_bits():
    return [bit for bit in tm_bits() if bit != SPLIT]


def gather_doubling(block, masks):
    block = block[None]
    for mask in reversed(masks):
        block = jnp.concatenate([block, swap_tm(block, mask)], axis=0)
    return block


def scatter_halving(blocks, masks, kind):
    total = blocks
    for mask in masks:
        low = total.astype(kind)
        half = low.shape[0] // 2
        total = low[:half].astype(F32) + swap_tm(low[half:], mask).astype(F32)
    return total[0]


def scatter_pair(even, odd):
    total = even.astype(F32) + swap_tm(odd, 1).astype(F32)
    return scatter_halving(total, tm_bits()[1:], BF)


def halving_order(n):
    return offsets([1 << i for i in range(1, n.bit_length() - 1)])


def head_mask(shape, head):
    return lax.broadcasted_iota(jnp.int32, shape, 1) // HEAD == head


def forward_kernel(at, x_ref, wq_ref, wk_ref, wv_ref, wo_ref, normed, qkv, probs, pooled, out, attn):
    shift, border = at[0], at[1]
    rows = x_ref.shape[0]
    cols = wq_ref.shape[0]

    @pl.when(pl.program_id(0) == 0)
    def _():
        x = x_ref[...].astype(F32)
        scale = lax.rsqrt(jnp.mean(x * x, axis=-1, keepdims=True) + 1e-05)
        normed[...] = (x * scale).astype(BF)
        out[...] = jnp.zeros_like(out)

    base = normed[...]
    for i, w_ref in enumerate((wq_ref, wk_ref, wv_ref)):
        qkv[i] = dot_nt(base, w_ref[...]).astype(BF)
    for w in range(rows // WINDOW):
        span = pl.ds(w * WINDOW, WINDOW)
        q, k, v = qkv[0, span, :], qkv[1, span, :], qkv[2, span, :]
        square = (WINDOW, WINDOW)
        key_at = lax.broadcasted_iota(jnp.int32, square, 0) + w * WINDOW
        query_at = lax.broadcasted_iota(jnp.int32, square, 1) + w * WINDOW
        allowed = (key_at >= border) == (query_at >= border)
        attended = None
        for h in range(cols // HEAD):
            own = head_mask(k.shape, h)
            scores = dot_nt(jnp.where(own, k, jnp.zeros_like(k)), q) * HEAD ** (-0.5)
            scores = jnp.where(allowed, scores, -1e30)
            terms = jnp.exp(scores - jnp.max(scores, axis=0, keepdims=True))
            low = (terms * (1.0 / jnp.sum(terms, axis=0, keepdims=True))).astype(BF)
            probs[0, w, h] = low
            part = dot_tn(low, v)
            attended = part if attended is None else jnp.where(own, part, attended)
        attn[span, :] = attended.astype(BF)
    tok_shape = (pooled.shape[0], rows)
    tok_of = (lax.broadcasted_iota(jnp.int32, tok_shape, 1) + shift) // POOL
    member = tok_of == lax.broadcasted_iota(jnp.int32, tok_shape, 0)
    pool = jnp.where(member, 1.0 / POOL, 0.0).astype(BF)
    low = dot(pool, attn[...]).astype(BF)
    pooled[...] = low
    out[...] += dot(low, wo_ref[...])


def encoder_forward(x_roll, w_t, weight_out, at, ext_tok):
    rows, width = x_roll.shape
    heads_w = weight_out.shape[0]
    cols = 2 * HEAD
    pairs = heads_w // cols
    windows = rows // WINDOW
    weight = lambda i: pl.BlockSpec((cols, width), lambda p, at: (i * pairs + p, 0))
    return pl.pallas_call(
        forward_kernel,
        grid_spec=pltpu.PrefetchScalarGridSpec(
            num_scalar_prefetch=1,
            grid=(pairs,),
            in_specs=[
                pl.BlockSpec((rows, width), lambda p, at: (0, 0)),
                weight(0),
                weight(1),
                weight(2),
                weight(0),
            ],
            out_specs=[
                pl.BlockSpec((rows, width), lambda p, at: (0, 0)),
                pl.BlockSpec((3, rows, cols), lambda p, at: (0, 0, p)),
                pl.BlockSpec((1, windows, 2, WINDOW, WINDOW), lambda p, at: (p, 0, 0, 0, 0)),
                pl.BlockSpec((ext_tok, cols), lambda p, at: (0, p)),
                pl.BlockSpec((ext_tok, width), lambda p, at: (0, 0)),
            ],
            scratch_shapes=[pltpu.VMEM((rows, cols), BF)],
        ),
        out_shape=[
            jax.ShapeDtypeStruct((rows, width), BF),
            jax.ShapeDtypeStruct((3, rows, heads_w), BF),
            jax.ShapeDtypeStruct((pairs, windows, 2, WINDOW, WINDOW), BF),
            jax.ShapeDtypeStruct((ext_tok, heads_w), BF),
            jax.ShapeDtypeStruct((ext_tok, width), F32),
        ],
        compiler_params=pltpu.CompilerParams(vmem_limit_bytes=VMEM_LIMIT),
        name="encoder_forward",
    )(at, x_roll, w_t, w_t, w_t, weight_out)


def out_grad_kernel(n, at, d_ref, wo_ref, pa_ref, d_attn, even, odd, turned):
    me = at[2]
    block = even.shape[1]
    d_ext = d_ref[...]
    d_attn[...] = (dot_nt(d_ext, wo_ref[...]) * (1.0 / POOL)).astype(BF)
    turned[...] = pa_ref[...].T
    for bit, ref in enumerate((even, odd)):
        for j, k in enumerate(halving_order(n)):
            start = pl.multiple_of((me ^ (k | bit)) * block, block)
            ref[j] = dot(turned[pl.ds(start, block), :], d_ext).astype(BF)


def out_grad(d_ext, weight_out, pooled_attn, at, n):
    heads_w, width = weight_out.shape
    blocks = jax.ShapeDtypeStruct((n // 2, heads_w // n, width), BF)
    whole = pl.BlockSpec(memory_space=pltpu.VMEM)
    return pl.pallas_call(
        functools.partial(out_grad_kernel, n),
        in_specs=[pl.BlockSpec(memory_space=pltpu.SMEM), whole, whole, whole],
        out_specs=[whole] * 3,
        out_shape=[jax.ShapeDtypeStruct(pooled_attn.shape, BF), blocks, blocks],
        scratch_shapes=[pltpu.VMEM((heads_w, pooled_attn.shape[0]), BF)],
        compiler_params=pltpu.CompilerParams(vmem_limit_bytes=VMEM_LIMIT),
        name="out_grad",
    )(at, d_ext, weight_out, pooled_attn)


def backward_kernel(n, at, n_ref, qkv, probs, d_ref, even, odd, turned, grads):
    shift, me = at[0], at[2]
    rows = n_ref.shape[0]
    cols = d_ref.shape[1]
    block = even.shape[2]

    @pl.when(pl.program_id(0) == 0)
    def _():
        turned[...] = n_ref[...].T

    tok_shape = (rows, d_ref.shape[0])
    tok_of = (lax.broadcasted_iota(jnp.int32, tok_shape, 0) + shift) // POOL
    member = tok_of == lax.broadcasted_iota(jnp.int32, tok_shape, 1)
    d_rows = dot(jnp.where(member, 1.0, 0.0).astype(BF), d_ref[...]).astype(BF)
    for w in range(rows // WINDOW):
        span = pl.ds(w * WINDOW, WINDOW)
        q, k, v = qkv[0, span, :], qkv[1, span, :], qkv[2, span, :]
        d_out = d_rows[w * WINDOW : (w + 1) * WINDOW]
        none = jnp.zeros_like(q)
        sums = [0.0, 0.0, 0.0]
        for h in range(cols // HEAD):
            own = head_mask(q.shape, h)
            low = probs[0, w, h]
            weight = low.astype(F32)
            d_weight = dot_nt(jnp.where(own, v, none), d_out)
            centre = jnp.sum(weight * d_weight, axis=0, keepdims=True)
            d_score = (weight * (d_weight - centre) * HEAD ** (-0.5)).astype(BF)
            sums[0] += dot_tn(d_score, jnp.where(own, k, none))
            sums[1] += dot(d_score, jnp.where(own, q, none))
            sums[2] += dot(low, jnp.where(own, d_out, none))
        for i in range(3):
            grads[span, i * cols : (i + 1) * cols] = sums[i].astype(BF)
    d_all = grads[...]
    for bit, ref in enumerate((even, odd)):
        for j, k in enumerate(halving_order(n)):
            start = pl.multiple_of((me ^ (k | bit)) * block, block)
            term = dot(turned[pl.ds(start, block), :], d_all).astype(BF)
            for i in range(3):
                ref[j, i] = term[:, i * cols : (i + 1) * cols]


def encoder_backward(normed, qkv, probs, d_attn, at, n, first, count):
    rows, width = normed.shape
    cols = 2 * HEAD
    windows = rows // WINDOW
    block = width // n
    out = pl.BlockSpec((n // 2, 3, block, cols), lambda p, at: (0, 0, 0, p))
    shape = jax.ShapeDtypeStruct((n // 2, 3, block, cols * count), BF)
    return pl.pallas_call(
        functools.partial(backward_kernel, n),
        grid_spec=pltpu.PrefetchScalarGridSpec(
            num_scalar_prefetch=1,
            grid=(count,),
            in_specs=[
                pl.BlockSpec((rows, width), lambda p, at: (0, 0)),
                pl.BlockSpec((3, rows, cols), lambda p, at: (0, 0, p + first)),
                pl.BlockSpec(
                    (1, windows, 2, WINDOW, WINDOW), lambda p, at: (p + first, 0, 0, 0, 0)
                ),
                pl.BlockSpec((d_attn.shape[0], cols), lambda p, at: (0, p + first)),
            ],
            out_specs=[out, out],
            scratch_shapes=[pltpu.VMEM((width, rows), BF), pltpu.VMEM((rows, 3 * cols), BF)],
        ),
        out_shape=[shape, shape],
        compiler_params=pltpu.CompilerParams(vmem_limit_bytes=VMEM_LIMIT),
        name="encoder_backward",
    )(at, normed, qkv, probs, d_attn)


def moves(order, piece):
    count = len(order)
    for e, offset in enumerate(order):
        for b in range(2):
            for i, step in enumerate(order):
                owner = order.index(offset ^ step)
                source_row = ((e * 2 + b) * count + i) * piece
                owner_row = ((owner * count + i) * 2 + b) * piece
                yield source_row, owner_row


def chunks_of(rows):
    return [slice(r, min(r + CHUNK, rows)) for r in range(0, rows, CHUNK)]


def lift_kernel(table, at, ta, tb, w_ref, gain, kva, kvb, lifted, send, keep, tok):
    half = ta.shape[1]
    feats = kva.shape[0]
    cols = send.shape[1]
    piece = ta.shape[0] // len(table) if table else 0
    for source_row, owner_row in table:
        tok[owner_row : owner_row + piece, :half] = ta[source_row : source_row + piece]
        tok[owner_row : owner_row + piece, half:] = tb[source_row : source_row + piece]
    if not table:
        tok[:, :half] = ta[...]
        tok[:, half:] = tb[...]
    core = at[3]
    for rows in chunks_of(tok.shape[0]):
        product = dot(tok[rows], w_ref[...])
        lifted[rows] = product
        low = (product * gain[...]).astype(BF)
        for ref, side in ((send, 1 - core), (keep, core)):
            span = pl.ds(pl.multiple_of(side * cols, cols), cols)
            part = dot(low[:, :feats], kva[:, span]) + dot(low[:, feats:], kvb[:, span])
            ref[rows] = part.astype(BF)


def lift(table, at, ta, tb, weight, gain, kva, kvb):
    rows, half = ta.shape
    cols = kva.shape[1] // 2
    whole = pl.BlockSpec(memory_space=pltpu.VMEM)
    return pl.pallas_call(
        functools.partial(lift_kernel, table),
        in_specs=[pl.BlockSpec(memory_space=pltpu.SMEM)] + [whole] * 6,
        out_specs=[whole] * 3,
        out_shape=[
            jax.ShapeDtypeStruct((rows, weight.shape[1]), F32),
            jax.ShapeDtypeStruct((rows, cols), BF),
            jax.ShapeDtypeStruct((rows, cols), BF),
        ],
        scratch_shapes=[pltpu.VMEM((rows, 2 * half), BF)],
        compiler_params=pltpu.CompilerParams(vmem_limit_bytes=VMEM_LIMIT),
        name="lift",
    )(at, ta, tb, weight, gain, kva, kvb)


def lower_kernel(table, at, ca, cb, kva, kvb, lifted, gain, inv, pull, w_ref, send, keep):
    half = send.shape[1]
    cols = ca.shape[1]
    core = at[3]
    own = pl.ds(pl.multiple_of(core * cols, cols), cols)
    other = pl.ds(pl.multiple_of((1 - core) * cols, cols), cols)
    piece = ca.shape[0] // len(table) if table else 0
    for rows in chunks_of(ca.shape[0]):
        parts = [
            dot_nt(ca[rows], w[:, own]) + dot_nt(cb[rows], w[:, other]) for w in (kva, kvb)
        ]
        d_normed = jnp.concatenate(parts, axis=1)
        d_lifted = inv[rows] * gain[...] * d_normed - lifted[rows] * pull[rows]
        low = d_lifted.astype(BF)
        for ref, w in ((send, w_ref[half:]), (keep, w_ref[:half])):
            part = dot_nt(low, w).astype(BF)
            if not table:
                ref[rows] = part
            for source_row, owner_row in table:
                if rows.start <= owner_row < rows.stop:
                    at_row = owner_row - rows.start
                    ref[source_row : source_row + piece] = part[at_row : at_row + piece]


def lower(table, at, ca, cb, kva, kvb, lifted, gain, inv, pull, weight):
    whole = pl.BlockSpec(memory_space=pltpu.VMEM)
    out = jax.ShapeDtypeStruct((ca.shape[0], weight.shape[0] // 2), BF)
    return pl.pallas_call(
        functools.partial(lower_kernel, table),
        in_specs=[pl.BlockSpec(memory_space=pltpu.SMEM)] + [whole] * 9,
        out_specs=[whole] * 2,
        out_shape=[out] * 2,
        compiler_params=pltpu.CompilerParams(vmem_limit_bytes=VMEM_LIMIT),
        name="lower",
    )(at, ca, cb, kva, kvb, lifted, gain, inv, pull, weight)


def on_device(frames, weight_qkv, weight_out, proj_in, norm_gain, proj_kv, shifts, route, d_kv):
    n = lax.axis_size("tm")
    me = lax.axis_index("tm")
    core = lax.axis_index("mp")
    rows, width = frames.shape
    half_w = width // 2
    shift = shifts[0]
    own_tok = rows // POOL
    tail_tok = WINDOW // POOL
    ext_tok = own_tok + tail_tok
    feats = proj_kv.shape[0]
    kv_half = proj_kv.shape[1] // 2
    piece = own_tok // n

    part = lax.dynamic_slice_in_dim(frames, core * (WINDOW // 2), WINDOW // 2, 0)
    mine = to_tm(part, -1, False)
    other = swap_mp(mine)
    halo = jnp.where(
        core == 0, jnp.concatenate([mine, other], 0), jnp.concatenate([other, mine], 0)
    )
    x_roll = lax.dynamic_slice_in_dim(jnp.concatenate([frames, halo], 0), shift, rows, 0)

    proj_in, proj_kv, x_roll = lax.optimization_barrier((proj_in, proj_kv, x_roll))
    kva, kvb = proj_kv, swap_tm(proj_kv, SPLIT)
    masks = group_bits()
    order = offsets(masks)
    members = order + [k | SPLIT for k in order]
    blocks = []
    for k in order:
        pair = [
            lax.dynamic_slice_in_dim(proj_in, (me ^ k ^ bit) * feats, feats, 1)
            for bit in (0, SPLIT)
        ]
        pair = jnp.stack(pair)
        blocks.append(swap_tm(pair, k) if k else pair)
    here = jnp.stack(blocks, axis=1)
    there = swap_tm(here[::-1], SPLIT)
    lift_w = jnp.concatenate([here, there], axis=1)
    natural = (jnp.arange(n, dtype=jnp.int32) + core * (n // 2)) % n
    found = (natural ^ me)[:, None] == jnp.array(members, jnp.int32)[None, :]
    place = jnp.sum(found * jnp.arange(n, dtype=jnp.int32)[None, :], axis=1)
    lift_w = jnp.take(lift_w, place, axis=1).reshape(2, width, feats)
    lift_w = jnp.concatenate([lift_w[0], lift_w[1]], axis=1)
    gain = jnp.concatenate(
        [
            lax.dynamic_slice_in_dim(norm_gain, (me ^ bit) * feats, feats, 0)
            for bit in (0, SPLIT)
        ]
    ).reshape(1, -1)
    owner_at = (lax.dynamic_index_in_dim(route, me, 0, keepdims=False) ^ me)[None, :]
    sort = owner_at == jnp.array(members, jnp.int32)[:, None]
    sort = jnp.kron(sort.astype(BF), jnp.eye(piece, dtype=BF))
    source_at = jnp.arange(n, dtype=jnp.int32) ^ me
    spread = source_at[:, None] == jnp.array(
        [k | bit for k in order for bit in (0, SPLIT)], jnp.int32
    )
    spread = jnp.kron(spread.astype(BF), jnp.eye(piece, dtype=BF))
    d_kv = dot_tn(spread, d_kv)

    w_t = jnp.transpose(weight_qkv, (1, 2, 0)).reshape(-1, width)
    at = jnp.stack([shift, rows * n - shift - me * rows, me, core]).astype(jnp.int32)
    normed, qkv, probs, pooled_attn, out_part = encoder_forward(
        x_roll, w_t, weight_out, at, ext_tok
    )
    out_low = out_part.astype(BF)
    low_own = lax.dynamic_slice_in_dim(out_low, core * half_w, half_w, 1)
    low_other = lax.dynamic_slice_in_dim(out_low, (1 - core) * half_w, half_w, 1)
    from_core = swap_mp(low_other[:own_tok])
    tail_a = to_tm(low_own[own_tok:], 1, False)
    tail_b = to_tm(low_other[own_tok:], 1, True)
    own_pool = (
        jnp.arange(rows, dtype=jnp.int32)[None, :] // POOL
        == jnp.arange(own_tok, dtype=jnp.int32)[:, None]
    ).astype(BF) * (1.0 / POOL)
    x_mean = dot(own_pool, lax.dynamic_slice_in_dim(frames, core * half_w, half_w, 1))
    pooled = (
        x_mean
        + lax.dynamic_slice_in_dim(out_part, core * half_w, half_w, 1)[:own_tok]
        + from_core.astype(F32)
    )
    tail = tail_a.astype(F32) + tail_b.astype(F32)
    pooled = jnp.concatenate([pooled[:tail_tok] + tail, pooled[tail_tok:]], 0).astype(BF)

    count = n // 2
    sorted_tok = dot(sort, pooled).astype(BF).reshape(2, count * piece, half_w)
    pair_tok = jnp.stack([sorted_tok[0], swap_tm(sorted_tok[1], SPLIT)])
    tok_half = gather_doubling(pair_tok, masks).reshape(-1, half_w)
    tok_other = swap_mp(tok_half)
    table = list(moves(order, piece))
    source_rows = np.concatenate([np.arange(r, r + piece) for r, _ in table])
    owner_rows = np.concatenate([np.arange(r, r + piece) for _, r in table])
    by_xla = piece % 16 != 0
    if by_xla:
        at_owner = source_rows[np.argsort(owner_rows)]
        tok_half, tok_other = tok_half[at_owner], tok_other[at_owner]
        table = []
    lifted, kv_send, kv_keep = lift(table, at, tok_half, tok_other, lift_w, gain, kva, kvb)
    squares = jnp.sum(lifted * lifted, axis=-1).reshape(count, own_tok)
    square_sum = scatter_halving(squares + swap_mp(squares), masks, F32)
    inv_rms = lax.rsqrt(square_sum / LLM_D + 1e-05)
    kv_part = kv_keep.astype(F32) + swap_mp(kv_send).astype(F32)
    kv_sum = scatter_halving(kv_part.reshape(count, own_tok, kv_half), masks, BF)
    kv_low = (kv_sum * inv_rms[:, None]).astype(BF)
    total_cot = (kv_low.astype(F32) + d_kv).astype(BF)
    kv = dot(spread, kv_low).astype(BF)
    inner = jnp.sum(total_cot.astype(F32) * kv_sum, axis=-1)
    inner = inner + swap_mp(inner)
    stats = gather_doubling(jnp.stack([inv_rms, inner]), masks)
    inv_all = stats[:, 0].reshape(-1, 1)
    pull = inv_all**3 * stats[:, 1].reshape(-1, 1) / LLM_D
    cot_half = gather_doubling(total_cot, masks).reshape(-1, kv_half)
    cot_other = swap_mp(cot_half)
    d_send, d_keep = lower(
        table, at, cot_half, cot_other, kva, kvb, lifted, gain, inv_all, pull, lift_w
    )
    if by_xla:
        at_source = owner_rows[np.argsort(source_rows)]
        d_send, d_keep = d_send[at_source], d_keep[at_source]
    d_part = d_keep.astype(F32) + swap_mp(d_send).astype(F32)
    d_pair = scatter_halving(d_part.reshape(count, 2, count * piece, half_w), masks, BF)
    d_sorted = jnp.concatenate([d_pair[0].astype(BF), swap_tm(d_pair[1].astype(BF), SPLIT)], 0)
    d_half = dot_tn(sort, d_sorted).astype(BF)

    d_other = swap_mp(d_half)
    next_a = to_tm(d_half[:tail_tok], -1, False)
    next_b = to_tm(d_half[:tail_tok], -1, True)
    left = jnp.concatenate([d_half, next_a], 0)
    right = jnp.concatenate([d_other, next_b], 0)
    d_ext = jnp.where(
        core == 0, jnp.concatenate([left, right], 1), jnp.concatenate([right, left], 1)
    )
    d_attn, out_even, out_odd = out_grad(d_ext, weight_out, pooled_attn, at, n)
    grad_out = scatter_pair(out_even, out_odd)
    chunks, count = [], weight_out.shape[0] // (4 * HEAD)
    for first in range(0, 2 * count, count):
        even, odd = encoder_backward(normed, qkv, probs, d_attn, at, n, first, count)
        chunks.append(scatter_pair(even, odd))
    grad_qkv = jnp.transpose(jnp.concatenate(chunks, axis=-1), (1, 0, 2))
    return kv, grad_qkv, grad_out


def solution(mesh):
    in_specs = (
        P(("groups", "tm"), None),
        P(None, None, "mp"),
        P("mp", None),
        P("tm", "mp"),
        P("mp"),
        P(("mp", "tm"), None),
        P(),
        P(),
        P(("groups", "tm"), "mp"),
    )
    out_specs = (
        P(("groups", "tm"), "mp"),
        P(("groups", "tm"), None, "mp"),
        P(("groups", "mp", "tm"), None),
    )
    return jax.shard_map(
        on_device, mesh=mesh, in_specs=in_specs, out_specs=out_specs, check_vma=False
    )
```

```python
import functools

import jax
import jax.numpy as jnp
import numpy as np
from jax import lax
from jax.experimental import pallas as pl
from jax.experimental.pallas import tpu as pltpu
from jax.sharding import PartitionSpec as P

HEAD = 64
WINDOW = 256
POOL = 4
LLM_D = 8192
BF = jnp.bfloat16
F32 = jnp.float32
VMEM_LIMIT = 48 << 20
SPLIT = 1
CHUNK = 512
LANES = 128


def dot(a, b):
    return jnp.dot(a, b, preferred_element_type=F32)


def dot_nt(a, b):
    return lax.dot_general(a, b, (((1,), (1,)), ((), ())), preferred_element_type=F32)


def dot_tn(a, b):
    return lax.dot_general(a, b, (((0,), (0,)), ((), ())), preferred_element_type=F32)


def swap_tm(block, mask):
    n = lax.axis_size("tm")
    return lax.ppermute(block, "tm", [(i, i ^ mask) for i in range(n)])


def swap_mp(block):
    n = lax.axis_size("mp")
    return lax.ppermute(block, "mp", [(i, n - 1 - i) for i in range(n)])


def to_tm(block, step, cross):
    n, m = lax.axis_size("tm"), lax.axis_size("mp")
    pairs = []
    for i in range(n):
        for c in range(m):
            pairs.append((i * m + c, (i + step) % n * m + (m - 1 - c if cross else c)))
    return lax.ppermute(block, ("tm", "mp"), pairs)


def offsets(masks):
    order = [0]
    for mask in reversed(masks):
        order = order + [k | mask for k in order]
    return order


def tm_bits():
    n = lax.axis_size("tm")
    return [1 << i for i in range(n.bit_length() - 1)]


def group_bits():
    return [bit for bit in tm_bits() if bit != SPLIT]


def gather_doubling(block, masks):
    block = block[None]
    for mask in reversed(masks):
        block = jnp.concatenate([block, swap_tm(block, mask)], axis=0)
    return block


def scatter_halving(blocks, masks, kind):
    total = blocks
    for mask in masks:
        low = total.astype(kind)
        half = low.shape[0] // 2
        total = low[:half].astype(F32) + swap_tm(low[half:], mask).astype(F32)
    return total[0]


def scatter_last(blocks, masks):
    low = blocks.astype(BF)
    for i, mask in enumerate(masks):
        half = low.shape[0] // 2
        got = swap_tm(low[half:], mask)
        if i + 1 == len(masks):
            return low[0], got[0]
        low = (low[:half].astype(F32) + got.astype(F32)).astype(BF)


def scatter_pair(even, odd):
    total = even.astype(F32) + swap_tm(odd, 1).astype(F32)
    return scatter_halving(total, tm_bits()[1:], BF)


def halving_order(n):
    return offsets([1 << i for i in range(1, n.bit_length() - 1)])


def head_mask(shape, head):
    return lax.broadcasted_iota(jnp.int32, shape, 1) // HEAD == head


def forward_kernel(at, x_ref, wq_ref, wk_ref, wv_ref, wo_ref, normed, qkv, probs, pooled, out, attn):
    shift, border = at[0], at[1]
    rows = x_ref.shape[0]
    cols = wq_ref.shape[0]

    @pl.when(pl.program_id(0) == 0)
    def _():
        x = x_ref[...].astype(F32)
        scale = lax.rsqrt(jnp.mean(x * x, axis=-1, keepdims=True) + 1e-05)
        normed[...] = (x * scale).astype(BF)
        out[...] = jnp.zeros_like(out)

    base = normed[...]
    for i, w_ref in enumerate((wq_ref, wk_ref, wv_ref)):
        qkv[i] = dot_nt(base, w_ref[...]).astype(BF)
    windows, heads = range(rows // WINDOW), range(cols // HEAD)
    spans = [pl.ds(w * WINDOW, WINDOW) for w in windows]
    own = [head_mask((WINDOW, cols), h) for h in heads]
    scores = []
    for w in windows:
        q, k = qkv[0, spans[w], :], qkv[1, spans[w], :]
        for h in heads:
            scores.append(dot_nt(jnp.where(own[h], k, jnp.zeros_like(k)), q))
    square = (WINDOW, WINDOW)
    key_at = lax.broadcasted_iota(jnp.int32, square, 0)
    query_at = lax.broadcasted_iota(jnp.int32, square, 1)
    lows = []
    for w in windows:
        edge = border - w * WINDOW
        allowed = (key_at >= edge) == (query_at >= edge)
        for h in heads:
            score = jnp.where(allowed, scores[w * len(heads) + h] * HEAD ** (-0.5), -1e30)
            terms = jnp.exp(score - jnp.max(score, axis=0, keepdims=True))
            low = (terms * (1.0 / jnp.sum(terms, axis=0, keepdims=True))).astype(BF)
            probs[0, w, h] = low
            lows.append(low)
    for w in windows:
        v = qkv[2, spans[w], :]
        attended = None
        for h in heads:
            part = dot_tn(lows[w * len(heads) + h], v)
            attended = part if attended is None else jnp.where(own[h], part, attended)
        attn[spans[w], :] = attended.astype(BF)
    tok_shape = (pooled.shape[0], rows)
    tok_of = (lax.broadcasted_iota(jnp.int32, tok_shape, 1) + shift) // POOL
    member = tok_of == lax.broadcasted_iota(jnp.int32, tok_shape, 0)
    pool = jnp.where(member, 1.0 / POOL, 0.0).astype(BF)
    low = dot(pool, attn[...]).astype(BF)
    pooled[...] = low
    out[...] += dot(low, wo_ref[...])


def encoder_forward(x_roll, w_t, weight_out, at, ext_tok):
    rows, width = x_roll.shape
    heads_w = weight_out.shape[0]
    cols = 2 * HEAD
    pairs = heads_w // cols
    windows = rows // WINDOW
    weight = lambda i: pl.BlockSpec((cols, width), lambda p, at: (i * pairs + p, 0))
    return pl.pallas_call(
        forward_kernel,
        grid_spec=pltpu.PrefetchScalarGridSpec(
            num_scalar_prefetch=1,
            grid=(pairs,),
            in_specs=[
                pl.BlockSpec((rows, width), lambda p, at: (0, 0)),
                weight(0),
                weight(1),
                weight(2),
                weight(0),
            ],
            out_specs=[
                pl.BlockSpec((rows, width), lambda p, at: (0, 0)),
                pl.BlockSpec((3, rows, cols), lambda p, at: (0, 0, p)),
                pl.BlockSpec((1, windows, 2, WINDOW, WINDOW), lambda p, at: (p, 0, 0, 0, 0)),
                pl.BlockSpec((ext_tok, cols), lambda p, at: (0, p)),
                pl.BlockSpec((ext_tok, width), lambda p, at: (0, 0)),
            ],
            scratch_shapes=[pltpu.VMEM((rows, cols), BF)],
        ),
        out_shape=[
            jax.ShapeDtypeStruct((rows, width), BF),
            jax.ShapeDtypeStruct((3, rows, heads_w), BF),
            jax.ShapeDtypeStruct((pairs, windows, 2, WINDOW, WINDOW), BF),
            jax.ShapeDtypeStruct((ext_tok, heads_w), BF),
            jax.ShapeDtypeStruct((ext_tok, width), F32),
        ],
        compiler_params=pltpu.CompilerParams(vmem_limit_bytes=VMEM_LIMIT),
        name="encoder_forward",
    )(at, x_roll, w_t, w_t, w_t, weight_out)


def out_grad_kernel(n, at, d_ref, wo_ref, pa_ref, d_attn, even, odd, turned):
    me = at[2]
    block = even.shape[1]
    d_ext = d_ref[...]
    d_attn[...] = (dot_nt(d_ext, wo_ref[...]) * (1.0 / POOL)).astype(BF)
    turned[...] = pa_ref[...].T
    for bit, ref in enumerate((even, odd)):
        for j, k in enumerate(halving_order(n)):
            start = pl.multiple_of((me ^ (k | bit)) * block, block)
            ref[j] = dot(turned[pl.ds(start, block), :], d_ext).astype(BF)


def out_grad(d_ext, weight_out, pooled_attn, at, n):
    heads_w, width = weight_out.shape
    blocks = jax.ShapeDtypeStruct((n // 2, heads_w // n, width), BF)
    whole = pl.BlockSpec(memory_space=pltpu.VMEM)
    return pl.pallas_call(
        functools.partial(out_grad_kernel, n),
        in_specs=[pl.BlockSpec(memory_space=pltpu.SMEM), whole, whole, whole],
        out_specs=[whole] * 3,
        out_shape=[jax.ShapeDtypeStruct(pooled_attn.shape, BF), blocks, blocks],
        scratch_shapes=[pltpu.VMEM((heads_w, pooled_attn.shape[0]), BF)],
        compiler_params=pltpu.CompilerParams(vmem_limit_bytes=VMEM_LIMIT),
        name="out_grad",
    )(at, d_ext, weight_out, pooled_attn)


def backward_kernel(n, at, turned, qkv, probs, d_ref, even, odd, grads):
    shift, me = at[0], at[2]
    rows = turned.shape[1]
    cols = d_ref.shape[1]
    block = even.shape[2]
    tok_shape = (rows, d_ref.shape[0])
    tok_of = (lax.broadcasted_iota(jnp.int32, tok_shape, 0) + shift) // POOL
    member = tok_of == lax.broadcasted_iota(jnp.int32, tok_shape, 1)
    d_rows = dot(jnp.where(member, 1.0, 0.0).astype(BF), d_ref[...]).astype(BF)
    for w in range(rows // WINDOW):
        span = pl.ds(w * WINDOW, WINDOW)
        q, k, v = qkv[0, span, :], qkv[1, span, :], qkv[2, span, :]
        d_out = d_rows[w * WINDOW : (w + 1) * WINDOW]
        none = jnp.zeros_like(q)
        sums = [0.0, 0.0, 0.0]
        for h in range(cols // HEAD):
            own = head_mask(q.shape, h)
            low = probs[0, w, h]
            weight = low.astype(F32)
            d_weight = dot_nt(jnp.where(own, v, none), d_out)
            centre = jnp.sum(weight * d_weight, axis=0, keepdims=True)
            d_score = (weight * (d_weight - centre) * HEAD ** (-0.5)).astype(BF)
            sums[0] += dot_tn(d_score, jnp.where(own, k, none))
            sums[1] += dot(d_score, jnp.where(own, q, none))
            sums[2] += dot(low, jnp.where(own, d_out, none))
        for i in range(3):
            grads[span, i * cols : (i + 1) * cols] = sums[i].astype(BF)
    d_all = grads[...]
    for bit, ref in enumerate((even, odd)):
        for j, k in enumerate(halving_order(n)):
            start = pl.multiple_of((me ^ (k | bit)) * block, block)
            term = dot(turned[pl.ds(start, block), :], d_all).astype(BF)
            for i in range(3):
                ref[j, i] = term[:, i * cols : (i + 1) * cols]


def encoder_backward(turned, qkv, probs, d_attn, at, n, first, count):
    width, rows = turned.shape
    cols = 2 * HEAD
    windows = rows // WINDOW
    block = width // n
    out = pl.BlockSpec((n // 2, 3, block, cols), lambda p, at: (0, 0, 0, p))
    shape = jax.ShapeDtypeStruct((n // 2, 3, block, cols * count), BF)
    return pl.pallas_call(
        functools.partial(backward_kernel, n),
        grid_spec=pltpu.PrefetchScalarGridSpec(
            num_scalar_prefetch=1,
            grid=(count,),
            in_specs=[
                pl.BlockSpec((width, rows), lambda p, at: (0, 0)),
                pl.BlockSpec((3, rows, cols), lambda p, at: (0, 0, p + first)),
                pl.BlockSpec(
                    (1, windows, 2, WINDOW, WINDOW), lambda p, at: (p + first, 0, 0, 0, 0)
                ),
                pl.BlockSpec((d_attn.shape[0], cols), lambda p, at: (0, p + first)),
            ],
            out_specs=[out, out],
            scratch_shapes=[pltpu.VMEM((rows, 3 * cols), BF)],
        ),
        out_shape=[shape, shape],
        compiler_params=pltpu.CompilerParams(vmem_limit_bytes=VMEM_LIMIT),
        name="encoder_backward",
    )(at, turned, qkv, probs, d_attn)


def moves(order, piece):
    count = len(order)
    for e, offset in enumerate(order):
        for b in range(2):
            for i, step in enumerate(order):
                owner = order.index(offset ^ step)
                source_row = ((e * 2 + b) * count + i) * piece
                owner_row = ((owner * count + i) * 2 + b) * piece
                yield source_row, owner_row


def chunks_of(rows):
    return [slice(r, min(r + CHUNK, rows)) for r in range(0, rows, CHUNK)]


def column_starts(order, at, block):
    if order is None:
        return None
    me, group = at[2], at[4]
    part = len(order) // 2
    across = [
        jnp.where(group == q, order[i], order[part + i]) | SPLIT
        for q in range(2)
        for i in range(part)
    ]
    return [pl.multiple_of((me ^ k) * block, block) for k in order + across]


def weight_rows(order, here, got, other, bit):
    flat = lambda w: w.reshape(-1, w.shape[-1])
    across = bit if order is None else 1 - bit
    parts = [flat(here[:, bit]), flat(got[:, across]), flat(other[:, across])]
    return jnp.concatenate(parts, axis=0)


def lift_kernel(table, order, at, ta, tb, here, got, other, gain, kva, kvb, lifted, send, keep, tok):
    core, group = at[3], at[4]
    half = ta.shape[1]
    feats = kva.shape[0]
    cols = send.shape[1]
    rows_all = ta.shape[0]
    near = pl.ds(pl.multiple_of(core * half, half), half)
    far = pl.ds(pl.multiple_of((1 - core) * half, half), half)
    piece = rows_all // len(table) if table else 0
    for source_row, owner_row in table:
        tok[owner_row : owner_row + piece, near] = ta[source_row : source_row + piece]
        tok[owner_row : owner_row + piece, far] = tb[source_row : source_row + piece]
    if not table:
        tok[:, near] = ta[...]
        tok[:, far] = tb[...]
    block = here.shape[2]
    starts = column_starts(order, at, block)
    for rows in chunks_of(rows_all):
        x = tok[rows]
        if starts:
            x = jnp.concatenate([tok[rows, pl.ds(start, block)] for start in starts], axis=1)
        lows = []
        for bit in range(2):
            span = slice(bit * feats, (bit + 1) * feats)
            weight = weight_rows(order, here, got, other, bit)
            product = dot(x, weight)
            lifted[rows, span] = product
            lows.append((product * gain[:, span]).astype(BF))
        for ref, side in ((send, 1 - core), (keep, core)):
            span = pl.ds(pl.multiple_of(side * cols, cols), cols)
            part = dot(lows[0], kva[:, span]) + dot(lows[1], kvb[side ^ group])
            ref[rows] = part.astype(BF)


def lift(table, order, at, ta, tb, here, got, other, gain, kva, kvb):
    rows, half = ta.shape
    feats, cols = kva.shape[0], kva.shape[1] // 2
    whole = pl.BlockSpec(memory_space=pltpu.VMEM)
    return pl.pallas_call(
        functools.partial(lift_kernel, table, order),
        in_specs=[pl.BlockSpec(memory_space=pltpu.SMEM)] + [whole] * 8,
        out_specs=[whole] * 3,
        out_shape=[
            jax.ShapeDtypeStruct((rows, 2 * feats), F32),
            jax.ShapeDtypeStruct((rows, cols), BF),
            jax.ShapeDtypeStruct((rows, cols), BF),
        ],
        scratch_shapes=[pltpu.VMEM((rows, 2 * half), BF)],
        compiler_params=pltpu.CompilerParams(vmem_limit_bytes=VMEM_LIMIT),
        name="lift",
    )(at, ta, tb, here, got, other, gain, kva, kvb)


def two_parts(column):
    high = column.astype(BF)
    return high, (column - high.astype(F32)).astype(BF)


def finish_kernel(mine, got, squares, d_kv, kv, load):
    rows, cols = kv.shape
    total = mine[...].astype(F32) + got[...].astype(F32)
    mean = jnp.broadcast_to(squares[...], (rows, rows)).T[:, :1] * (1.0 / LLM_D)
    inv = lax.rsqrt(mean + 1e-05)
    low = (total * inv).astype(BF)
    kv[...] = low
    cot = (low.astype(F32) + d_kv[...].astype(F32)).astype(BF)
    load[:, :cols] = cot
    inner = jnp.sum(cot.astype(F32) * total, axis=1, keepdims=True)
    lane = lax.broadcasted_iota(jnp.int32, (rows, load.shape[1] - cols), 1)
    extra = jnp.zeros(lane.shape, F32)
    for i, part in enumerate(two_parts(inv) + two_parts(inner)):
        extra = jnp.where(lane == i, part.astype(F32), extra)
    load[:, cols:] = extra.astype(BF)


def finish(mine, got, squares, d_kv):
    rows, cols = mine.shape
    return pl.pallas_call(
        finish_kernel,
        out_shape=[
            jax.ShapeDtypeStruct((rows, cols), BF),
            jax.ShapeDtypeStruct((rows, cols + LANES), BF),
        ],
        compiler_params=pltpu.CompilerParams(vmem_limit_bytes=VMEM_LIMIT),
        name="finish",
    )(mine, got, squares, d_kv)


def lower_kernel(table, order, at, ca, cb, here, got, other, gain, kva, kvb, lifted, send, keep, nat):
    core, group = at[3], at[4]
    half = send.shape[1]
    feats = kva.shape[0]
    cols = kva.shape[1] // 2
    block = here.shape[2]
    starts = column_starts(order, at, block)
    near = pl.ds(pl.multiple_of(core * half, half), half)
    far = pl.ds(pl.multiple_of((1 - core) * half, half), half)
    piece = ca.shape[0] // len(table) if table else 0
    for rows in chunks_of(ca.shape[0]):
        extra = ca[rows, cols:].astype(F32)
        extra_b = cb[rows, cols:].astype(F32)
        inv = extra[:, 0:1] + extra[:, 1:2]
        inner = extra[:, 2:3] + extra[:, 3:4] + extra_b[:, 2:3] + extra_b[:, 3:4]
        pull = inv * inv * inv * inner * (1.0 / LLM_D)
        cots = ((ca[rows, :cols], core), (cb[rows, :cols], 1 - core))
        d_tok = None
        for bit in range(2):
            d_normed = None
            for cot, side in cots:
                span = pl.ds(pl.multiple_of(side * cols, cols), cols)
                part = dot_nt(cot, kvb[side ^ group] if bit else kva[:, span])
                d_normed = part if d_normed is None else d_normed + part
            span = slice(bit * feats, (bit + 1) * feats)
            low = (inv * gain[:, span] * d_normed - lifted[rows, span] * pull).astype(BF)
            weight = weight_rows(order, here, got, other, bit)
            part = dot_nt(low, weight)
            d_tok = part if d_tok is None else d_tok + part
        if not starts:
            nat[rows] = d_tok.astype(BF)
        for i, start in enumerate(starts or ()):
            nat[rows, pl.ds(start, block)] = d_tok[:, i * block : (i + 1) * block].astype(BF)
    for source_row, owner_row in table:
        send[source_row : source_row + piece] = nat[owner_row : owner_row + piece, far]
        keep[source_row : source_row + piece] = nat[owner_row : owner_row + piece, near]
    if not table:
        send[...] = nat[:, far]
        keep[...] = nat[:, near]


def lower(table, order, at, ca, cb, here, got, other, gain, kva, kvb, lifted):
    rows = ca.shape[0]
    width = 2 * here.shape[0] * here.shape[2]
    whole = pl.BlockSpec(memory_space=pltpu.VMEM)
    out = jax.ShapeDtypeStruct((rows, width // 2), BF)
    return pl.pallas_call(
        functools.partial(lower_kernel, table, order),
        in_specs=[pl.BlockSpec(memory_space=pltpu.SMEM)] + [whole] * 9,
        out_specs=[whole] * 2,
        out_shape=[out] * 2,
        scratch_shapes=[pltpu.VMEM((rows, width), BF)],
        compiler_params=pltpu.CompilerParams(vmem_limit_bytes=VMEM_LIMIT),
        name="lower",
    )(at, ca, cb, here, got, other, gain, kva, kvb, lifted)


def on_device(frames, weight_qkv, weight_out, proj_in, norm_gain, proj_kv, shifts, route, d_kv):
    n = lax.axis_size("tm")
    me = lax.axis_index("tm")
    core = lax.axis_index("mp")
    rows, width = frames.shape
    half_w = width // 2
    shift = shifts[0]
    own_tok = rows // POOL
    tail_tok = WINDOW // POOL
    ext_tok = own_tok + tail_tok
    feats = proj_kv.shape[0]
    kv_half = proj_kv.shape[1] // 2
    piece = own_tok // n

    part = lax.dynamic_slice_in_dim(frames, core * (WINDOW // 2), WINDOW // 2, 0)
    mine = to_tm(part, -1, False)
    w_t = jnp.transpose(weight_qkv, (1, 2, 0)).reshape(-1, width)
    proj_in, proj_kv, w_t = lax.optimization_barrier((proj_in, proj_kv, w_t))

    masks = group_bits()
    order = offsets(masks)
    members = order + [k | SPLIT for k in order]
    count = n // 2
    blocks = []
    for k in order:
        pair = [
            lax.dynamic_slice_in_dim(proj_in, (me ^ k ^ bit) * feats, feats, 1)
            for bit in (0, SPLIT)
        ]
        pair = jnp.stack(pair)
        blocks.append(swap_tm(pair, k) if k else pair)
    here = jnp.stack(blocks)
    group = lax.axis_index("groups")
    if lax.axis_size("groups") == 2:
        swap_groups = lambda block: lax.ppermute(block, "groups", [(0, 1), (1, 0)])
        kv_near = swap_tm(lax.dynamic_slice_in_dim(proj_kv, group * kv_half, kv_half, 1), SPLIT)
        kv_far = swap_groups(kv_near)
        in_near = swap_tm(
            lax.dynamic_slice_in_dim(here, group * (count // 2), count // 2, 0), SPLIT
        )
        in_far = swap_groups(in_near)
    else:
        group = group * 0
        kv_near = swap_tm(proj_kv[:, :kv_half], SPLIT)
        kv_far = swap_tm(proj_kv[:, kv_half:], SPLIT)
        in_near = swap_tm(here[: count // 2], SPLIT)
        in_far = swap_tm(here[count // 2 :], SPLIT)
    kva, kvb = proj_kv, jnp.stack([kv_near, kv_far])
    at_rows = order
    if width // n % LANES:
        stacked = jnp.concatenate([here, in_near[:, ::-1], in_far[:, ::-1]])
        source = jnp.arange(n, dtype=jnp.int32) ^ me
        found = source[:, None] == jnp.array(members, jnp.int32)[None, :]
        place = jnp.sum(found * jnp.arange(n, dtype=jnp.int32)[None, :], axis=1)
        stacked = jnp.take(stacked, place, axis=0)
        here, in_near, in_far = jnp.split(stacked, [count, count + count // 2])
        at_rows = None

    other = swap_mp(mine)
    halo = jnp.where(
        core == 0, jnp.concatenate([mine, other], 0), jnp.concatenate([other, mine], 0)
    )
    x_roll = lax.dynamic_slice_in_dim(jnp.concatenate([frames, halo], 0), shift, rows, 0)

    at = jnp.stack([shift, rows * n - shift - me * rows, me, core, group]).astype(jnp.int32)
    normed, qkv, probs, pooled_attn, out_part = encoder_forward(
        x_roll, w_t, weight_out, at, ext_tok
    )
    turned = normed.T
    route, norm_gain, d_kv, pooled_attn = lax.optimization_barrier(
        (route, norm_gain, d_kv, pooled_attn)
    )
    gain = jnp.concatenate(
        [
            lax.dynamic_slice_in_dim(norm_gain, (me ^ bit) * feats, feats, 0)
            for bit in (0, SPLIT)
        ]
    ).reshape(1, -1)
    owner_at = (lax.dynamic_index_in_dim(route, me, 0, keepdims=False) ^ me)[None, :]
    sort = owner_at == jnp.array(members, jnp.int32)[:, None]
    sort = jnp.kron(sort.astype(BF), jnp.eye(piece, dtype=BF))
    source_at = jnp.arange(n, dtype=jnp.int32) ^ me
    spread = source_at[:, None] == jnp.array(
        [k | bit for k in order for bit in (0, SPLIT)], jnp.int32
    )
    spread = jnp.kron(spread.astype(BF), jnp.eye(piece, dtype=BF))
    d_kv = dot_tn(spread, d_kv).astype(BF)

    out_low = out_part.astype(BF)
    low_own = lax.dynamic_slice_in_dim(out_low, core * half_w, half_w, 1)
    low_other = lax.dynamic_slice_in_dim(out_low, (1 - core) * half_w, half_w, 1)
    from_core = swap_mp(low_other[:own_tok])
    tail_a = to_tm(low_own[own_tok:], 1, False)
    tail_b = to_tm(low_other[own_tok:], 1, True)
    own_pool = (
        jnp.arange(rows, dtype=jnp.int32)[None, :] // POOL
        == jnp.arange(own_tok, dtype=jnp.int32)[:, None]
    ).astype(BF) * (1.0 / POOL)
    x_mean = dot(own_pool, lax.dynamic_slice_in_dim(frames, core * half_w, half_w, 1))
    pooled = (
        x_mean
        + lax.dynamic_slice_in_dim(out_part, core * half_w, half_w, 1)[:own_tok]
        + from_core.astype(F32)
    )
    tail = tail_a.astype(F32) + tail_b.astype(F32)
    pooled = jnp.concatenate([pooled[:tail_tok] + tail, pooled[tail_tok:]], 0).astype(BF)

    sorted_tok = dot(sort, pooled).astype(BF).reshape(2, count * piece, half_w)
    pair_tok = jnp.stack([sorted_tok[0], swap_tm(sorted_tok[1], SPLIT)])
    tok_half = gather_doubling(pair_tok, masks).reshape(-1, half_w)
    tok_other = swap_mp(tok_half)
    table = list(moves(order, piece))
    source_rows = np.concatenate([np.arange(r, r + piece) for r, _ in table])
    owner_rows = np.concatenate([np.arange(r, r + piece) for _, r in table])
    by_xla = piece % 16 != 0
    if by_xla:
        at_owner = source_rows[np.argsort(owner_rows)]
        tok_half, tok_other = tok_half[at_owner], tok_other[at_owner]
        table = []
    lifted, kv_send, kv_keep = lift(
        table, at_rows, at, tok_half, tok_other, here, in_near, in_far, gain, kva, kvb
    )
    squares = jnp.sum(lifted * lifted, axis=-1).reshape(count, own_tok)
    square_sum = scatter_halving(squares + swap_mp(squares), masks, F32)
    kv_part = kv_keep.astype(F32) + swap_mp(kv_send).astype(F32)
    kv_mine, kv_got = scatter_last(kv_part.reshape(count, own_tok, kv_half), masks)
    kv_low, load = finish(kv_mine, kv_got, square_sum.reshape(1, own_tok), d_kv)
    kv = dot(spread, kv_low).astype(BF)
    cot_half = gather_doubling(load, masks).reshape(count * own_tok, -1)
    cot_other = swap_mp(cot_half)
    d_send, d_keep = lower(
        table, at_rows, at, cot_half, cot_other, here, in_near, in_far, gain, kva, kvb, lifted
    )
    if by_xla:
        at_source = owner_rows[np.argsort(source_rows)]
        d_send, d_keep = d_send[at_source], d_keep[at_source]
    d_part = d_keep.astype(F32) + swap_mp(d_send).astype(F32)
    d_pair = scatter_halving(d_part.reshape(count, 2, count * piece, half_w), masks, BF)
    d_sorted = jnp.concatenate([d_pair[0].astype(BF), swap_tm(d_pair[1].astype(BF), SPLIT)], 0)
    d_half = dot_tn(sort, d_sorted).astype(BF)

    d_other = swap_mp(d_half)
    next_a = to_tm(d_half[:tail_tok], -1, False)
    next_b = to_tm(d_half[:tail_tok], -1, True)
    left = jnp.concatenate([d_half, next_a], 0)
    right = jnp.concatenate([d_other, next_b], 0)
    d_ext = jnp.where(
        core == 0, jnp.concatenate([left, right], 1), jnp.concatenate([right, left], 1)
    )
    d_attn, out_even, out_odd = out_grad(d_ext, weight_out, pooled_attn, at, n)
    grad_out = scatter_pair(out_even, out_odd)
    chunks, first = [], 0
    for pairs in (2, 1, 1):
        even, odd = encoder_backward(turned, qkv, probs, d_attn, at, n, first, pairs)
        chunks.append(scatter_pair(even, odd))
        first += pairs
    grad_qkv = jnp.transpose(jnp.concatenate(chunks, axis=-1), (1, 0, 2))
    return kv, grad_qkv, grad_out


def solution(mesh):
    in_specs = (
        P(("groups", "tm"), None),
        P(None, None, "mp"),
        P("mp", None),
        P("tm", "mp"),
        P("mp"),
        P(("mp", "tm"), None),
        P(),
        P(),
        P(("groups", "tm"), "mp"),
    )
    out_specs = (
        P(("groups", "tm"), "mp"),
        P(("groups", "tm"), None, "mp"),
        P(("groups", "mp", "tm"), None),
    )
    return jax.shard_map(
        on_device, mesh=mesh, in_specs=in_specs, out_specs=out_specs, check_vma=False
    )
```

```python
import functools

import jax
import jax.numpy as jnp
import numpy as np
from jax import lax
from jax.experimental import pallas as pl
from jax.experimental.pallas import tpu as pltpu
from jax.sharding import PartitionSpec as P

HEAD = 64
WINDOW = 256
POOL = 4
LLM_D = 8192
BF = jnp.bfloat16
F32 = jnp.float32
VMEM_LIMIT = 48 << 20
SPLIT = 1
CHUNK = 512
LANES = 128


def dot(a, b):
    return jnp.dot(a, b, preferred_element_type=F32)


def dot_nt(a, b):
    return lax.dot_general(a, b, (((1,), (1,)), ((), ())), preferred_element_type=F32)


def dot_tn(a, b):
    return lax.dot_general(a, b, (((0,), (0,)), ((), ())), preferred_element_type=F32)


def swap_tm(block, mask):
    n = lax.axis_size("tm")
    return lax.ppermute(block, "tm", [(i, i ^ mask) for i in range(n)])


def swap_mp(block):
    n = lax.axis_size("mp")
    return lax.ppermute(block, "mp", [(i, n - 1 - i) for i in range(n)])


def to_tm(block, step, cross):
    n, m = lax.axis_size("tm"), lax.axis_size("mp")
    pairs = []
    for i in range(n):
        for c in range(m):
            pairs.append((i * m + c, (i + step) % n * m + (m - 1 - c if cross else c)))
    return lax.ppermute(block, ("tm", "mp"), pairs)


def offsets(masks):
    order = [0]
    for mask in reversed(masks):
        order = order + [k | mask for k in order]
    return order


def tm_bits():
    n = lax.axis_size("tm")
    return [1 << i for i in range(n.bit_length() - 1)]


def group_bits():
    return [bit for bit in tm_bits() if bit != SPLIT]


def gather_doubling(block, masks):
    block = block[None]
    for mask in reversed(masks):
        block = jnp.concatenate([block, swap_tm(block, mask)], axis=0)
    return block


def scatter_halving(blocks, masks, kind):
    total = blocks
    for mask in masks:
        low = total.astype(kind)
        half = low.shape[0] // 2
        total = low[:half].astype(F32) + swap_tm(low[half:], mask).astype(F32)
    return total[0]


def scatter_last(blocks, masks):
    low = blocks.astype(BF)
    for i, mask in enumerate(masks):
        half = low.shape[0] // 2
        got = swap_tm(low[half:], mask)
        if i + 1 == len(masks):
            return low[0], got[0]
        low = (low[:half].astype(F32) + got.astype(F32)).astype(BF)


def scatter_chunks(chunks, lead):
    sums = [lower for lower, _, _ in chunks]
    sends = [upper for _, upper, _ in chunks]
    for stage in range(len(chunks[0][2])):
        for i, (_, _, masks) in enumerate(chunks):
            total = sums[i].astype(F32) + swap_tm(sends[i], masks[stage]).astype(F32)
            if total.shape[0] == 1:
                sums[i] = total[0]
                continue
            low = total.astype(BF)
            if i == lead:
                done = low
            if i + 1 == len(chunks):
                low, done = lax.optimization_barrier((low, done))
            half = low.shape[0] // 2
            sums[i], sends[i] = low[:half], low[half:]
    return sums


def head_mask(shape, head):
    return lax.broadcasted_iota(jnp.int32, shape, 1) // HEAD == head


def forward_kernel(at, x_ref, wq_ref, wk_ref, wv_ref, wo_ref, normed, qkv, probs, pooled, out, attn):
    shift, border = at[0], at[1]
    rows = x_ref.shape[0]
    cols = wq_ref.shape[0]

    @pl.when(pl.program_id(0) == 0)
    def _():
        x = x_ref[...].astype(F32)
        scale = lax.rsqrt(jnp.mean(x * x, axis=-1, keepdims=True) + 1e-05)
        normed[...] = (x * scale).astype(BF)
        out[...] = jnp.zeros_like(out)

    base = normed[...]
    for i, w_ref in enumerate((wq_ref, wk_ref, wv_ref)):
        qkv[i] = dot_nt(base, w_ref[...]).astype(BF)
    windows, heads = range(rows // WINDOW), range(cols // HEAD)
    spans = [pl.ds(w * WINDOW, WINDOW) for w in windows]
    own = [head_mask((WINDOW, cols), h) for h in heads]
    scores = []
    for w in windows:
        q, k = qkv[0, spans[w], :], qkv[1, spans[w], :]
        for h in heads:
            scores.append(dot_nt(jnp.where(own[h], k, jnp.zeros_like(k)), q))
    square = (WINDOW, WINDOW)
    key_at = lax.broadcasted_iota(jnp.int32, square, 0)
    query_at = lax.broadcasted_iota(jnp.int32, square, 1)
    lows = []
    for w in windows:
        edge = border - w * WINDOW
        allowed = (key_at >= edge) == (query_at >= edge)
        for h in heads:
            score = jnp.where(allowed, scores[w * len(heads) + h] * HEAD ** (-0.5), -1e30)
            terms = jnp.exp(score - jnp.max(score, axis=0, keepdims=True))
            low = (terms * (1.0 / jnp.sum(terms, axis=0, keepdims=True))).astype(BF)
            probs[0, w, h] = low
            lows.append(low)
    for w in windows:
        v = qkv[2, spans[w], :]
        attended = None
        for h in heads:
            part = dot_tn(lows[w * len(heads) + h], v)
            attended = part if attended is None else jnp.where(own[h], part, attended)
        attn[spans[w], :] = attended.astype(BF)
    tok_shape = (pooled.shape[0], rows)
    tok_of = (lax.broadcasted_iota(jnp.int32, tok_shape, 1) + shift) // POOL
    member = tok_of == lax.broadcasted_iota(jnp.int32, tok_shape, 0)
    pool = jnp.where(member, 1.0 / POOL, 0.0).astype(BF)
    low = dot(pool, attn[...]).astype(BF)
    pooled[...] = low
    out[...] += dot(low, wo_ref[...])


def encoder_forward(x_roll, w_t, weight_out, at, ext_tok):
    rows, width = x_roll.shape
    heads_w = weight_out.shape[0]
    cols = 2 * HEAD
    pairs = heads_w // cols
    windows = rows // WINDOW
    weight = lambda i: pl.BlockSpec((cols, width), lambda p, at: (i * pairs + p, 0))
    return pl.pallas_call(
        forward_kernel,
        grid_spec=pltpu.PrefetchScalarGridSpec(
            num_scalar_prefetch=1,
            grid=(pairs,),
            in_specs=[
                pl.BlockSpec((rows, width), lambda p, at: (0, 0)),
                weight(0),
                weight(1),
                weight(2),
                weight(0),
            ],
            out_specs=[
                pl.BlockSpec((rows, width), lambda p, at: (0, 0)),
                pl.BlockSpec((3, rows, cols), lambda p, at: (0, 0, p)),
                pl.BlockSpec((1, windows, 2, WINDOW, WINDOW), lambda p, at: (p, 0, 0, 0, 0)),
                pl.BlockSpec((ext_tok, cols), lambda p, at: (0, p)),
                pl.BlockSpec((ext_tok, width), lambda p, at: (0, 0)),
            ],
            scratch_shapes=[pltpu.VMEM((rows, cols), BF)],
        ),
        out_shape=[
            jax.ShapeDtypeStruct((rows, width), BF),
            jax.ShapeDtypeStruct((3, rows, heads_w), BF),
            jax.ShapeDtypeStruct((pairs, windows, 2, WINDOW, WINDOW), BF),
            jax.ShapeDtypeStruct((ext_tok, heads_w), BF),
            jax.ShapeDtypeStruct((ext_tok, width), F32),
        ],
        compiler_params=pltpu.CompilerParams(vmem_limit_bytes=VMEM_LIMIT),
        name="encoder_forward",
    )(at, x_roll, w_t, w_t, w_t, weight_out)


def out_grad_kernel(masks, at, d_ref, wo_ref, pa_ref, d_attn, even, odd, turned):
    me = at[2]
    block = even.shape[1]
    d_ext = d_ref[...]
    d_attn[...] = (dot_nt(d_ext, wo_ref[...]) * (1.0 / POOL)).astype(BF)
    turned[...] = pa_ref[...].T
    for bit, ref in ((0, even), (masks[0], odd)):
        for j, k in enumerate(offsets(masks[1:])):
            start = pl.multiple_of((me ^ (k | bit)) * block, block)
            ref[j] = dot(turned[pl.ds(start, block), :], d_ext).astype(BF)


def out_grad(d_ext, weight_out, pooled_attn, at, masks):
    heads_w, width = weight_out.shape
    n = 2 ** len(masks)
    blocks = jax.ShapeDtypeStruct((n // 2, heads_w // n, width), BF)
    whole = pl.BlockSpec(memory_space=pltpu.VMEM)
    return pl.pallas_call(
        functools.partial(out_grad_kernel, masks),
        in_specs=[pl.BlockSpec(memory_space=pltpu.SMEM), whole, whole, whole],
        out_specs=[whole] * 3,
        out_shape=[jax.ShapeDtypeStruct(pooled_attn.shape, BF), blocks, blocks],
        scratch_shapes=[pltpu.VMEM((heads_w, pooled_attn.shape[0]), BF)],
        compiler_params=pltpu.CompilerParams(vmem_limit_bytes=VMEM_LIMIT),
        name="out_grad",
    )(at, d_ext, weight_out, pooled_attn)


def backward_kernel(masks, at, turned, qkv, probs, d_ref, even, odd, grads):
    shift, me = at[0], at[2]
    rows = turned.shape[1]
    cols = d_ref.shape[1]
    block = even.shape[2]
    tok_shape = (rows, d_ref.shape[0])
    tok_of = (lax.broadcasted_iota(jnp.int32, tok_shape, 0) + shift) // POOL
    member = tok_of == lax.broadcasted_iota(jnp.int32, tok_shape, 1)
    d_rows = dot(jnp.where(member, 1.0, 0.0).astype(BF), d_ref[...]).astype(BF)
    for w in range(rows // WINDOW):
        span = pl.ds(w * WINDOW, WINDOW)
        q, k, v = qkv[0, span, :], qkv[1, span, :], qkv[2, span, :]
        d_out = d_rows[w * WINDOW : (w + 1) * WINDOW]
        none = jnp.zeros_like(q)
        sums = [0.0, 0.0, 0.0]
        for h in range(cols // HEAD):
            own = head_mask(q.shape, h)
            low = probs[0, w, h]
            weight = low.astype(F32)
            d_weight = dot_nt(jnp.where(own, v, none), d_out)
            centre = jnp.sum(weight * d_weight, axis=0, keepdims=True)
            d_score = (weight * (d_weight - centre) * HEAD ** (-0.5)).astype(BF)
            sums[0] += dot_tn(d_score, jnp.where(own, k, none))
            sums[1] += dot(d_score, jnp.where(own, q, none))
            sums[2] += dot(low, jnp.where(own, d_out, none))
        for i in range(3):
            grads[span, i * cols : (i + 1) * cols] = sums[i].astype(BF)
    d_all = grads[...]
    for bit, ref in ((0, even), (masks[0], odd)):
        for j, k in enumerate(offsets(masks[1:])):
            start = pl.multiple_of((me ^ (k | bit)) * block, block)
            term = dot(turned[pl.ds(start, block), :], d_all).astype(BF)
            for i in range(3):
                ref[j, i] = term[:, i * cols : (i + 1) * cols]


def encoder_backward(turned, qkv, probs, d_attn, at, masks, first, count):
    width, rows = turned.shape
    n = 2 ** len(masks)
    cols = 2 * HEAD
    windows = rows // WINDOW
    block = width // n
    out = pl.BlockSpec((n // 2, 3, block, cols), lambda p, at: (0, 0, 0, p))
    shape = jax.ShapeDtypeStruct((n // 2, 3, block, cols * count), BF)
    return pl.pallas_call(
        functools.partial(backward_kernel, masks),
        grid_spec=pltpu.PrefetchScalarGridSpec(
            num_scalar_prefetch=1,
            grid=(count,),
            in_specs=[
                pl.BlockSpec((width, rows), lambda p, at: (0, 0)),
                pl.BlockSpec((3, rows, cols), lambda p, at: (0, 0, p + first)),
                pl.BlockSpec(
                    (1, windows, 2, WINDOW, WINDOW), lambda p, at: (p + first, 0, 0, 0, 0)
                ),
                pl.BlockSpec((d_attn.shape[0], cols), lambda p, at: (0, p + first)),
            ],
            out_specs=[out, out],
            scratch_shapes=[pltpu.VMEM((rows, 3 * cols), BF)],
        ),
        out_shape=[shape, shape],
        compiler_params=pltpu.CompilerParams(vmem_limit_bytes=VMEM_LIMIT),
        name="encoder_backward",
    )(at, turned, qkv, probs, d_attn)


def moves(order, piece):
    count = len(order)
    for e, offset in enumerate(order):
        for b in range(2):
            for i, step in enumerate(order):
                owner = order.index(offset ^ step)
                source_row = ((e * 2 + b) * count + i) * piece
                owner_row = ((owner * count + i) * 2 + b) * piece
                yield source_row, owner_row


def chunks_of(rows):
    return [slice(r, min(r + CHUNK, rows)) for r in range(0, rows, CHUNK)]


def column_starts(order, at, block):
    if order is None:
        return None
    me, group = at[2], at[4]
    part = len(order) // 2
    across = [
        jnp.where(group == q, order[i], order[part + i]) | SPLIT
        for q in range(2)
        for i in range(part)
    ]
    return [pl.multiple_of((me ^ k) * block, block) for k in order + across]


def weight_rows(order, here, got, other, bit):
    flat = lambda w: w.reshape(-1, w.shape[-1])
    across = bit if order is None else 1 - bit
    parts = [flat(here[:, bit]), flat(got[:, across]), flat(other[:, across])]
    return jnp.concatenate(parts, axis=0)


def lift_kernel(table, order, at, ta, tb, here, got, other, gain, kva, kvb, lifted, send, keep, tok):
    core, group = at[3], at[4]
    half = ta.shape[1]
    feats = kva.shape[0]
    cols = send.shape[1]
    rows_all = ta.shape[0]
    near = pl.ds(pl.multiple_of(core * half, half), half)
    far = pl.ds(pl.multiple_of((1 - core) * half, half), half)
    piece = rows_all // len(table) if table else 0
    for source_row, owner_row in table:
        tok[owner_row : owner_row + piece, near] = ta[source_row : source_row + piece]
        tok[owner_row : owner_row + piece, far] = tb[source_row : source_row + piece]
    if not table:
        tok[:, near] = ta[...]
        tok[:, far] = tb[...]
    block = here.shape[2]
    starts = column_starts(order, at, block)
    for rows in chunks_of(rows_all):
        x = tok[rows]
        if starts:
            x = jnp.concatenate([tok[rows, pl.ds(start, block)] for start in starts], axis=1)
        lows = []
        for bit in range(2):
            span = slice(bit * feats, (bit + 1) * feats)
            weight = weight_rows(order, here, got, other, bit)
            product = dot(x, weight)
            lifted[rows, span] = product
            lows.append((product * gain[:, span]).astype(BF))
        for ref, side in ((send, 1 - core), (keep, core)):
            span = pl.ds(pl.multiple_of(side * cols, cols), cols)
            part = dot(lows[0], kva[:, span]) + dot(lows[1], kvb[side ^ group])
            ref[rows] = part.astype(BF)


def lift(table, order, at, ta, tb, here, got, other, gain, kva, kvb):
    rows, half = ta.shape
    feats, cols = kva.shape[0], kva.shape[1] // 2
    whole = pl.BlockSpec(memory_space=pltpu.VMEM)
    return pl.pallas_call(
        functools.partial(lift_kernel, table, order),
        in_specs=[pl.BlockSpec(memory_space=pltpu.SMEM)] + [whole] * 8,
        out_specs=[whole] * 3,
        out_shape=[
            jax.ShapeDtypeStruct((rows, 2 * feats), F32),
            jax.ShapeDtypeStruct((rows, cols), BF),
            jax.ShapeDtypeStruct((rows, cols), BF),
        ],
        scratch_shapes=[pltpu.VMEM((rows, 2 * half), BF)],
        compiler_params=pltpu.CompilerParams(vmem_limit_bytes=VMEM_LIMIT),
        name="lift",
    )(at, ta, tb, here, got, other, gain, kva, kvb)


def two_parts(column):
    high = column.astype(BF)
    return high, (column - high.astype(F32)).astype(BF)


def finish_kernel(mine, got, squares, d_kv, kv, load):
    rows, cols = kv.shape
    total = mine[...].astype(F32) + got[...].astype(F32)
    mean = jnp.broadcast_to(squares[...], (rows, rows)).T[:, :1] * (1.0 / LLM_D)
    inv = lax.rsqrt(mean + 1e-05)
    low = (total * inv).astype(BF)
    kv[...] = low
    cot = (low.astype(F32) + d_kv[...].astype(F32)).astype(BF)
    load[:, :cols] = cot
    inner = jnp.sum(cot.astype(F32) * total, axis=1, keepdims=True)
    lane = lax.broadcasted_iota(jnp.int32, (rows, load.shape[1] - cols), 1)
    extra = jnp.zeros(lane.shape, F32)
    for i, part in enumerate(two_parts(inv) + two_parts(inner)):
        extra = jnp.where(lane == i, part.astype(F32), extra)
    load[:, cols:] = extra.astype(BF)


def finish(mine, got, squares, d_kv):
    rows, cols = mine.shape
    return pl.pallas_call(
        finish_kernel,
        out_shape=[
            jax.ShapeDtypeStruct((rows, cols), BF),
            jax.ShapeDtypeStruct((rows, cols + LANES), BF),
        ],
        compiler_params=pltpu.CompilerParams(vmem_limit_bytes=VMEM_LIMIT),
        name="finish",
    )(mine, got, squares, d_kv)


def lower_kernel(table, order, at, ca, cb, here, got, other, gain, kva, kvb, lifted, send, keep, nat):
    core, group = at[3], at[4]
    half = send.shape[1]
    feats = kva.shape[0]
    cols = kva.shape[1] // 2
    block = here.shape[2]
    starts = column_starts(order, at, block)
    near = pl.ds(pl.multiple_of(core * half, half), half)
    far = pl.ds(pl.multiple_of((1 - core) * half, half), half)
    piece = ca.shape[0] // len(table) if table else 0
    for rows in chunks_of(ca.shape[0]):
        extra = ca[rows, cols:].astype(F32)
        extra_b = cb[rows, cols:].astype(F32)
        inv = extra[:, 0:1] + extra[:, 1:2]
        inner = extra[:, 2:3] + extra[:, 3:4] + extra_b[:, 2:3] + extra_b[:, 3:4]
        pull = inv * inv * inv * inner * (1.0 / LLM_D)
        cots = ((ca[rows, :cols], core), (cb[rows, :cols], 1 - core))
        d_tok = None
        for bit in range(2):
            d_normed = None
            for cot, side in cots:
                span = pl.ds(pl.multiple_of(side * cols, cols), cols)
                part = dot_nt(cot, kvb[side ^ group] if bit else kva[:, span])
                d_normed = part if d_normed is None else d_normed + part
            span = slice(bit * feats, (bit + 1) * feats)
            low = (inv * gain[:, span] * d_normed - lifted[rows, span] * pull).astype(BF)
            weight = weight_rows(order, here, got, other, bit)
            part = dot_nt(low, weight)
            d_tok = part if d_tok is None else d_tok + part
        if not starts:
            nat[rows] = d_tok.astype(BF)
        for i, start in enumerate(starts or ()):
            nat[rows, pl.ds(start, block)] = d_tok[:, i * block : (i + 1) * block].astype(BF)
    for source_row, owner_row in table:
        send[source_row : source_row + piece] = nat[owner_row : owner_row + piece, far]
        keep[source_row : source_row + piece] = nat[owner_row : owner_row + piece, near]
    if not table:
        send[...] = nat[:, far]
        keep[...] = nat[:, near]


def lower(table, order, at, ca, cb, here, got, other, gain, kva, kvb, lifted):
    rows = ca.shape[0]
    width = 2 * here.shape[0] * here.shape[2]
    whole = pl.BlockSpec(memory_space=pltpu.VMEM)
    out = jax.ShapeDtypeStruct((rows, width // 2), BF)
    return pl.pallas_call(
        functools.partial(lower_kernel, table, order),
        in_specs=[pl.BlockSpec(memory_space=pltpu.SMEM)] + [whole] * 9,
        out_specs=[whole] * 2,
        out_shape=[out] * 2,
        scratch_shapes=[pltpu.VMEM((rows, width), BF)],
        compiler_params=pltpu.CompilerParams(vmem_limit_bytes=VMEM_LIMIT),
        name="lower",
    )(at, ca, cb, here, got, other, gain, kva, kvb, lifted)


def on_device(frames, weight_qkv, weight_out, proj_in, norm_gain, proj_kv, shifts, route, d_kv):
    n = lax.axis_size("tm")
    me = lax.axis_index("tm")
    core = lax.axis_index("mp")
    rows, width = frames.shape
    half_w = width // 2
    shift = shifts[0]
    own_tok = rows // POOL
    tail_tok = WINDOW // POOL
    ext_tok = own_tok + tail_tok
    feats = proj_kv.shape[0]
    kv_half = proj_kv.shape[1] // 2
    piece = own_tok // n

    part = lax.dynamic_slice_in_dim(frames, core * (WINDOW // 2), WINDOW // 2, 0)
    mine = to_tm(part, -1, False)
    w_t = jnp.transpose(weight_qkv, (1, 2, 0)).reshape(-1, width)
    group = lax.axis_index("groups")
    two_groups = lax.axis_size("groups") == 2
    if not two_groups:
        group = group * 0
    proj_kv, part = lax.optimization_barrier((proj_kv, part))
    kv_near = swap_tm(lax.dynamic_slice_in_dim(proj_kv, group * kv_half, kv_half, 1), SPLIT)
    proj_in, w_t = lax.optimization_barrier((proj_in, w_t))

    masks = group_bits()
    order = offsets(masks)
    members = order + [k | SPLIT for k in order]
    count = n // 2
    blocks = []
    for k in order:
        pair = [
            lax.dynamic_slice_in_dim(proj_in, (me ^ k ^ bit) * feats, feats, 1)
            for bit in (0, SPLIT)
        ]
        pair = jnp.stack(pair)
        blocks.append(swap_tm(pair, k) if k else pair)

    other = swap_mp(mine)
    halo = jnp.where(
        core == 0, jnp.concatenate([mine, other], 0), jnp.concatenate([other, mine], 0)
    )
    x_roll = lax.dynamic_slice_in_dim(jnp.concatenate([frames, halo], 0), shift, rows, 0)

    at = jnp.stack([shift, rows * n - shift - me * rows, me, core, group]).astype(jnp.int32)
    normed, qkv, probs, pooled_attn, out_part = encoder_forward(
        x_roll, w_t, weight_out, at, ext_tok
    )
    out_part, kv_near = lax.optimization_barrier((out_part, kv_near))
    swap_groups = lambda block: lax.ppermute(block, "groups", [(0, 1), (1, 0)])
    if two_groups:
        kv_far = swap_groups(kv_near)
    else:
        kv_far = swap_tm(proj_kv[:, kv_half:], SPLIT)
    turned = normed.T
    route, norm_gain, d_kv, pooled_attn = lax.optimization_barrier(
        (route, norm_gain, d_kv, pooled_attn)
    )
    gain = jnp.concatenate(
        [
            lax.dynamic_slice_in_dim(norm_gain, (me ^ bit) * feats, feats, 0)
            for bit in (0, SPLIT)
        ]
    ).reshape(1, -1)
    owner_at = (lax.dynamic_index_in_dim(route, me, 0, keepdims=False) ^ me)[None, :]
    sort = owner_at == jnp.array(members, jnp.int32)[:, None]
    sort = jnp.kron(sort.astype(BF), jnp.eye(piece, dtype=BF))
    source_at = jnp.arange(n, dtype=jnp.int32) ^ me
    spread = source_at[:, None] == jnp.array(
        [k | bit for k in order for bit in (0, SPLIT)], jnp.int32
    )
    spread = jnp.kron(spread.astype(BF), jnp.eye(piece, dtype=BF))
    d_kv = dot_tn(spread, d_kv).astype(BF)

    out_low = out_part.astype(BF)
    low_own = lax.dynamic_slice_in_dim(out_low, core * half_w, half_w, 1)
    low_other = lax.dynamic_slice_in_dim(out_low, (1 - core) * half_w, half_w, 1)
    from_core = swap_mp(low_other[:own_tok])
    tail_a = to_tm(low_own[own_tok:], 1, False)
    tail_b = to_tm(low_other[own_tok:], 1, True)
    tail_a, tail_b, from_core, blocks = lax.optimization_barrier(
        (tail_a, tail_b, from_core, blocks)
    )
    here = jnp.stack(blocks)
    in_near = swap_tm(
        lax.dynamic_slice_in_dim(here, group * (count // 2), count // 2, 0), SPLIT
    )
    in_far = swap_groups(in_near) if two_groups else swap_tm(here[count // 2 :], SPLIT)
    kva, kvb = proj_kv, jnp.stack([kv_near, kv_far])
    at_rows = order
    if width // n % LANES:
        stacked = jnp.concatenate([here, in_near[:, ::-1], in_far[:, ::-1]])
        source = jnp.arange(n, dtype=jnp.int32) ^ me
        found = source[:, None] == jnp.array(members, jnp.int32)[None, :]
        place = jnp.sum(found * jnp.arange(n, dtype=jnp.int32)[None, :], axis=1)
        stacked = jnp.take(stacked, place, axis=0)
        here, in_near, in_far = jnp.split(stacked, [count, count + count // 2])
        at_rows = None
    own_pool = (
        jnp.arange(rows, dtype=jnp.int32)[None, :] // POOL
        == jnp.arange(own_tok, dtype=jnp.int32)[:, None]
    ).astype(BF) * (1.0 / POOL)
    x_mean = dot(own_pool, lax.dynamic_slice_in_dim(frames, core * half_w, half_w, 1))
    pooled = (
        x_mean
        + lax.dynamic_slice_in_dim(out_part, core * half_w, half_w, 1)[:own_tok]
        + from_core.astype(F32)
    )
    tail = tail_a.astype(F32) + tail_b.astype(F32)
    pooled = jnp.concatenate([pooled[:tail_tok] + tail, pooled[tail_tok:]], 0).astype(BF)

    sorted_tok = dot(sort, pooled).astype(BF).reshape(2, count * piece, half_w)
    pair_tok = jnp.stack([sorted_tok[0], swap_tm(sorted_tok[1], SPLIT)])
    tok_half = gather_doubling(pair_tok, masks).reshape(-1, half_w)
    tok_other = swap_mp(tok_half)
    table = list(moves(order, piece))
    source_rows = np.concatenate([np.arange(r, r + piece) for r, _ in table])
    owner_rows = np.concatenate([np.arange(r, r + piece) for _, r in table])
    by_xla = piece % 16 != 0
    if by_xla:
        at_owner = source_rows[np.argsort(owner_rows)]
        tok_half, tok_other = tok_half[at_owner], tok_other[at_owner]
        table = []
    lifted, kv_send, kv_keep = lift(
        table, at_rows, at, tok_half, tok_other, here, in_near, in_far, gain, kva, kvb
    )
    squares = jnp.sum(lifted * lifted, axis=-1).reshape(count, own_tok)
    square_sum = scatter_halving(squares + swap_mp(squares), masks, F32)
    kv_part = kv_keep.astype(F32) + swap_mp(kv_send).astype(F32)
    kv_mine, kv_got = scatter_last(kv_part.reshape(count, own_tok, kv_half), masks)
    kv_low, load = finish(kv_mine, kv_got, square_sum.reshape(1, own_tok), d_kv)
    kv = dot(spread, kv_low).astype(BF)
    cot_half = gather_doubling(load, masks).reshape(count * own_tok, -1)
    cot_other = swap_mp(cot_half)
    d_send, d_keep = lower(
        table, at_rows, at, cot_half, cot_other, here, in_near, in_far, gain, kva, kvb, lifted
    )
    if by_xla:
        at_source = owner_rows[np.argsort(source_rows)]
        d_send, d_keep = d_send[at_source], d_keep[at_source]
    d_part = d_keep.astype(F32) + swap_mp(d_send).astype(F32)
    d_pair = scatter_halving(d_part.reshape(count, 2, count * piece, half_w), masks, BF)
    d_sorted = jnp.concatenate([d_pair[0].astype(BF), swap_tm(d_pair[1].astype(BF), SPLIT)], 0)
    d_half = dot_tn(sort, d_sorted).astype(BF)

    d_other = swap_mp(d_half)
    next_a = to_tm(d_half[:tail_tok], -1, False)
    next_b = to_tm(d_half[:tail_tok], -1, True)
    left = jnp.concatenate([d_half, next_a], 0)
    right = jnp.concatenate([d_other, next_b], 0)
    d_ext = jnp.where(
        core == 0, jnp.concatenate([left, right], 1), jnp.concatenate([right, left], 1)
    )
    bits = tm_bits()
    crossed = [bits[1], bits[0]] + bits[2:]
    d_attn, out_even, out_odd = out_grad(d_ext, weight_out, pooled_attn, at, bits)
    chunks = []
    for pair, path in enumerate((bits, crossed, bits, bits)):
        even, odd = encoder_backward(turned, qkv, probs, d_attn, at, path, pair, 1)
        even, odd, at = lax.optimization_barrier((even, odd, at))
        chunks.append((even, odd, path))
    chunks.insert(2, (out_even, out_odd, bits))
    chunks = scatter_chunks(chunks, 2)
    grad_out = chunks.pop(2)
    grad_qkv = jnp.transpose(jnp.concatenate(chunks, axis=-1), (1, 0, 2))
    return kv, grad_qkv, grad_out


def solution(mesh):
    in_specs = (
        P(("groups", "tm"), None),
        P(None, None, "mp"),
        P("mp", None),
        P("tm", "mp"),
        P("mp"),
        P(("mp", "tm"), None),
        P(),
        P(),
        P(("groups", "tm"), "mp"),
    )
    out_specs = (
        P(("groups", "tm"), "mp"),
        P(("groups", "tm"), None, "mp"),
        P(("groups", "mp", "tm"), None),
    )
    return jax.shard_map(
        on_device, mesh=mesh, in_specs=in_specs, out_specs=out_specs, check_vma=False
    )
```

```python
import functools

import jax
import jax.numpy as jnp
import numpy as np
from jax import lax
from jax.experimental import pallas as pl
from jax.experimental.pallas import tpu as pltpu
from jax.sharding import PartitionSpec as P

HEAD = 64
WINDOW = 256
POOL = 4
LLM_D = 8192
BF = jnp.bfloat16
F32 = jnp.float32
VMEM_LIMIT = 48 << 20
SPLIT = 1
CHUNK = 512
LANES = 128


def dot(a, b):
    return jnp.dot(a, b, preferred_element_type=F32)


def dot_nt(a, b):
    return lax.dot_general(a, b, (((1,), (1,)), ((), ())), preferred_element_type=F32)


def dot_tn(a, b):
    return lax.dot_general(a, b, (((0,), (0,)), ((), ())), preferred_element_type=F32)


def swap_tm(block, mask):
    n = lax.axis_size("tm")
    return lax.ppermute(block, "tm", [(i, i ^ mask) for i in range(n)])


def swap_mp(block):
    n = lax.axis_size("mp")
    return lax.ppermute(block, "mp", [(i, n - 1 - i) for i in range(n)])


def to_tm(block, step, cross):
    n, m = lax.axis_size("tm"), lax.axis_size("mp")
    pairs = []
    for i in range(n):
        for c in range(m):
            pairs.append((i * m + c, (i + step) % n * m + (m - 1 - c if cross else c)))
    return lax.ppermute(block, ("tm", "mp"), pairs)


def offsets(masks):
    order = [0]
    for mask in reversed(masks):
        order = order + [k | mask for k in order]
    return order


def tm_bits():
    n = lax.axis_size("tm")
    return [1 << i for i in range(n.bit_length() - 1)]


def group_bits():
    return [bit for bit in tm_bits() if bit != SPLIT]


def gather_doubling(block, masks):
    block = block[None]
    for mask in reversed(masks):
        block = jnp.concatenate([block, swap_tm(block, mask)], axis=0)
    return block


def scatter_halving(blocks, masks, kind):
    total = blocks
    for mask in masks:
        low = total.astype(kind)
        half = low.shape[0] // 2
        total = low[:half].astype(F32) + swap_tm(low[half:], mask).astype(F32)
    return total[0]


def scatter_last(blocks, masks):
    low = blocks.astype(BF)
    for i, mask in enumerate(masks):
        half = low.shape[0] // 2
        got = swap_tm(low[half:], mask)
        if i + 1 == len(masks):
            return low[0], got[0]
        low = (low[:half].astype(F32) + got.astype(F32)).astype(BF)


def scatter_chunks(chunks):
    sums = [lower for lower, _, _ in chunks]
    sends = [upper for _, upper, _ in chunks]
    stages = len(chunks[0][2])
    steps = [(i + 1.5 * t, -t, i) for i in range(len(chunks)) for t in range(stages)]
    last = None
    for _, t, i in sorted(steps):
        got = swap_tm(sends[i], chunks[i][2][-t])
        if last is not None:
            got, _ = lax.optimization_barrier((got, last))
        total = sums[i].astype(F32) + got.astype(F32)
        if total.shape[0] == 1:
            sums[i] = total[0]
            continue
        low = last = total.astype(BF)
        half = low.shape[0] // 2
        sums[i], sends[i] = low[:half], low[half:]
    return sums


def head_mask(shape, head):
    return lax.broadcasted_iota(jnp.int32, shape, 1) // HEAD == head


def forward_kernel(at, x_ref, wq_ref, wk_ref, wv_ref, wo_ref, normed, qkv, probs, pooled, out, attn):
    shift, border = at[0], at[1]
    rows = x_ref.shape[0]
    cols = wq_ref.shape[0]

    @pl.when(pl.program_id(0) == 0)
    def _():
        x = x_ref[...].astype(F32)
        scale = lax.rsqrt(jnp.mean(x * x, axis=-1, keepdims=True) + 1e-05)
        normed[...] = (x * scale).astype(BF)
        out[...] = jnp.zeros_like(out)

    base = normed[...]
    for i, w_ref in enumerate((wq_ref, wk_ref, wv_ref)):
        qkv[i] = dot_nt(base, w_ref[...]).astype(BF)
    windows, heads = range(rows // WINDOW), range(cols // HEAD)
    spans = [pl.ds(w * WINDOW, WINDOW) for w in windows]
    own = [head_mask((WINDOW, cols), h) for h in heads]
    scores = []
    for w in windows:
        q, k = qkv[0, spans[w], :], qkv[1, spans[w], :]
        for h in heads:
            scores.append(dot_nt(jnp.where(own[h], k, jnp.zeros_like(k)), q))
    square = (WINDOW, WINDOW)
    key_at = lax.broadcasted_iota(jnp.int32, square, 0)
    query_at = lax.broadcasted_iota(jnp.int32, square, 1)
    lows = []
    for w in windows:
        edge = border - w * WINDOW
        allowed = (key_at >= edge) == (query_at >= edge)
        for h in heads:
            score = jnp.where(allowed, scores[w * len(heads) + h] * HEAD ** (-0.5), -1e30)
            terms = jnp.exp(score - jnp.max(score, axis=0, keepdims=True))
            low = (terms * (1.0 / jnp.sum(terms, axis=0, keepdims=True))).astype(BF)
            probs[0, w, h] = low
            lows.append(low)
    for w in windows:
        v = qkv[2, spans[w], :]
        attended = None
        for h in heads:
            part = dot_tn(lows[w * len(heads) + h], v)
            attended = part if attended is None else jnp.where(own[h], part, attended)
        attn[spans[w], :] = attended.astype(BF)
    tok_shape = (pooled.shape[0], rows)
    tok_of = (lax.broadcasted_iota(jnp.int32, tok_shape, 1) + shift) // POOL
    member = tok_of == lax.broadcasted_iota(jnp.int32, tok_shape, 0)
    pool = jnp.where(member, 1.0 / POOL, 0.0).astype(BF)
    low = dot(pool, attn[...]).astype(BF)
    pooled[...] = low
    out[...] += dot(low, wo_ref[...])


def encoder_forward(x_roll, w_t, weight_out, at, ext_tok):
    rows, width = x_roll.shape
    heads_w = weight_out.shape[0]
    cols = 2 * HEAD
    pairs = heads_w // cols
    windows = rows // WINDOW
    weight = lambda i: pl.BlockSpec((cols, width), lambda p, at: (i * pairs + p, 0))
    return pl.pallas_call(
        forward_kernel,
        grid_spec=pltpu.PrefetchScalarGridSpec(
            num_scalar_prefetch=1,
            grid=(pairs,),
            in_specs=[
                pl.BlockSpec((rows, width), lambda p, at: (0, 0)),
                weight(0),
                weight(1),
                weight(2),
                weight(0),
            ],
            out_specs=[
                pl.BlockSpec((rows, width), lambda p, at: (0, 0)),
                pl.BlockSpec((3, rows, cols), lambda p, at: (0, 0, p)),
                pl.BlockSpec((1, windows, 2, WINDOW, WINDOW), lambda p, at: (p, 0, 0, 0, 0)),
                pl.BlockSpec((ext_tok, cols), lambda p, at: (0, p)),
                pl.BlockSpec((ext_tok, width), lambda p, at: (0, 0)),
            ],
            scratch_shapes=[pltpu.VMEM((rows, cols), BF)],
        ),
        out_shape=[
            pltpu.HBM((rows, width), BF),
            pltpu.HBM((3, rows, heads_w), BF),
            pltpu.HBM((pairs, windows, 2, WINDOW, WINDOW), BF),
            pltpu.HBM((ext_tok, heads_w), BF),
            jax.ShapeDtypeStruct((ext_tok, width), F32),
        ],
        compiler_params=pltpu.CompilerParams(vmem_limit_bytes=VMEM_LIMIT),
        name="encoder_forward",
    )(at, x_roll, w_t, w_t, w_t, weight_out)


def out_grad_kernel(masks, at, d_ref, wo_ref, pa_ref, d_attn, even, odd, turned):
    me = at[2]
    block = even.shape[1]
    d_ext = d_ref[...]
    d_attn[...] = (dot_nt(d_ext, wo_ref[...]) * (1.0 / POOL)).astype(BF)
    turned[...] = pa_ref[...].T
    for bit, ref in ((0, even), (masks[0], odd)):
        for j, k in enumerate(offsets(masks[1:])):
            start = pl.multiple_of((me ^ (k | bit)) * block, block)
            ref[j] = dot(turned[pl.ds(start, block), :], d_ext).astype(BF)


def out_grad(d_ext, weight_out, pooled_attn, at, masks):
    heads_w, width = weight_out.shape
    n = 2 ** len(masks)
    blocks = jax.ShapeDtypeStruct((n // 2, heads_w // n, width), BF)
    whole = pl.BlockSpec(memory_space=pltpu.VMEM)
    return pl.pallas_call(
        functools.partial(out_grad_kernel, masks),
        in_specs=[pl.BlockSpec(memory_space=pltpu.SMEM), whole, whole, whole],
        out_specs=[whole] * 3,
        out_shape=[jax.ShapeDtypeStruct(pooled_attn.shape, BF), blocks, blocks],
        scratch_shapes=[pltpu.VMEM((heads_w, pooled_attn.shape[0]), BF)],
        compiler_params=pltpu.CompilerParams(vmem_limit_bytes=VMEM_LIMIT),
        name="out_grad",
    )(at, d_ext, weight_out, pooled_attn)


def backward_kernel(masks, at, turned, qkv, probs, d_ref, even, odd, grads):
    shift, me = at[0], at[2]
    rows = turned.shape[1]
    cols = d_ref.shape[1]
    block = even.shape[2]
    tok_shape = (rows, d_ref.shape[0])
    tok_of = (lax.broadcasted_iota(jnp.int32, tok_shape, 0) + shift) // POOL
    member = tok_of == lax.broadcasted_iota(jnp.int32, tok_shape, 1)
    d_rows = dot(jnp.where(member, 1.0, 0.0).astype(BF), d_ref[...]).astype(BF)
    for w in range(rows // WINDOW):
        span = pl.ds(w * WINDOW, WINDOW)
        q, k, v = qkv[0, span, :], qkv[1, span, :], qkv[2, span, :]
        d_out = d_rows[w * WINDOW : (w + 1) * WINDOW]
        none = jnp.zeros_like(q)
        sums = [0.0, 0.0, 0.0]
        for h in range(cols // HEAD):
            own = head_mask(q.shape, h)
            low = probs[0, w, h]
            weight = low.astype(F32)
            d_weight = dot_nt(jnp.where(own, v, none), d_out)
            centre = jnp.sum(weight * d_weight, axis=0, keepdims=True)
            d_score = (weight * (d_weight - centre) * HEAD ** (-0.5)).astype(BF)
            sums[0] += dot_tn(d_score, jnp.where(own, k, none))
            sums[1] += dot(d_score, jnp.where(own, q, none))
            sums[2] += dot(low, jnp.where(own, d_out, none))
        for i in range(3):
            grads[span, i * cols : (i + 1) * cols] = sums[i].astype(BF)
    d_all = grads[...]
    for bit, ref in ((0, even), (masks[0], odd)):
        for j, k in enumerate(offsets(masks[1:])):
            start = pl.multiple_of((me ^ (k | bit)) * block, block)
            term = dot(turned[pl.ds(start, block), :], d_all).astype(BF)
            for i in range(3):
                ref[j, i] = term[:, i * cols : (i + 1) * cols]


def encoder_backward(turned, qkv, probs, d_attn, at, masks, first, count):
    width, rows = turned.shape
    n = 2 ** len(masks)
    cols = 2 * HEAD
    windows = rows // WINDOW
    block = width // n
    out = pl.BlockSpec((n // 2, 3, block, cols), lambda p, at: (0, 0, 0, p))
    shape = jax.ShapeDtypeStruct((n // 2, 3, block, cols * count), BF)
    return pl.pallas_call(
        functools.partial(backward_kernel, masks),
        grid_spec=pltpu.PrefetchScalarGridSpec(
            num_scalar_prefetch=1,
            grid=(count,),
            in_specs=[
                pl.BlockSpec((width, rows), lambda p, at: (0, 0)),
                pl.BlockSpec((3, rows, cols), lambda p, at: (0, 0, p + first)),
                pl.BlockSpec(
                    (1, windows, 2, WINDOW, WINDOW), lambda p, at: (p + first, 0, 0, 0, 0)
                ),
                pl.BlockSpec((d_attn.shape[0], cols), lambda p, at: (0, p + first)),
            ],
            out_specs=[out, out],
            scratch_shapes=[pltpu.VMEM((rows, 3 * cols), BF)],
        ),
        out_shape=[shape, shape],
        compiler_params=pltpu.CompilerParams(vmem_limit_bytes=VMEM_LIMIT),
        name="encoder_backward",
    )(at, turned, qkv, probs, d_attn)


def moves(order, piece):
    count = len(order)
    for e, offset in enumerate(order):
        for b in range(2):
            for i, step in enumerate(order):
                owner = order.index(offset ^ step)
                source_row = ((e * 2 + b) * count + i) * piece
                owner_row = ((owner * count + i) * 2 + b) * piece
                yield source_row, owner_row


def chunks_of(rows):
    return [slice(r, min(r + CHUNK, rows)) for r in range(0, rows, CHUNK)]


def column_starts(order, at, block):
    if order is None:
        return None
    me, group = at[2], at[4]
    part = len(order) // 2
    across = [
        jnp.where(group == q, order[i], order[part + i]) | SPLIT
        for q in range(2)
        for i in range(part)
    ]
    return [pl.multiple_of((me ^ k) * block, block) for k in order + across]


def weight_rows(order, here, got, other, bit):
    flat = lambda w: w.reshape(-1, w.shape[-1])
    across = bit if order is None else 1 - bit
    parts = [flat(here[:, bit]), flat(got[:, across]), flat(other[:, across])]
    return jnp.concatenate(parts, axis=0)


def lift_kernel(table, order, at, ta, tb, here, got, other, gain, kva, kvb, lifted, send, keep, tok):
    core, group = at[3], at[4]
    half = ta.shape[1]
    feats = kva.shape[0]
    cols = send.shape[1]
    rows_all = ta.shape[0]
    near = pl.ds(pl.multiple_of(core * half, half), half)
    far = pl.ds(pl.multiple_of((1 - core) * half, half), half)
    piece = rows_all // len(table) if table else 0
    for source_row, owner_row in table:
        tok[owner_row : owner_row + piece, near] = ta[source_row : source_row + piece]
        tok[owner_row : owner_row + piece, far] = tb[source_row : source_row + piece]
    if not table:
        tok[:, near] = ta[...]
        tok[:, far] = tb[...]
    block = here.shape[2]
    starts = column_starts(order, at, block)
    for rows in chunks_of(rows_all):
        x = tok[rows]
        if starts:
            x = jnp.concatenate([tok[rows, pl.ds(start, block)] for start in starts], axis=1)
        lows = []
        for bit in range(2):
            span = slice(bit * feats, (bit + 1) * feats)
            weight = weight_rows(order, here, got, other, bit)
            product = dot(x, weight)
            lifted[rows, span] = product
            lows.append((product * gain[:, span]).astype(BF))
        for ref, side in ((send, 1 - core), (keep, core)):
            span = pl.ds(pl.multiple_of(side * cols, cols), cols)
            part = dot(lows[0], kva[:, span]) + dot(lows[1], kvb[side ^ group])
            ref[rows] = part.astype(BF)


def lift(table, order, at, ta, tb, here, got, other, gain, kva, kvb):
    rows, half = ta.shape
    feats, cols = kva.shape[0], kva.shape[1] // 2
    whole = pl.BlockSpec(memory_space=pltpu.VMEM)
    return pl.pallas_call(
        functools.partial(lift_kernel, table, order),
        in_specs=[pl.BlockSpec(memory_space=pltpu.SMEM)] + [whole] * 8,
        out_specs=[whole] * 3,
        out_shape=[
            jax.ShapeDtypeStruct((rows, 2 * feats), F32),
            jax.ShapeDtypeStruct((rows, cols), BF),
            jax.ShapeDtypeStruct((rows, cols), BF),
        ],
        scratch_shapes=[pltpu.VMEM((rows, 2 * half), BF)],
        compiler_params=pltpu.CompilerParams(vmem_limit_bytes=VMEM_LIMIT),
        name="lift",
    )(at, ta, tb, here, got, other, gain, kva, kvb)


def two_parts(column):
    high = column.astype(BF)
    return high, (column - high.astype(F32)).astype(BF)


def finish_kernel(mine, got, squares, d_kv, kv, load):
    rows, cols = kv.shape
    total = mine[...].astype(F32) + got[...].astype(F32)
    mean = jnp.broadcast_to(squares[...], (rows, rows)).T[:, :1] * (1.0 / LLM_D)
    inv = lax.rsqrt(mean + 1e-05)
    low = (total * inv).astype(BF)
    kv[...] = low
    cot = (low.astype(F32) + d_kv[...].astype(F32)).astype(BF)
    load[:, :cols] = cot
    inner = jnp.sum(cot.astype(F32) * total, axis=1, keepdims=True)
    lane = lax.broadcasted_iota(jnp.int32, (rows, load.shape[1] - cols), 1)
    extra = jnp.zeros(lane.shape, F32)
    for i, part in enumerate(two_parts(inv) + two_parts(inner)):
        extra = jnp.where(lane == i, part.astype(F32), extra)
    load[:, cols:] = extra.astype(BF)


def finish(mine, got, squares, d_kv):
    rows, cols = mine.shape
    return pl.pallas_call(
        finish_kernel,
        out_shape=[
            jax.ShapeDtypeStruct((rows, cols), BF),
            jax.ShapeDtypeStruct((rows, cols + LANES), BF),
        ],
        compiler_params=pltpu.CompilerParams(vmem_limit_bytes=VMEM_LIMIT),
        name="finish",
    )(mine, got, squares, d_kv)


def lower_kernel(table, order, at, ca, cb, here, got, other, gain, kva, kvb, lifted, send, keep, nat):
    core, group = at[3], at[4]
    half = send.shape[1]
    feats = kva.shape[0]
    cols = kva.shape[1] // 2
    block = here.shape[2]
    starts = column_starts(order, at, block)
    near = pl.ds(pl.multiple_of(core * half, half), half)
    far = pl.ds(pl.multiple_of((1 - core) * half, half), half)
    piece = ca.shape[0] // len(table) if table else 0
    for rows in chunks_of(ca.shape[0]):
        extra = ca[rows, cols:].astype(F32)
        extra_b = cb[rows, cols:].astype(F32)
        inv = extra[:, 0:1] + extra[:, 1:2]
        inner = extra[:, 2:3] + extra[:, 3:4] + extra_b[:, 2:3] + extra_b[:, 3:4]
        pull = inv * inv * inv * inner * (1.0 / LLM_D)
        cots = ((ca[rows, :cols], core), (cb[rows, :cols], 1 - core))
        d_tok = None
        for bit in range(2):
            d_normed = None
            for cot, side in cots:
                span = pl.ds(pl.multiple_of(side * cols, cols), cols)
                part = dot_nt(cot, kvb[side ^ group] if bit else kva[:, span])
                d_normed = part if d_normed is None else d_normed + part
            span = slice(bit * feats, (bit + 1) * feats)
            low = (inv * gain[:, span] * d_normed - lifted[rows, span] * pull).astype(BF)
            weight = weight_rows(order, here, got, other, bit)
            part = dot_nt(low, weight)
            d_tok = part if d_tok is None else d_tok + part
        if not starts:
            nat[rows] = d_tok.astype(BF)
        for i, start in enumerate(starts or ()):
            nat[rows, pl.ds(start, block)] = d_tok[:, i * block : (i + 1) * block].astype(BF)
    for source_row, owner_row in table:
        send[source_row : source_row + piece] = nat[owner_row : owner_row + piece, far]
        keep[source_row : source_row + piece] = nat[owner_row : owner_row + piece, near]
    if not table:
        send[...] = nat[:, far]
        keep[...] = nat[:, near]


def lower(table, order, at, ca, cb, here, got, other, gain, kva, kvb, lifted):
    rows = ca.shape[0]
    width = 2 * here.shape[0] * here.shape[2]
    whole = pl.BlockSpec(memory_space=pltpu.VMEM)
    out = jax.ShapeDtypeStruct((rows, width // 2), BF)
    return pl.pallas_call(
        functools.partial(lower_kernel, table, order),
        in_specs=[pl.BlockSpec(memory_space=pltpu.SMEM)] + [whole] * 9,
        out_specs=[whole] * 2,
        out_shape=[out] * 2,
        scratch_shapes=[pltpu.VMEM((rows, width), BF)],
        compiler_params=pltpu.CompilerParams(vmem_limit_bytes=VMEM_LIMIT),
        name="lower",
    )(at, ca, cb, here, got, other, gain, kva, kvb, lifted)


def on_device(frames, weight_qkv, weight_out, proj_in, norm_gain, proj_kv, shifts, route, d_kv):
    n = lax.axis_size("tm")
    me = lax.axis_index("tm")
    core = lax.axis_index("mp")
    rows, width = frames.shape
    half_w = width // 2
    shift = shifts[0]
    own_tok = rows // POOL
    tail_tok = WINDOW // POOL
    ext_tok = own_tok + tail_tok
    feats = proj_kv.shape[0]
    kv_half = proj_kv.shape[1] // 2
    piece = own_tok // n

    part = lax.dynamic_slice_in_dim(frames, core * (WINDOW // 2), WINDOW // 2, 0)
    mine = to_tm(part, -1, False)
    w_t = jnp.transpose(weight_qkv, (1, 2, 0)).reshape(-1, width)
    group = lax.axis_index("groups")
    two_groups = lax.axis_size("groups") == 2
    if not two_groups:
        group = group * 0
    proj_kv, part = lax.optimization_barrier((proj_kv, part))
    kv_cut = lax.dynamic_slice_in_dim(proj_kv, group * kv_half, kv_half, 1)
    kv_near = [swap_tm(part, SPLIT) for part in jnp.split(kv_cut, 2)]
    proj_in, w_t = lax.optimization_barrier((proj_in, w_t))

    masks = group_bits()
    order = offsets(masks)
    members = order + [k | SPLIT for k in order]
    count = n // 2
    blocks = []
    for k in order:
        pair = [
            lax.dynamic_slice_in_dim(proj_in, (me ^ k ^ bit) * feats, feats, 1)
            for bit in (0, SPLIT)
        ]
        pair = jnp.stack(pair)
        blocks.append(swap_tm(pair, k) if k else pair)

    other = swap_mp(mine)
    halo = jnp.where(
        core == 0, jnp.concatenate([mine, other], 0), jnp.concatenate([other, mine], 0)
    )
    x_roll = lax.dynamic_slice_in_dim(jnp.concatenate([frames, halo], 0), shift, rows, 0)

    swap_groups = lambda block: lax.ppermute(block, "groups", [(0, 1), (1, 0)])
    x_roll, kv_near[0] = lax.optimization_barrier((x_roll, kv_near[0]))
    kv_far = [swap_groups(kv_near[0])] if two_groups else []
    at = jnp.stack([shift, rows * n - shift - me * rows, me, core, group]).astype(jnp.int32)
    normed, qkv, probs, pooled_attn, out_part = encoder_forward(
        x_roll, w_t, weight_out, at, ext_tok
    )
    out_part, kv_near, blocks, kv_far = lax.optimization_barrier(
        (out_part, kv_near, blocks, kv_far)
    )
    if two_groups:
        kv_far.append(swap_groups(kv_near[1]))
    else:
        kv_far.append(swap_tm(proj_kv[:, kv_half:], SPLIT))
    here = jnp.stack(blocks)
    in_near = swap_tm(
        lax.dynamic_slice_in_dim(here, group * (count // 2), count // 2, 0), SPLIT
    )
    turned = normed.T
    route, norm_gain, d_kv, pooled_attn = lax.optimization_barrier(
        (route, norm_gain, d_kv, pooled_attn)
    )
    gain = jnp.concatenate(
        [
            lax.dynamic_slice_in_dim(norm_gain, (me ^ bit) * feats, feats, 0)
            for bit in (0, SPLIT)
        ]
    ).reshape(1, -1)
    owner_at = (lax.dynamic_index_in_dim(route, me, 0, keepdims=False) ^ me)[None, :]
    sort = owner_at == jnp.array(members, jnp.int32)[:, None]
    sort = jnp.kron(sort.astype(BF), jnp.eye(piece, dtype=BF))
    source_at = jnp.arange(n, dtype=jnp.int32) ^ me
    spread = source_at[:, None] == jnp.array(
        [k | bit for k in order for bit in (0, SPLIT)], jnp.int32
    )
    spread = jnp.kron(spread.astype(BF), jnp.eye(piece, dtype=BF))
    d_kv = dot_tn(spread, d_kv).astype(BF)

    out_low = out_part.astype(BF)
    low_own = lax.dynamic_slice_in_dim(out_low, core * half_w, half_w, 1)
    low_other = lax.dynamic_slice_in_dim(out_low, (1 - core) * half_w, half_w, 1)
    from_core = swap_mp(low_other[:own_tok])
    tail_a = to_tm(low_own[own_tok:], 1, False)
    tail_b = to_tm(low_other[own_tok:], 1, True)
    own_pool = (
        jnp.arange(rows, dtype=jnp.int32)[None, :] // POOL
        == jnp.arange(own_tok, dtype=jnp.int32)[:, None]
    ).astype(BF) * (1.0 / POOL)
    x_mean = dot(own_pool, lax.dynamic_slice_in_dim(frames, core * half_w, half_w, 1))
    pooled = (
        x_mean
        + lax.dynamic_slice_in_dim(out_part, core * half_w, half_w, 1)[:own_tok]
        + from_core.astype(F32)
    )
    tail = tail_a.astype(F32) + tail_b.astype(F32)
    pooled = jnp.concatenate([pooled[:tail_tok] + tail, pooled[tail_tok:]], 0).astype(BF)

    sorted_tok = dot(sort, pooled).astype(BF).reshape(2, count * piece, half_w)
    pair_tok = jnp.stack([sorted_tok[0], swap_tm(sorted_tok[1], SPLIT)])
    pair_tok, in_near, kv_far = lax.optimization_barrier((pair_tok, in_near, kv_far))
    tok_half = gather_doubling(pair_tok, masks).reshape(-1, half_w)
    in_far = swap_groups(in_near) if two_groups else swap_tm(here[count // 2 :], SPLIT)
    kva = proj_kv
    kvb = jnp.stack([jnp.concatenate(kv_near), jnp.concatenate(kv_far)])
    at_rows = order
    if width // n % LANES:
        stacked = jnp.concatenate([here, in_near[:, ::-1], in_far[:, ::-1]])
        source = jnp.arange(n, dtype=jnp.int32) ^ me
        found = source[:, None] == jnp.array(members, jnp.int32)[None, :]
        place = jnp.sum(found * jnp.arange(n, dtype=jnp.int32)[None, :], axis=1)
        stacked = jnp.take(stacked, place, axis=0)
        here, in_near, in_far = jnp.split(stacked, [count, count + count // 2])
        at_rows = None
    tok_other = swap_mp(tok_half)
    table = list(moves(order, piece))
    source_rows = np.concatenate([np.arange(r, r + piece) for r, _ in table])
    owner_rows = np.concatenate([np.arange(r, r + piece) for _, r in table])
    by_xla = piece % 16 != 0
    if by_xla:
        at_owner = source_rows[np.argsort(owner_rows)]
        tok_half, tok_other = tok_half[at_owner], tok_other[at_owner]
        table = []
    lifted, kv_send, kv_keep = lift(
        table, at_rows, at, tok_half, tok_other, here, in_near, in_far, gain, kva, kvb
    )
    squares = jnp.sum(lifted * lifted, axis=-1).reshape(count, own_tok)
    square_sum = scatter_halving(squares + swap_mp(squares), masks, F32)
    kv_part = kv_keep.astype(F32) + swap_mp(kv_send).astype(F32)
    kv_part, turned = lax.optimization_barrier((kv_part, turned))
    kv_mine, kv_got = scatter_last(kv_part.reshape(count, own_tok, kv_half), masks)
    kv_low, load = finish(kv_mine, kv_got, square_sum.reshape(1, own_tok), d_kv)
    kv = dot(spread, kv_low).astype(BF)
    cot_half = gather_doubling(load, masks).reshape(count * own_tok, -1)
    cot_other = swap_mp(cot_half)
    d_send, d_keep = lower(
        table, at_rows, at, cot_half, cot_other, here, in_near, in_far, gain, kva, kvb, lifted
    )
    if by_xla:
        at_source = owner_rows[np.argsort(source_rows)]
        d_send, d_keep = d_send[at_source], d_keep[at_source]
    d_part = d_keep.astype(F32) + swap_mp(d_send).astype(F32)
    d_pair = scatter_halving(d_part.reshape(count, 2, count * piece, half_w), masks, BF)
    d_sorted = jnp.concatenate([d_pair[0].astype(BF), swap_tm(d_pair[1].astype(BF), SPLIT)], 0)
    d_half = dot_tn(sort, d_sorted).astype(BF)

    d_other = swap_mp(d_half)
    next_a = to_tm(d_half[:tail_tok], -1, False)
    next_b = to_tm(d_half[:tail_tok], -1, True)
    left = jnp.concatenate([d_half, next_a], 0)
    right = jnp.concatenate([d_other, next_b], 0)
    d_ext = jnp.where(
        core == 0, jnp.concatenate([left, right], 1), jnp.concatenate([right, left], 1)
    )
    bits = tm_bits()
    crossed = [bits[1], bits[0]] + bits[2:]
    d_attn, out_even, out_odd = out_grad(d_ext, weight_out, pooled_attn, at, bits)
    chunks = []
    for pair, path in enumerate((bits, crossed, bits, bits)):
        even, odd = encoder_backward(turned, qkv, probs, d_attn, at, path, pair, 1)
        even, odd, at = lax.optimization_barrier((even, odd, at))
        chunks.append((even, odd, path))
    chunks.insert(2, (out_even, out_odd, bits))
    chunks = scatter_chunks(chunks)
    grad_out = chunks.pop(2)
    grad_qkv = jnp.transpose(jnp.concatenate(chunks, axis=-1), (1, 0, 2))
    return kv, grad_qkv, grad_out


def solution(mesh):
    in_specs = (
        P(("groups", "tm"), None),
        P(None, None, "mp"),
        P("mp", None),
        P("tm", "mp"),
        P("mp"),
        P(("mp", "tm"), None),
        P(),
        P(),
        P(("groups", "tm"), "mp"),
    )
    out_specs = (
        P(("groups", "tm"), "mp"),
        P(("groups", "tm"), None, "mp"),
        P(("groups", "mp", "tm"), None),
    )
    return jax.shard_map(
        on_device, mesh=mesh, in_specs=in_specs, out_specs=out_specs, check_vma=False
    )
```

```python
import functools

import jax
import jax.numpy as jnp
import numpy as np
from jax import lax
from jax.experimental import pallas as pl
from jax.experimental.pallas import tpu as pltpu
from jax.sharding import PartitionSpec as P

HEAD = 64
WINDOW = 256
POOL = 4
LLM_D = 8192
BF = jnp.bfloat16
F32 = jnp.float32
VMEM_LIMIT = 48 << 20
SPLIT = 1
CHUNK = 512
LANES = 128


def dot(a, b):
    return jnp.dot(a, b, preferred_element_type=F32)


def dot_nt(a, b):
    return lax.dot_general(a, b, (((1,), (1,)), ((), ())), preferred_element_type=F32)


def dot_tn(a, b):
    return lax.dot_general(a, b, (((0,), (0,)), ((), ())), preferred_element_type=F32)


def swap_tm(block, mask):
    n = lax.axis_size("tm")
    return lax.ppermute(block, "tm", [(i, i ^ mask) for i in range(n)])


def swap_mp(block):
    n = lax.axis_size("mp")
    return lax.ppermute(block, "mp", [(i, n - 1 - i) for i in range(n)])


def to_tm(block, step, cross):
    n, m = lax.axis_size("tm"), lax.axis_size("mp")
    pairs = []
    for i in range(n):
        for c in range(m):
            pairs.append((i * m + c, (i + step) % n * m + (m - 1 - c if cross else c)))
    return lax.ppermute(block, ("tm", "mp"), pairs)


def offsets(masks):
    order = [0]
    for mask in reversed(masks):
        order = order + [k | mask for k in order]
    return order


def tm_bits():
    n = lax.axis_size("tm")
    return [1 << i for i in range(n.bit_length() - 1)]


def group_bits():
    return [bit for bit in tm_bits() if bit != SPLIT]


def gather_doubling(block, masks):
    block = block[None]
    for mask in reversed(masks):
        block = jnp.concatenate([block, swap_tm(block, mask)], axis=0)
    return block


def scatter_halving(blocks, masks, kind):
    total = blocks
    for mask in masks:
        low = total.astype(kind)
        half = low.shape[0] // 2
        total = low[:half].astype(F32) + swap_tm(low[half:], mask).astype(F32)
    return total[0]


def in_turn(got, last):
    return got if last is None else lax.optimization_barrier((got, last))[0]


def scatter_last(parts, masks):
    lows, pairs, last = list(parts), [], None
    for mask in masks:
        for i, low in enumerate(lows):
            half = low.shape[0] // 2
            got = in_turn(swap_tm(low[half:], mask), last)
            if mask == masks[-1]:
                pairs.append((low[0], got[0]))
                last = got
                continue
            lows[i] = last = (low[:half].astype(F32) + got.astype(F32)).astype(BF)
    return pairs


def gather_parts(parts, masks):
    parts, last = [part[None] for part in parts], None
    for mask in reversed(masks):
        for i, part in enumerate(parts):
            got = in_turn(swap_tm(part, mask), last)
            parts[i] = last = jnp.concatenate([part, got], axis=0)
    return parts


def scatter_chunks(chunks, steps):
    sums = [lower for lower, _, _ in chunks]
    sends = [upper for _, upper, _ in chunks]
    stage, last = [0] * len(chunks), None
    for i in steps:
        got = in_turn(swap_tm(sends[i], chunks[i][2][stage[i]]), last)
        stage[i] += 1
        total = sums[i].astype(F32) + got.astype(F32)
        if total.shape[0] == 1:
            sums[i] = total[0]
            continue
        low = last = total.astype(BF)
        half = low.shape[0] // 2
        sums[i], sends[i] = low[:half], low[half:]
    return sums


def head_mask(shape, head):
    return lax.broadcasted_iota(jnp.int32, shape, 1) // HEAD == head


def forward_kernel(at, x_ref, wq_ref, wk_ref, wv_ref, wo_ref, *refs):
    normed, qkv, probs, pooled, own_near, own_far, tail_near, tail_far, attn, out = refs
    shift, border, core = at[0], at[1], at[3]
    rows = x_ref.shape[0]
    cols = wq_ref.shape[0]

    @pl.when(pl.program_id(0) == 0)
    def _():
        x = x_ref[...].astype(F32)
        scale = lax.rsqrt(jnp.mean(x * x, axis=-1, keepdims=True) + 1e-05)
        normed[...] = (x * scale).astype(BF)
        out[...] = jnp.zeros_like(out)

    base = normed[...]
    for i, w_ref in enumerate((wq_ref, wk_ref, wv_ref)):
        qkv[i] = dot_nt(base, w_ref[...]).astype(BF)
    windows, heads = range(rows // WINDOW), range(cols // HEAD)
    spans = [pl.ds(w * WINDOW, WINDOW) for w in windows]
    own = [head_mask((WINDOW, cols), h) for h in heads]
    scores = []
    for w in windows:
        q, k = qkv[0, spans[w], :], qkv[1, spans[w], :]
        for h in heads:
            scores.append(dot_nt(jnp.where(own[h], k, jnp.zeros_like(k)), q))
    square = (WINDOW, WINDOW)
    key_at = lax.broadcasted_iota(jnp.int32, square, 0)
    query_at = lax.broadcasted_iota(jnp.int32, square, 1)
    lows = []
    for w in windows:
        edge = border - w * WINDOW
        allowed = (key_at >= edge) == (query_at >= edge)
        for h in heads:
            score = jnp.where(allowed, scores[w * len(heads) + h] * HEAD ** (-0.5), -1e30)
            terms = jnp.exp(score - jnp.max(score, axis=0, keepdims=True))
            low = (terms * (1.0 / jnp.sum(terms, axis=0, keepdims=True))).astype(BF)
            probs[0, w, h] = low
            lows.append(low)
    for w in windows:
        v = qkv[2, spans[w], :]
        attended = None
        for h in heads:
            part = dot_tn(lows[w * len(heads) + h], v)
            attended = part if attended is None else jnp.where(own[h], part, attended)
        attn[spans[w], :] = attended.astype(BF)
    tok_shape = (pooled.shape[0], rows)
    tok_of = (lax.broadcasted_iota(jnp.int32, tok_shape, 1) + shift) // POOL
    member = tok_of == lax.broadcasted_iota(jnp.int32, tok_shape, 0)
    pool = jnp.where(member, 1.0 / POOL, 0.0).astype(BF)
    low = dot(pool, attn[...]).astype(BF)
    pooled[...] = low
    out[...] += dot(low, wo_ref[...])

    @pl.when(pl.program_id(0) == pl.num_programs(0) - 1)
    def _():
        count, half = own_near.shape
        near = pl.ds(pl.multiple_of(core * half, half), half)
        far = pl.ds(pl.multiple_of((1 - core) * half, half), half)
        own_near[...] = out[:count, near]
        own_far[...] = out[:count, far].astype(BF)
        tail_near[...] = out[count:, near].astype(BF)
        tail_far[...] = out[count:, far].astype(BF)


def encoder_forward(x_roll, w_t, weight_out, at, ext_tok):
    rows, width = x_roll.shape
    heads_w = weight_out.shape[0]
    cols = 2 * HEAD
    pairs = heads_w // cols
    windows = rows // WINDOW
    weight = lambda i: pl.BlockSpec((cols, width), lambda p, at: (i * pairs + p, 0))
    own_tok = rows // POOL
    piece = lambda count: pl.BlockSpec((count, width // 2), lambda p, at: (0, 0))
    return pl.pallas_call(
        forward_kernel,
        grid_spec=pltpu.PrefetchScalarGridSpec(
            num_scalar_prefetch=1,
            grid=(pairs,),
            in_specs=[
                pl.BlockSpec((rows, width), lambda p, at: (0, 0)),
                weight(0),
                weight(1),
                weight(2),
                weight(0),
            ],
            out_specs=[
                pl.BlockSpec((rows, width), lambda p, at: (0, 0)),
                pl.BlockSpec((3, rows, cols), lambda p, at: (0, 0, p)),
                pl.BlockSpec((1, windows, 2, WINDOW, WINDOW), lambda p, at: (p, 0, 0, 0, 0)),
                pl.BlockSpec((ext_tok, cols), lambda p, at: (0, p)),
                piece(own_tok),
                piece(own_tok),
                piece(ext_tok - own_tok),
                piece(ext_tok - own_tok),
            ],
            scratch_shapes=[pltpu.VMEM((rows, cols), BF), pltpu.VMEM((ext_tok, width), F32)],
        ),
        out_shape=[
            pltpu.HBM((rows, width), BF),
            pltpu.HBM((3, rows, heads_w), BF),
            pltpu.HBM((pairs, windows, 2, WINDOW, WINDOW), BF),
            pltpu.HBM((ext_tok, heads_w), BF),
            jax.ShapeDtypeStruct((own_tok, width // 2), F32),
            jax.ShapeDtypeStruct((own_tok, width // 2), BF),
            jax.ShapeDtypeStruct((ext_tok - own_tok, width // 2), BF),
            jax.ShapeDtypeStruct((ext_tok - own_tok, width // 2), BF),
        ],
        compiler_params=pltpu.CompilerParams(vmem_limit_bytes=VMEM_LIMIT),
        name="encoder_forward",
    )(at, x_roll, w_t, w_t, w_t, weight_out)


def out_grad_kernel(masks, at, d_ref, wo_ref, pa_ref, d_attn, even, odd, turned):
    me = at[2]
    block = even.shape[1]
    d_ext = d_ref[...]
    d_attn[...] = (dot_nt(d_ext, wo_ref[...]) * (1.0 / POOL)).astype(BF)
    turned[...] = pa_ref[...].T
    for bit, ref in ((0, even), (masks[0], odd)):
        for j, k in enumerate(offsets(masks[1:])):
            start = pl.multiple_of((me ^ (k | bit)) * block, block)
            ref[j] = dot(turned[pl.ds(start, block), :], d_ext).astype(BF)


def out_grad(d_ext, weight_out, pooled_attn, at, masks):
    heads_w, width = weight_out.shape
    n = 2 ** len(masks)
    blocks = jax.ShapeDtypeStruct((n // 2, heads_w // n, width), BF)
    whole = pl.BlockSpec(memory_space=pltpu.VMEM)
    return pl.pallas_call(
        functools.partial(out_grad_kernel, masks),
        in_specs=[pl.BlockSpec(memory_space=pltpu.SMEM), whole, whole, whole],
        out_specs=[whole] * 3,
        out_shape=[jax.ShapeDtypeStruct(pooled_attn.shape, BF), blocks, blocks],
        scratch_shapes=[pltpu.VMEM((heads_w, pooled_attn.shape[0]), BF)],
        compiler_params=pltpu.CompilerParams(vmem_limit_bytes=VMEM_LIMIT),
        name="out_grad",
    )(at, d_ext, weight_out, pooled_attn)


def backward_kernel(masks, at, turned, qkv, probs, d_ref, even, odd, grads):
    shift, me = at[0], at[2]
    rows = turned.shape[1]
    cols = d_ref.shape[1]
    block = even.shape[2]
    tok_shape = (rows, d_ref.shape[0])
    tok_of = (lax.broadcasted_iota(jnp.int32, tok_shape, 0) + shift) // POOL
    member = tok_of == lax.broadcasted_iota(jnp.int32, tok_shape, 1)
    d_rows = dot(jnp.where(member, 1.0, 0.0).astype(BF), d_ref[...]).astype(BF)
    for w in range(rows // WINDOW):
        span = pl.ds(w * WINDOW, WINDOW)
        q, k, v = qkv[0, span, :], qkv[1, span, :], qkv[2, span, :]
        d_out = d_rows[w * WINDOW : (w + 1) * WINDOW]
        none = jnp.zeros_like(q)
        sums = [0.0, 0.0, 0.0]
        for h in range(cols // HEAD):
            own = head_mask(q.shape, h)
            low = probs[0, w, h]
            weight = low.astype(F32)
            d_weight = dot_nt(jnp.where(own, v, none), d_out)
            centre = jnp.sum(weight * d_weight, axis=0, keepdims=True)
            d_score = (weight * (d_weight - centre) * HEAD ** (-0.5)).astype(BF)
            sums[0] += dot_tn(d_score, jnp.where(own, k, none))
            sums[1] += dot(d_score, jnp.where(own, q, none))
            sums[2] += dot(low, jnp.where(own, d_out, none))
        for i in range(3):
            grads[span, i * cols : (i + 1) * cols] = sums[i].astype(BF)
    d_all = grads[...]
    for bit, ref in ((0, even), (masks[0], odd)):
        for j, k in enumerate(offsets(masks[1:])):
            start = pl.multiple_of((me ^ (k | bit)) * block, block)
            term = dot(turned[pl.ds(start, block), :], d_all).astype(BF)
            for i in range(3):
                ref[j, i] = term[:, i * cols : (i + 1) * cols]


def encoder_backward(turned, qkv, probs, d_attn, at, masks, first, count):
    width, rows = turned.shape
    n = 2 ** len(masks)
    cols = 2 * HEAD
    windows = rows // WINDOW
    block = width // n
    out = pl.BlockSpec((n // 2, 3, block, cols), lambda p, at: (0, 0, 0, p))
    shape = jax.ShapeDtypeStruct((n // 2, 3, block, cols * count), BF)
    return pl.pallas_call(
        functools.partial(backward_kernel, masks),
        grid_spec=pltpu.PrefetchScalarGridSpec(
            num_scalar_prefetch=1,
            grid=(count,),
            in_specs=[
                pl.BlockSpec((width, rows), lambda p, at: (0, 0)),
                pl.BlockSpec((3, rows, cols), lambda p, at: (0, 0, p + first)),
                pl.BlockSpec(
                    (1, windows, 2, WINDOW, WINDOW), lambda p, at: (p + first, 0, 0, 0, 0)
                ),
                pl.BlockSpec((d_attn.shape[0], cols), lambda p, at: (0, p + first)),
            ],
            out_specs=[out, out],
            scratch_shapes=[pltpu.VMEM((rows, 3 * cols), BF)],
        ),
        out_shape=[shape, shape],
        compiler_params=pltpu.CompilerParams(vmem_limit_bytes=VMEM_LIMIT),
        name="encoder_backward",
    )(at, turned, qkv, probs, d_attn)


def moves(order, piece):
    count = len(order)
    for e, offset in enumerate(order):
        for b in range(2):
            for i, step in enumerate(order):
                owner = order.index(offset ^ step)
                source_row = ((e * 2 + b) * count + i) * piece
                owner_row = ((owner * count + i) * 2 + b) * piece
                yield source_row, owner_row


def chunks_of(rows):
    return [slice(r, min(r + CHUNK, rows)) for r in range(0, rows, CHUNK)]


def column_starts(order, at, block):
    if order is None:
        return None
    offset = [k | bit for bit in (0, SPLIT) for k in order]
    return [pl.multiple_of((at[2] ^ k) * block, block) for k in offset]


def weight_rows(here, there):
    return jnp.concatenate([w[...].reshape(-1, w.shape[-1]) for w in (here, there)], axis=0)


def both(index, size):
    return (
        pl.ds(pl.multiple_of(index * size, size), size),
        pl.ds(pl.multiple_of((1 - index) * size, size), size),
    )


def lift_kernel(table, order, at, ta, tb, here, there, gain, kva, kvb, *refs):
    lifted, send, keep, tok, low = refs
    core, group = at[3], at[4]
    feats, cols = kva.shape[0], send.shape[1]
    near, far = both(core, ta.shape[1])
    mine, across = both(at[2] % 2, feats)
    piece = ta.shape[0] // len(table) if table else 0
    for source_row, owner_row in table:
        tok[owner_row : owner_row + piece, near] = ta[source_row : source_row + piece]
        tok[owner_row : owner_row + piece, far] = tb[source_row : source_row + piece]
    if not table:
        tok[:, near] = ta[...]
        tok[:, far] = tb[...]
    block = here.shape[1]
    starts = column_starts(order, at, block)
    weight = weight_rows(here, there)
    for rows in chunks_of(tok.shape[0]):
        x = tok[rows]
        if starts:
            x = jnp.concatenate([tok[rows, pl.ds(start, block)] for start in starts], axis=1)
        product = dot(x, weight)
        lifted[rows] = product
        low[rows] = (product * gain[...]).astype(BF)
        for ref, side in ((send, 1 - core), (keep, core)):
            span = pl.ds(pl.multiple_of(side * cols, cols), cols)
            part = dot(low[rows, mine], kva[:, span]) + dot(low[rows, across], kvb[side ^ group])
            ref[rows] = part.astype(BF)


def lift(table, order, at, ta, tb, here, there, gain, kva, kvb):
    rows, half = ta.shape
    feats, cols = kva.shape[0], kva.shape[1] // 2
    whole = pl.BlockSpec(memory_space=pltpu.VMEM)
    return pl.pallas_call(
        functools.partial(lift_kernel, table, order),
        in_specs=[pl.BlockSpec(memory_space=pltpu.SMEM)] + [whole] * 7,
        out_specs=[whole] * 3,
        out_shape=[
            jax.ShapeDtypeStruct((rows, 2 * feats), F32),
            jax.ShapeDtypeStruct((rows, cols), BF),
            jax.ShapeDtypeStruct((rows, cols), BF),
        ],
        scratch_shapes=[pltpu.VMEM((rows, 2 * half), BF), pltpu.VMEM((rows, 2 * feats), BF)],
        compiler_params=pltpu.CompilerParams(vmem_limit_bytes=VMEM_LIMIT),
        name="lift",
    )(at, ta, tb, here, there, gain, kva, kvb)


def two_parts(column):
    high = column.astype(BF)
    return high, (column - high.astype(F32)).astype(BF)


def finish_kernel(mine, got, squares, d_kv, *refs):
    rows, cols = mine.shape
    kv, load, inner = refs[-3:]
    total = mine[...].astype(F32) + got[...].astype(F32)
    mean = jnp.broadcast_to(squares[...], (rows, rows)).T[:, :1] * (1.0 / LLM_D)
    inv = lax.rsqrt(mean + 1e-05)
    low = (total * inv).astype(BF)
    kv[...] = low
    cot = (low.astype(F32) + d_kv[...].astype(F32)).astype(BF)
    load[:, :cols] = cot
    pull = jnp.sum(cot.astype(F32) * total, axis=1, keepdims=True)
    if len(refs) == 4:
        pull += refs[0][...]
        lane = lax.broadcasted_iota(jnp.int32, (rows, load.shape[1] - cols), 1)
        extra = jnp.zeros(lane.shape, F32)
        for i, part in enumerate(two_parts(inv) + two_parts(pull)):
            extra = jnp.where(lane == i, part.astype(F32), extra)
        load[:, cols:] = extra.astype(BF)
    inner[...] = pull


def finish(mine, got, squares, d_kv, *inner):
    rows, cols = mine.shape
    return pl.pallas_call(
        finish_kernel,
        out_shape=[
            jax.ShapeDtypeStruct((rows, cols), BF),
            jax.ShapeDtypeStruct((rows, cols + LANES * len(inner)), BF),
            jax.ShapeDtypeStruct((rows, 1), F32),
        ],
        compiler_params=pltpu.CompilerParams(vmem_limit_bytes=VMEM_LIMIT),
        name="finish",
    )(mine, got, squares, d_kv, *inner)


def lower_kernel(table, order, at, ca0, ca1, cb0, cb1, here, there, gain, kva, kvb, *refs):
    lifted, send, keep, nat, low = refs
    core, group = at[3], at[4]
    feats, half = kva.shape[0], send.shape[1]
    cols = kva.shape[1] // 2
    near, far = both(core, half)
    mine, across = both(at[2] % 2, feats)
    block = here.shape[1]
    starts = column_starts(order, at, block)
    weight = weight_rows(here, there)
    part_cols = ca0.shape[1]
    piece = ca0.shape[0] // len(table) if table else 0
    for rows in chunks_of(ca0.shape[0]):
        extra = ca1[rows, part_cols:].astype(F32)
        extra_b = cb1[rows, part_cols:].astype(F32)
        inv = extra[:, 0:1] + extra[:, 1:2]
        inner = extra[:, 2:3] + extra[:, 3:4] + extra_b[:, 2:3] + extra_b[:, 3:4]
        pull = inv * inv * inv * inner * (1.0 / LLM_D)
        cots = [
            (jnp.concatenate([c0[rows], c1[rows, :part_cols]], axis=1), side)
            for c0, c1, side in ((ca0, ca1, core), (cb0, cb1, 1 - core))
        ]
        for is_mine, span in ((True, mine), (False, across)):
            d_normed = None
            for cot, side in cots:
                at_side = pl.ds(pl.multiple_of(side * cols, cols), cols)
                part = dot_nt(cot, kva[:, at_side] if is_mine else kvb[side ^ group])
                d_normed = part if d_normed is None else d_normed + part
            low[rows, span] = (
                inv * gain[:, span] * d_normed - lifted[rows, span] * pull
            ).astype(BF)
        d_tok = dot_nt(low[rows], weight).astype(BF)
        if not starts:
            nat[rows] = d_tok
        for i, start in enumerate(starts or ()):
            nat[rows, pl.ds(start, block)] = d_tok[:, i * block : (i + 1) * block]
    for source_row, owner_row in table:
        send[source_row : source_row + piece] = nat[owner_row : owner_row + piece, far]
        keep[source_row : source_row + piece] = nat[owner_row : owner_row + piece, near]
    if not table:
        send[...] = nat[:, far]
        keep[...] = nat[:, near]


def lower(table, order, at, cots, here, there, gain, kva, kvb, lifted):
    rows, width = cots[0].shape[0], lifted.shape[1]
    tok_width = 2 * here.shape[0] * here.shape[1]
    whole = pl.BlockSpec(memory_space=pltpu.VMEM)
    out = jax.ShapeDtypeStruct((rows, tok_width // 2), BF)
    return pl.pallas_call(
        functools.partial(lower_kernel, table, order),
        in_specs=[pl.BlockSpec(memory_space=pltpu.SMEM)] + [whole] * 10,
        out_specs=[whole] * 2,
        out_shape=[out] * 2,
        scratch_shapes=[pltpu.VMEM((rows, tok_width), BF), pltpu.VMEM((rows, width), BF)],
        compiler_params=pltpu.CompilerParams(vmem_limit_bytes=VMEM_LIMIT),
        name="lower",
    )(at, *cots, here, there, gain, kva, kvb, lifted)


def on_device(frames, weight_qkv, weight_out, proj_in, norm_gain, proj_kv, shifts, route, d_kv):
    n = lax.axis_size("tm")
    me = lax.axis_index("tm")
    core = lax.axis_index("mp")
    rows, width = frames.shape
    half_w = width // 2
    shift = shifts[0]
    own_tok = rows // POOL
    tail_tok = WINDOW // POOL
    ext_tok = own_tok + tail_tok
    feats = proj_kv.shape[0]
    kv_half = proj_kv.shape[1] // 2
    piece = own_tok // n

    part = lax.dynamic_slice_in_dim(frames, core * (WINDOW // 2), WINDOW // 2, 0)
    mine = to_tm(part, -1, False)
    w_t = jnp.transpose(weight_qkv, (1, 2, 0)).reshape(-1, width)
    group = lax.axis_index("groups")
    two_groups = lax.axis_size("groups") == 2
    if not two_groups:
        group = group * 0
    proj_kv, part = lax.optimization_barrier((proj_kv, part))
    kv_near = swap_tm(lax.dynamic_slice_in_dim(proj_kv, group * kv_half, kv_half, 1), SPLIT)
    proj_in, w_t = lax.optimization_barrier((proj_in, w_t))

    masks = group_bits()
    order = offsets(masks)
    members = order + [k | SPLIT for k in order]
    count = n // 2
    blocks = []
    for k in order:
        pair = lax.dynamic_slice_in_dim(proj_in, (me ^ k) // 2 * 2 * feats, 2 * feats, 1)
        blocks.append(swap_tm(pair, k) if k else pair)

    other = swap_mp(mine)
    halo = jnp.where(
        core == 0, jnp.concatenate([mine, other], 0), jnp.concatenate([other, mine], 0)
    )
    x_roll = lax.dynamic_slice_in_dim(jnp.concatenate([frames, halo], 0), shift, rows, 0)

    at = jnp.stack([shift, rows * n - shift - me * rows, me, core, group]).astype(jnp.int32)
    normed, qkv, probs, pooled_attn, own_near, own_far, tail_near, tail_far = encoder_forward(
        x_roll, w_t, weight_out, at, ext_tok
    )
    own_far, kv_near = lax.optimization_barrier((own_far, kv_near))
    swap_groups = lambda block: lax.ppermute(block, "groups", [(0, 1), (1, 0)])
    if two_groups:
        kv_far = swap_groups(kv_near)
    else:
        kv_far = swap_tm(proj_kv[:, kv_half:], SPLIT)
    turned = normed.T
    route, norm_gain, d_kv, pooled_attn = lax.optimization_barrier(
        (route, norm_gain, d_kv, pooled_attn)
    )
    gain = lax.dynamic_slice_in_dim(norm_gain, me // 2 * 2 * feats, 2 * feats, 0)
    gain = gain.reshape(1, -1)
    owner_at = (lax.dynamic_index_in_dim(route, me, 0, keepdims=False) ^ me)[None, :]
    sort = owner_at == jnp.array(members, jnp.int32)[:, None]
    sort = jnp.kron(sort.astype(BF), jnp.eye(piece, dtype=BF))
    source_at = jnp.arange(n, dtype=jnp.int32) ^ me
    spread = source_at[:, None] == jnp.array(
        [k | bit for k in order for bit in (0, SPLIT)], jnp.int32
    )
    spread = jnp.kron(spread.astype(BF), jnp.eye(piece, dtype=BF))
    d_kv = dot_tn(spread, d_kv).astype(BF)

    from_core = swap_mp(own_far)
    tail_a = to_tm(tail_near, 1, False)
    tail_b = to_tm(tail_far, 1, True)
    tail_a, tail_b, from_core, blocks = lax.optimization_barrier(
        (tail_a, tail_b, from_core, blocks)
    )
    own_pool = (
        jnp.arange(rows, dtype=jnp.int32)[None, :] // POOL
        == jnp.arange(own_tok, dtype=jnp.int32)[:, None]
    ).astype(BF) * (1.0 / POOL)
    x_mean = dot(own_pool, lax.dynamic_slice_in_dim(frames, core * half_w, half_w, 1))
    pooled = x_mean + own_near + from_core.astype(F32)
    tail = tail_a.astype(F32) + tail_b.astype(F32)
    pooled = jnp.concatenate([pooled[:tail_tok] + tail, pooled[tail_tok:]], 0).astype(BF)

    sorted_tok = dot(sort, pooled).astype(BF).reshape(2, count * piece, half_w)
    handed = swap_tm(sorted_tok[1], SPLIT)
    here = jnp.stack(blocks)
    handed, here = lax.optimization_barrier((handed, here))
    there = swap_tm(here, SPLIT)
    pair_tok = jnp.stack([sorted_tok[0], handed])
    tok_half = gather_doubling(pair_tok, masks[-1:])
    tok_half, kv_far = lax.optimization_barrier((tok_half, kv_far))
    kva, kvb = proj_kv, jnp.stack([kv_near, kv_far])
    at_rows = order
    if width // n % LANES:
        stacked = jnp.concatenate([here, there])
        source = jnp.arange(n, dtype=jnp.int32) ^ me
        found = source[:, None] == jnp.array(members, jnp.int32)[None, :]
        place = jnp.sum(found * jnp.arange(n, dtype=jnp.int32)[None, :], axis=1)
        stacked = jnp.take(stacked, place, axis=0)
        here, there = jnp.split(stacked, 2)
        at_rows = None
    for mask in reversed(masks[:-1]):
        tok_half = jnp.concatenate([tok_half, swap_tm(tok_half, mask)], axis=0)
    tok_half = tok_half.reshape(-1, half_w)
    tok_other = swap_mp(tok_half)
    table = list(moves(order, piece))
    source_rows = np.concatenate([np.arange(r, r + piece) for r, _ in table])
    owner_rows = np.concatenate([np.arange(r, r + piece) for _, r in table])
    by_xla = piece % 16 != 0
    if by_xla:
        at_owner = source_rows[np.argsort(owner_rows)]
        tok_half, tok_other = tok_half[at_owner], tok_other[at_owner]
        table = []
    lifted, kv_send, kv_keep = lift(
        table, at_rows, at, tok_half, tok_other, here, there, gain, kva, kvb
    )
    squares = jnp.sum(lifted * lifted, axis=-1).reshape(count, own_tok)
    square_sum = scatter_halving(squares + swap_mp(squares), masks, F32)
    kv_part = (kv_keep.astype(F32) + swap_mp(kv_send).astype(F32)).astype(BF)
    kv_part, turned = lax.optimization_barrier((kv_part, turned))
    kv_parts = jnp.split(kv_part.reshape(count, own_tok, kv_half), 2, axis=2)
    (mine_a, got_a), (mine_b, got_b) = scatter_last(kv_parts, masks)
    square_sum = square_sum.reshape(1, own_tok)
    d_kv_a, d_kv_b = jnp.split(d_kv, 2, axis=1)
    kv_a, load_a, inner = finish(mine_a, got_a, square_sum, d_kv_a)
    kv_b, load_b, _ = finish(mine_b, got_b, square_sum, d_kv_b, inner)
    kv = dot(spread, jnp.concatenate([kv_a, kv_b], axis=1)).astype(BF)
    loads = gather_parts([load_a, load_b], masks)
    loads = [load.reshape(count * own_tok, -1) for load in loads]
    cots = loads + [swap_mp(load) for load in loads]
    d_send, d_keep = lower(
        table, at_rows, at, cots, here, there, gain, kva, kvb, lifted
    )
    if by_xla:
        at_source = owner_rows[np.argsort(source_rows)]
        d_send, d_keep = d_send[at_source], d_keep[at_source]
    d_part = d_keep.astype(F32) + swap_mp(d_send).astype(F32)
    d_pair = scatter_halving(d_part.reshape(count, 2, count * piece, half_w), masks, BF)
    d_sorted = jnp.concatenate([d_pair[0].astype(BF), swap_tm(d_pair[1].astype(BF), SPLIT)], 0)
    d_half = dot_tn(sort, d_sorted).astype(BF)

    d_other = swap_mp(d_half)
    next_a = to_tm(d_half[:tail_tok], -1, False)
    next_b = to_tm(d_half[:tail_tok], -1, True)
    left = jnp.concatenate([d_half, next_a], 0)
    right = jnp.concatenate([d_other, next_b], 0)
    d_ext = jnp.where(
        core == 0, jnp.concatenate([left, right], 1), jnp.concatenate([right, left], 1)
    )
    bits = tm_bits()
    crossed = [bits[1], bits[0]] + bits[2:]
    d_attn, out_even, out_odd = out_grad(d_ext, weight_out, pooled_attn, at, bits)
    chunks = []
    for pair, path in enumerate((bits, bits, bits, crossed)):
        even, odd = encoder_backward(turned, qkv, probs, d_attn, at, path, pair, 1)
        even, odd, at = lax.optimization_barrier((even, odd, at))
        chunks.append((even, odd, path))
    chunks.append((out_even, out_odd, bits))
    steps = list(range(len(chunks))) * len(bits)
    if len(bits) == 3:
        steps = [0, 0, 1, 3, 0, 1, 4, 1, 4, 2, 3, 4, 2, 3, 2]
    chunks = scatter_chunks(chunks, steps)
    grad_out = chunks.pop()
    grad_qkv = jnp.transpose(jnp.concatenate(chunks, axis=-1), (1, 0, 2))
    return kv, grad_qkv, grad_out


def solution(mesh):
    in_specs = (
        P(("groups", "tm"), None),
        P(None, None, "mp"),
        P("mp", None),
        P("tm", "mp"),
        P("mp"),
        P(("mp", "tm"), None),
        P(),
        P(),
        P(("groups", "tm"), "mp"),
    )
    out_specs = (
        P(("groups", "tm"), "mp"),
        P(("groups", "tm"), None, "mp"),
        P(("groups", "mp", "tm"), None),
    )
    return jax.shard_map(
        on_device, mesh=mesh, in_specs=in_specs, out_specs=out_specs, check_vma=False
    )
```

```python
import functools

import jax
import jax.numpy as jnp
import numpy as np
from jax import lax
from jax.experimental import pallas as pl
from jax.experimental.pallas import tpu as pltpu
from jax.sharding import PartitionSpec as P

HEAD = 64
WINDOW = 256
POOL = 4
LLM_D = 8192
BF = jnp.bfloat16
F32 = jnp.float32
VMEM_LIMIT = 48 << 20
SPLIT = 1
CHUNK = 512
LANES = 128


def dot(a, b):
    return jnp.dot(a, b, preferred_element_type=F32)


def dot_nt(a, b):
    return lax.dot_general(a, b, (((1,), (1,)), ((), ())), preferred_element_type=F32)


def dot_tn(a, b):
    return lax.dot_general(a, b, (((0,), (0,)), ((), ())), preferred_element_type=F32)


def swap_tm(block, mask):
    n = lax.axis_size("tm")
    return lax.ppermute(block, "tm", [(i, i ^ mask) for i in range(n)])


def swap_mp(block):
    n = lax.axis_size("mp")
    return lax.ppermute(block, "mp", [(i, n - 1 - i) for i in range(n)])


def to_tm(block, step, cross):
    n, m = lax.axis_size("tm"), lax.axis_size("mp")
    pairs = []
    for i in range(n):
        for c in range(m):
            pairs.append((i * m + c, (i + step) % n * m + (m - 1 - c if cross else c)))
    return lax.ppermute(block, ("tm", "mp"), pairs)


def offsets(masks):
    order = [0]
    for mask in reversed(masks):
        order = order + [k | mask for k in order]
    return order


def tm_bits():
    n = lax.axis_size("tm")
    return [1 << i for i in range(n.bit_length() - 1)]


def group_bits():
    return [bit for bit in tm_bits() if bit != SPLIT]


def gather_doubling(block, masks):
    block = block[None]
    for mask in reversed(masks):
        block = jnp.concatenate([block, swap_tm(block, mask)], axis=0)
    return block


def scatter_halving(blocks, masks, kind):
    total = blocks
    for mask in masks:
        low = total.astype(kind)
        half = low.shape[0] // 2
        total = low[:half].astype(F32) + swap_tm(low[half:], mask).astype(F32)
    return total[0]


def in_turn(got, last):
    return got if last is None else lax.optimization_barrier((got, last))[0]


def scatter_last(parts, masks):
    lows, pairs, last = list(parts), [], None
    for mask in masks:
        for i, low in enumerate(lows):
            half = low.shape[0] // 2
            got = in_turn(swap_tm(low[half:], mask), last)
            if mask == masks[-1]:
                pairs.append((low[0], got[0]))
                last = got
                continue
            lows[i] = last = (low[:half].astype(F32) + got.astype(F32)).astype(BF)
    return pairs


def gather_parts(parts, masks):
    parts, last = [part[None] for part in parts], None
    for mask in reversed(masks):
        for i, part in enumerate(parts):
            got = in_turn(swap_tm(part, mask), last)
            parts[i] = last = jnp.concatenate([part, got], axis=0)
    return parts


def scatter_chunks(chunks, steps, last):
    sums = [lower for lower, _, _ in chunks]
    sends = [upper for _, upper, _ in chunks]
    stage = [0] * len(chunks)
    for i in steps:
        got = in_turn(swap_tm(sends[i], chunks[i][2][stage[i]]), last)
        stage[i] += 1
        total = sums[i].astype(F32) + got.astype(F32)
        if total.shape[0] == 1:
            sums[i] = total[0]
            continue
        low = last = total.astype(BF)
        half = low.shape[0] // 2
        sums[i], sends[i] = low[:half], low[half:]
    return sums


def head_mask(shape, head):
    return lax.broadcasted_iota(jnp.int32, shape, 1) // HEAD == head


def forward_kernel(at, x_ref, wq_ref, wk_ref, wv_ref, wo_ref, *refs):
    normed, qkv, probs, pooled, own_near, own_far, tail_near, tail_far, attn, out = refs
    shift, border, core = at[0], at[1], at[3]
    rows = x_ref.shape[0]
    cols = wq_ref.shape[0]

    @pl.when(pl.program_id(0) == 0)
    def _():
        x = x_ref[...].astype(F32)
        scale = lax.rsqrt(jnp.mean(x * x, axis=-1, keepdims=True) + 1e-05)
        normed[...] = (x * scale).astype(BF)
        out[...] = jnp.zeros_like(out)

    base = normed[...]
    for i, w_ref in enumerate((wq_ref, wk_ref, wv_ref)):
        qkv[i] = dot_nt(base, w_ref[...]).astype(BF)
    windows, heads = range(rows // WINDOW), range(cols // HEAD)
    spans = [pl.ds(w * WINDOW, WINDOW) for w in windows]
    own = [head_mask((WINDOW, cols), h) for h in heads]
    scores = []
    for w in windows:
        q, k = qkv[0, spans[w], :], qkv[1, spans[w], :]
        for h in heads:
            scores.append(dot_nt(jnp.where(own[h], k, jnp.zeros_like(k)), q))
    square = (WINDOW, WINDOW)
    key_at = lax.broadcasted_iota(jnp.int32, square, 0)
    query_at = lax.broadcasted_iota(jnp.int32, square, 1)
    lows = []
    for w in windows:
        edge = border - w * WINDOW
        allowed = (key_at >= edge) == (query_at >= edge)
        for h in heads:
            score = jnp.where(allowed, scores[w * len(heads) + h] * HEAD ** (-0.5), -1e30)
            terms = jnp.exp(score - jnp.max(score, axis=0, keepdims=True))
            low = (terms * (1.0 / jnp.sum(terms, axis=0, keepdims=True))).astype(BF)
            probs[0, w, h] = low
            lows.append(low)
    for w in windows:
        v = qkv[2, spans[w], :]
        attended = None
        for h in heads:
            part = dot_tn(lows[w * len(heads) + h], v)
            attended = part if attended is None else jnp.where(own[h], part, attended)
        attn[spans[w], :] = attended.astype(BF)
    tok_shape = (pooled.shape[0], rows)
    tok_of = (lax.broadcasted_iota(jnp.int32, tok_shape, 1) + shift) // POOL
    member = tok_of == lax.broadcasted_iota(jnp.int32, tok_shape, 0)
    pool = jnp.where(member, 1.0 / POOL, 0.0).astype(BF)
    low = dot(pool, attn[...]).astype(BF)
    pooled[...] = low
    out[...] += dot(low, wo_ref[...])

    @pl.when(pl.program_id(0) == pl.num_programs(0) - 1)
    def _():
        count, half = own_near.shape
        near = pl.ds(pl.multiple_of(core * half, half), half)
        far = pl.ds(pl.multiple_of((1 - core) * half, half), half)
        own_near[...] = out[:count, near]
        own_far[...] = out[:count, far].astype(BF)
        tail_near[...] = out[count:, near].astype(BF)
        tail_far[...] = out[count:, far].astype(BF)


def encoder_forward(x_roll, w_t, weight_out, at, ext_tok):
    rows, width = x_roll.shape
    heads_w = weight_out.shape[0]
    cols = 2 * HEAD
    pairs = heads_w // cols
    windows = rows // WINDOW
    weight = lambda i: pl.BlockSpec((cols, width), lambda p, at: (i * pairs + p, 0))
    own_tok = rows // POOL
    piece = lambda count: pl.BlockSpec((count, width // 2), lambda p, at: (0, 0))
    return pl.pallas_call(
        forward_kernel,
        grid_spec=pltpu.PrefetchScalarGridSpec(
            num_scalar_prefetch=1,
            grid=(pairs,),
            in_specs=[
                pl.BlockSpec((rows, width), lambda p, at: (0, 0)),
                weight(0),
                weight(1),
                weight(2),
                weight(0),
            ],
            out_specs=[
                pl.BlockSpec((rows, width), lambda p, at: (0, 0)),
                pl.BlockSpec((3, rows, cols), lambda p, at: (0, 0, p)),
                pl.BlockSpec((1, windows, 2, WINDOW, WINDOW), lambda p, at: (p, 0, 0, 0, 0)),
                pl.BlockSpec((ext_tok, cols), lambda p, at: (0, p)),
                piece(own_tok),
                piece(own_tok),
                piece(ext_tok - own_tok),
                piece(ext_tok - own_tok),
            ],
            scratch_shapes=[pltpu.VMEM((rows, cols), BF), pltpu.VMEM((ext_tok, width), F32)],
        ),
        out_shape=[
            pltpu.HBM((rows, width), BF),
            pltpu.HBM((3, rows, heads_w), BF),
            pltpu.HBM((pairs, windows, 2, WINDOW, WINDOW), BF),
            pltpu.HBM((ext_tok, heads_w), BF),
            jax.ShapeDtypeStruct((own_tok, width // 2), F32),
            jax.ShapeDtypeStruct((own_tok, width // 2), BF),
            jax.ShapeDtypeStruct((ext_tok - own_tok, width // 2), BF),
            jax.ShapeDtypeStruct((ext_tok - own_tok, width // 2), BF),
        ],
        compiler_params=pltpu.CompilerParams(vmem_limit_bytes=VMEM_LIMIT),
        name="encoder_forward",
    )(at, x_roll, w_t, w_t, w_t, weight_out)


def out_grad_kernel(masks, at, d_ref, wo_ref, pa_ref, d_attn, even, odd, turned):
    me = at[2]
    block = even.shape[1]
    d_ext = d_ref[...]
    d_attn[...] = (dot_nt(d_ext, wo_ref[...]) * (1.0 / POOL)).astype(BF)
    turned[...] = pa_ref[...].T
    for bit, ref in ((0, even), (masks[0], odd)):
        for j, k in enumerate(offsets(masks[1:])):
            start = pl.multiple_of((me ^ (k | bit)) * block, block)
            ref[j] = dot(turned[pl.ds(start, block), :], d_ext).astype(BF)


def out_grad(d_ext, weight_out, pooled_attn, at, masks):
    heads_w, width = weight_out.shape
    n = 2 ** len(masks)
    blocks = jax.ShapeDtypeStruct((n // 2, heads_w // n, width), BF)
    whole = pl.BlockSpec(memory_space=pltpu.VMEM)
    return pl.pallas_call(
        functools.partial(out_grad_kernel, masks),
        in_specs=[pl.BlockSpec(memory_space=pltpu.SMEM), whole, whole, whole],
        out_specs=[whole] * 3,
        out_shape=[jax.ShapeDtypeStruct(pooled_attn.shape, BF), blocks, blocks],
        scratch_shapes=[pltpu.VMEM((heads_w, pooled_attn.shape[0]), BF)],
        compiler_params=pltpu.CompilerParams(vmem_limit_bytes=VMEM_LIMIT),
        name="out_grad",
    )(at, d_ext, weight_out, pooled_attn)


def backward_kernel(masks, at, turned, qkv, probs, d_ref, even, odd, grads):
    shift, me = at[0], at[2]
    rows = turned.shape[1]
    cols = d_ref.shape[1]
    block = even.shape[2]
    tok_shape = (rows, d_ref.shape[0])
    tok_of = (lax.broadcasted_iota(jnp.int32, tok_shape, 0) + shift) // POOL
    member = tok_of == lax.broadcasted_iota(jnp.int32, tok_shape, 1)
    d_rows = dot(jnp.where(member, 1.0, 0.0).astype(BF), d_ref[...]).astype(BF)
    for w in range(rows // WINDOW):
        span = pl.ds(w * WINDOW, WINDOW)
        q, k, v = qkv[0, span, :], qkv[1, span, :], qkv[2, span, :]
        d_out = d_rows[w * WINDOW : (w + 1) * WINDOW]
        none = jnp.zeros_like(q)
        sums = [0.0, 0.0, 0.0]
        for h in range(cols // HEAD):
            own = head_mask(q.shape, h)
            low = probs[0, w, h]
            weight = low.astype(F32)
            d_weight = dot_nt(jnp.where(own, v, none), d_out)
            centre = jnp.sum(weight * d_weight, axis=0, keepdims=True)
            d_score = (weight * (d_weight - centre) * HEAD ** (-0.5)).astype(BF)
            sums[0] += dot_tn(d_score, jnp.where(own, k, none))
            sums[1] += dot(d_score, jnp.where(own, q, none))
            sums[2] += dot(low, jnp.where(own, d_out, none))
        for i in range(3):
            grads[span, i * cols : (i + 1) * cols] = sums[i].astype(BF)
    d_all = grads[...]
    for bit, ref in ((0, even), (masks[0], odd)):
        for j, k in enumerate(offsets(masks[1:])):
            start = pl.multiple_of((me ^ (k | bit)) * block, block)
            term = dot(turned[pl.ds(start, block), :], d_all).astype(BF)
            for i in range(3):
                ref[j, i] = term[:, i * cols : (i + 1) * cols]


def encoder_backward(turned, qkv, probs, d_attn, at, masks, first, count):
    width, rows = turned.shape
    n = 2 ** len(masks)
    cols = 2 * HEAD
    windows = rows // WINDOW
    block = width // n
    out = pl.BlockSpec((n // 2, 3, block, cols), lambda p, at: (0, 0, 0, p))
    shape = jax.ShapeDtypeStruct((n // 2, 3, block, cols * count), BF)
    return pl.pallas_call(
        functools.partial(backward_kernel, masks),
        grid_spec=pltpu.PrefetchScalarGridSpec(
            num_scalar_prefetch=1,
            grid=(count,),
            in_specs=[
                pl.BlockSpec((width, rows), lambda p, at: (0, 0)),
                pl.BlockSpec((3, rows, cols), lambda p, at: (0, 0, p + first)),
                pl.BlockSpec(
                    (1, windows, 2, WINDOW, WINDOW), lambda p, at: (p + first, 0, 0, 0, 0)
                ),
                pl.BlockSpec((d_attn.shape[0], cols), lambda p, at: (0, p + first)),
            ],
            out_specs=[out, out],
            scratch_shapes=[pltpu.VMEM((rows, 3 * cols), BF)],
        ),
        out_shape=[shape, shape],
        compiler_params=pltpu.CompilerParams(vmem_limit_bytes=VMEM_LIMIT),
        name="encoder_backward",
    )(at, turned, qkv, probs, d_attn)


def moves(order, piece):
    count = len(order)
    for e, offset in enumerate(order):
        for b in range(2):
            for i, step in enumerate(order):
                owner = order.index(offset ^ step)
                source_row = ((e * 2 + b) * count + i) * piece
                owner_row = ((owner * count + i) * 2 + b) * piece
                yield source_row, owner_row


def chunks_of(rows):
    return [slice(r, min(r + CHUNK, rows)) for r in range(0, rows, CHUNK)]


def column_starts(order, at, block):
    if order is None:
        return None
    offset = [k | bit for bit in (0, SPLIT) for k in order]
    return [pl.multiple_of((at[2] ^ k) * block, block) for k in offset]


def weight_rows(here, there):
    return jnp.concatenate([w[...].reshape(-1, w.shape[-1]) for w in (here, there)], axis=0)


def both(index, size):
    return (
        pl.ds(pl.multiple_of(index * size, size), size),
        pl.ds(pl.multiple_of((1 - index) * size, size), size),
    )


def kv_columns(low, at, kva, kvb, side, rows):
    feats, cols = kva.shape[0], kvb.shape[2]
    mine, across = both(at[2] % 2, feats)
    span = pl.ds(pl.multiple_of(side * cols, cols), cols)
    part = dot(low[rows, mine], kva[:, span]) + dot(low[rows, across], kvb[side ^ at[4]])
    return part.astype(BF)


def lift_kernel(table, order, at, ta, tb, here, there, gain, kva, kvb, *refs):
    lifted, squares, low, send, tok = refs
    core = at[3]
    near, far = both(core, ta.shape[1])
    piece = ta.shape[0] // len(table) if table else 0
    for source_row, owner_row in table:
        tok[owner_row : owner_row + piece, near] = ta[source_row : source_row + piece]
        tok[owner_row : owner_row + piece, far] = tb[source_row : source_row + piece]
    if not table:
        tok[:, near] = ta[...]
        tok[:, far] = tb[...]
    block = here.shape[1]
    starts = column_starts(order, at, block)
    weight = weight_rows(here, there)
    group_rows = squares.shape[1]
    for rows in chunks_of(tok.shape[0]):
        x = tok[rows]
        if starts:
            x = jnp.concatenate([tok[rows, pl.ds(start, block)] for start in starts], axis=1)
        product = dot(x, weight)
        lifted[rows] = product.astype(BF)
        low[rows] = (product * gain[...]).astype(BF)
        sums = jnp.sum(product * product, axis=1, keepdims=True)
        for first in range(0, rows.stop - rows.start, group_rows):
            column = sums[first : first + group_rows]
            owner = (rows.start + first) // group_rows
            squares[owner : owner + 1] = jnp.broadcast_to(column, (group_rows,) * 2).T[:1]
        send[rows] = kv_columns(low, at, kva, kvb, 1 - core, rows)


def lift(table, order, at, own_tok, ta, tb, here, there, gain, kva, kvb):
    rows, half = ta.shape
    feats, cols = kva.shape[0], kva.shape[1] // 2
    whole = pl.BlockSpec(memory_space=pltpu.VMEM)
    return pl.pallas_call(
        functools.partial(lift_kernel, table, order),
        in_specs=[pl.BlockSpec(memory_space=pltpu.SMEM)] + [whole] * 7,
        out_specs=[whole] * 4,
        out_shape=[
            jax.ShapeDtypeStruct((rows, 2 * feats), BF),
            jax.ShapeDtypeStruct((rows // own_tok, own_tok), F32),
            jax.ShapeDtypeStruct((rows, 2 * feats), BF),
            jax.ShapeDtypeStruct((rows, cols), BF),
        ],
        scratch_shapes=[pltpu.VMEM((rows, 2 * half), BF)],
        compiler_params=pltpu.CompilerParams(vmem_limit_bytes=VMEM_LIMIT),
        name="lift",
    )(at, ta, tb, here, there, gain, kva, kvb)


def keep_kernel(at, low, kva, kvb, keep):
    for rows in chunks_of(low.shape[0]):
        keep[rows] = kv_columns(low, at, kva, kvb, at[3], rows)


def keep_columns(at, low, kva, kvb):
    whole = pl.BlockSpec(memory_space=pltpu.VMEM)
    return pl.pallas_call(
        keep_kernel,
        in_specs=[pl.BlockSpec(memory_space=pltpu.SMEM)] + [whole] * 3,
        out_specs=whole,
        out_shape=jax.ShapeDtypeStruct((low.shape[0], kva.shape[1] // 2), BF),
        compiler_params=pltpu.CompilerParams(vmem_limit_bytes=VMEM_LIMIT),
        name="keep_columns",
    )(at, low, kva, kvb)


def two_parts(column):
    high = column.astype(BF)
    return high, (column - high.astype(F32)).astype(BF)


def finish_kernel(mine, got, squares, d_kv, *refs):
    rows, cols = mine.shape
    kv, load, inner = refs[-3:]
    total = mine[...].astype(F32) + got[...].astype(F32)
    mean = jnp.broadcast_to(squares[...], (rows, rows)).T[:, :1] * (1.0 / LLM_D)
    inv = lax.rsqrt(mean + 1e-05)
    low = (total * inv).astype(BF)
    kv[...] = low
    cot = (low.astype(F32) + d_kv[...].astype(F32)).astype(BF)
    load[:, :cols] = cot
    pull = jnp.sum(cot.astype(F32) * total, axis=1, keepdims=True)
    if len(refs) == 4:
        pull += refs[0][...]
        lane = lax.broadcasted_iota(jnp.int32, (rows, load.shape[1] - cols), 1)
        extra = jnp.zeros(lane.shape, F32)
        for i, part in enumerate(two_parts(inv) + two_parts(pull)):
            extra = jnp.where(lane == i, part.astype(F32), extra)
        load[:, cols:] = extra.astype(BF)
    inner[...] = pull


def finish(mine, got, squares, d_kv, *inner):
    rows, cols = mine.shape
    return pl.pallas_call(
        finish_kernel,
        out_shape=[
            jax.ShapeDtypeStruct((rows, cols), BF),
            jax.ShapeDtypeStruct((rows, cols + LANES * len(inner)), BF),
            jax.ShapeDtypeStruct((rows, 1), F32),
        ],
        compiler_params=pltpu.CompilerParams(vmem_limit_bytes=VMEM_LIMIT),
        name="finish",
    )(mine, got, squares, d_kv, *inner)


def lower_kernel(table, order, at, ca0, ca1, cb0, cb1, here, there, gain, kva, kvb, *refs):
    lifted, send, keep, nat, low = refs
    core, group = at[3], at[4]
    feats, half = kva.shape[0], send.shape[1]
    cols = kva.shape[1] // 2
    near, far = both(core, half)
    mine, across = both(at[2] % 2, feats)
    block = here.shape[1]
    starts = column_starts(order, at, block)
    weight = weight_rows(here, there)
    part_cols = ca0.shape[1]
    piece = ca0.shape[0] // len(table) if table else 0
    for rows in chunks_of(ca0.shape[0]):
        extra = ca1[rows, part_cols:].astype(F32)
        extra_b = cb1[rows, part_cols:].astype(F32)
        inv = extra[:, 0:1] + extra[:, 1:2]
        inner = extra[:, 2:3] + extra[:, 3:4] + extra_b[:, 2:3] + extra_b[:, 3:4]
        pull = inv * inv * inv * inner * (1.0 / LLM_D)
        cots = [
            (jnp.concatenate([c0[rows], c1[rows, :part_cols]], axis=1), side)
            for c0, c1, side in ((ca0, ca1, core), (cb0, cb1, 1 - core))
        ]
        for is_mine, span in ((True, mine), (False, across)):
            d_normed = None
            for cot, side in cots:
                at_side = pl.ds(pl.multiple_of(side * cols, cols), cols)
                part = dot_nt(cot, kva[:, at_side] if is_mine else kvb[side ^ group])
                d_normed = part if d_normed is None else d_normed + part
            low[rows, span] = (
                inv * gain[:, span] * d_normed - lifted[rows, span].astype(F32) * pull
            ).astype(BF)
        d_tok = dot_nt(low[rows], weight).astype(BF)
        if not starts:
            nat[rows] = d_tok
        for i, start in enumerate(starts or ()):
            nat[rows, pl.ds(start, block)] = d_tok[:, i * block : (i + 1) * block]
    for source_row, owner_row in table:
        send[source_row : source_row + piece] = nat[owner_row : owner_row + piece, far]
        keep[source_row : source_row + piece] = nat[owner_row : owner_row + piece, near]
    if not table:
        send[...] = nat[:, far]
        keep[...] = nat[:, near]


def lower(table, order, at, cots, here, there, gain, kva, kvb, lifted):
    rows, width = cots[0].shape[0], lifted.shape[1]
    tok_width = 2 * here.shape[0] * here.shape[1]
    whole = pl.BlockSpec(memory_space=pltpu.VMEM)
    out = jax.ShapeDtypeStruct((rows, tok_width // 2), BF)
    return pl.pallas_call(
        functools.partial(lower_kernel, table, order),
        in_specs=[pl.BlockSpec(memory_space=pltpu.SMEM)] + [whole] * 10,
        out_specs=[whole] * 2,
        out_shape=[out] * 2,
        scratch_shapes=[pltpu.VMEM((rows, tok_width), BF), pltpu.VMEM((rows, width), BF)],
        compiler_params=pltpu.CompilerParams(vmem_limit_bytes=VMEM_LIMIT),
        name="lower",
    )(at, *cots, here, there, gain, kva, kvb, lifted)


def on_device(frames, weight_qkv, weight_out, proj_in, norm_gain, proj_kv, shifts, route, d_kv):
    n = lax.axis_size("tm")
    me = lax.axis_index("tm")
    core = lax.axis_index("mp")
    rows, width = frames.shape
    half_w = width // 2
    shift = shifts[0]
    own_tok = rows // POOL
    tail_tok = WINDOW // POOL
    ext_tok = own_tok + tail_tok
    feats = proj_kv.shape[0]
    kv_half = proj_kv.shape[1] // 2
    piece = own_tok // n

    part = lax.dynamic_slice_in_dim(frames, core * (WINDOW // 2), WINDOW // 2, 0)
    mine = to_tm(part, -1, False)
    w_t = jnp.transpose(weight_qkv, (1, 2, 0)).reshape(-1, width)
    group = lax.axis_index("groups")
    two_groups = lax.axis_size("groups") == 2
    if not two_groups:
        group = group * 0
    proj_kv, part = lax.optimization_barrier((proj_kv, part))
    kv_near = swap_tm(lax.dynamic_slice_in_dim(proj_kv, group * kv_half, kv_half, 1), SPLIT)
    proj_in, w_t = lax.optimization_barrier((proj_in, w_t))

    masks = group_bits()
    order = offsets(masks)
    members = order + [k | SPLIT for k in order]
    count = n // 2
    blocks = []
    for k in order:
        pair = lax.dynamic_slice_in_dim(proj_in, (me ^ k) // 2 * 2 * feats, 2 * feats, 1)
        blocks.append(swap_tm(pair, k) if k else pair)

    other = swap_mp(mine)
    halo = jnp.where(
        core == 0, jnp.concatenate([mine, other], 0), jnp.concatenate([other, mine], 0)
    )
    x_roll = lax.dynamic_slice_in_dim(jnp.concatenate([frames, halo], 0), shift, rows, 0)

    at = jnp.stack([shift, rows * n - shift - me * rows, me, core, group]).astype(jnp.int32)
    normed, qkv, probs, pooled_attn, own_near, own_far, tail_near, tail_far = encoder_forward(
        x_roll, w_t, weight_out, at, ext_tok
    )
    own_far, kv_near = lax.optimization_barrier((own_far, kv_near))
    swap_groups = lambda block: lax.ppermute(block, "groups", [(0, 1), (1, 0)])
    if two_groups:
        kv_far = swap_groups(kv_near)
    else:
        kv_far = swap_tm(proj_kv[:, kv_half:], SPLIT)
    turned = normed.T
    route, norm_gain, d_kv, pooled_attn = lax.optimization_barrier(
        (route, norm_gain, d_kv, pooled_attn)
    )
    gain = lax.dynamic_slice_in_dim(norm_gain, me // 2 * 2 * feats, 2 * feats, 0)
    gain = gain.reshape(1, -1)
    owner_at = (lax.dynamic_index_in_dim(route, me, 0, keepdims=False) ^ me)[None, :]
    sort = owner_at == jnp.array(members, jnp.int32)[:, None]
    sort = jnp.kron(sort.astype(BF), jnp.eye(piece, dtype=BF))
    source_at = jnp.arange(n, dtype=jnp.int32) ^ me
    spread = source_at[:, None] == jnp.array(
        [k | bit for k in order for bit in (0, SPLIT)], jnp.int32
    )
    spread = jnp.kron(spread.astype(BF), jnp.eye(piece, dtype=BF))
    d_kv = dot_tn(spread, d_kv).astype(BF)

    from_core = swap_mp(own_far)
    tail_a = to_tm(tail_near, 1, False)
    tail_b = to_tm(tail_far, 1, True)
    tail_a, tail_b, from_core, blocks = lax.optimization_barrier(
        (tail_a, tail_b, from_core, blocks)
    )
    own_pool = (
        jnp.arange(rows, dtype=jnp.int32)[None, :] // POOL
        == jnp.arange(own_tok, dtype=jnp.int32)[:, None]
    ).astype(BF) * (1.0 / POOL)
    x_mean = dot(own_pool, lax.dynamic_slice_in_dim(frames, core * half_w, half_w, 1))
    pooled = x_mean + own_near + from_core.astype(F32)
    tail = tail_a.astype(F32) + tail_b.astype(F32)
    pooled = jnp.concatenate([pooled[:tail_tok] + tail, pooled[tail_tok:]], 0).astype(BF)

    sorted_tok = dot(sort, pooled).astype(BF).reshape(2, count * piece, half_w)
    handed = swap_tm(sorted_tok[1], SPLIT)
    here = jnp.stack(blocks)
    handed, here = lax.optimization_barrier((handed, here))
    there = swap_tm(here, SPLIT)
    pair_tok = jnp.stack([sorted_tok[0], handed])
    tok_half = gather_doubling(pair_tok, masks[-1:])
    tok_half, turned, d_kv = lax.optimization_barrier((tok_half, turned, d_kv))
    kva, kvb = proj_kv, jnp.stack([kv_near, kv_far])
    at_rows = order
    if width // n % LANES:
        stacked = jnp.concatenate([here, there])
        source = jnp.arange(n, dtype=jnp.int32) ^ me
        found = source[:, None] == jnp.array(members, jnp.int32)[None, :]
        place = jnp.sum(found * jnp.arange(n, dtype=jnp.int32)[None, :], axis=1)
        stacked = jnp.take(stacked, place, axis=0)
        here, there = jnp.split(stacked, 2)
        at_rows = None
    for mask in reversed(masks[:-1]):
        tok_half = jnp.concatenate([tok_half, swap_tm(tok_half, mask)], axis=0)
    tok_half = tok_half.reshape(-1, half_w)
    tok_other = swap_mp(tok_half)
    table = list(moves(order, piece))
    source_rows = np.concatenate([np.arange(r, r + piece) for r, _ in table])
    owner_rows = np.concatenate([np.arange(r, r + piece) for _, r in table])
    by_xla = piece % 16 != 0
    if by_xla:
        at_owner = source_rows[np.argsort(owner_rows)]
        tok_half, tok_other = tok_half[at_owner], tok_other[at_owner]
        table = []
    lifted, squares, scaled, kv_send = lift(
        table, at_rows, at, own_tok, tok_half, tok_other, here, there, gain, kva, kvb
    )
    kv_got = swap_mp(kv_send)
    kv_keep = keep_columns(at, scaled, kva, kvb)
    square_sum = scatter_halving(squares + swap_mp(squares), masks, F32)
    kv_part = (kv_keep.astype(F32) + kv_got.astype(F32)).astype(BF)
    kv_parts = jnp.split(kv_part.reshape(count, own_tok, kv_half), 2, axis=2)
    (mine_a, got_a), (mine_b, got_b) = scatter_last(kv_parts, masks)
    square_sum = square_sum.reshape(1, own_tok)
    d_kv_a, d_kv_b = jnp.split(d_kv, 2, axis=1)
    kv_a, load_a, inner = finish(mine_a, got_a, square_sum, d_kv_a)
    kv_b, load_b, _ = finish(mine_b, got_b, square_sum, d_kv_b, inner)
    kv = dot(spread, jnp.concatenate([kv_a, kv_b], axis=1)).astype(BF)
    loads = gather_parts([load_a, load_b], masks)
    loads = [load.reshape(count * own_tok, -1) for load in loads]
    cots = loads + [swap_mp(load) for load in loads]
    d_send, d_keep = lower(
        table, at_rows, at, cots, here, there, gain, kva, kvb, lifted
    )
    if by_xla:
        at_source = owner_rows[np.argsort(source_rows)]
        d_send, d_keep = d_send[at_source], d_keep[at_source]
    d_part = d_keep.astype(F32) + swap_mp(d_send).astype(F32)
    d_pair = scatter_halving(d_part.reshape(count, 2, count * piece, half_w), masks, BF)
    d_sorted = jnp.concatenate([d_pair[0].astype(BF), swap_tm(d_pair[1].astype(BF), SPLIT)], 0)
    d_half = dot_tn(sort, d_sorted).astype(BF)

    d_other = swap_mp(d_half)
    next_a = to_tm(d_half[:tail_tok], -1, False)
    next_b = to_tm(d_half[:tail_tok], -1, True)
    left = jnp.concatenate([d_half, next_a], 0)
    right = jnp.concatenate([d_other, next_b], 0)
    d_ext = jnp.where(
        core == 0, jnp.concatenate([left, right], 1), jnp.concatenate([right, left], 1)
    )
    bits = tm_bits()
    crossed = [bits[1], bits[0]] + bits[2:]
    d_attn, out_even, out_odd = out_grad(d_ext, weight_out, pooled_attn, at, bits)
    chunks = []
    for pair, path in enumerate((bits, bits, bits, crossed)):
        even, odd = encoder_backward(turned, qkv, probs, d_attn, at, path, pair, 1)
        even, odd, at = lax.optimization_barrier((even, odd, at))
        chunks.append((even, odd, path))
    chunks.append((out_even, out_odd, bits))
    steps = list(range(len(chunks))) * len(bits)
    if len(bits) == 3:
        steps = [0, 0, 1, 3, 0, 1, 4, 1, 4, 2, 3, 4, 2, 3, 2]
    chunks = scatter_chunks(chunks, steps, even)
    grad_out = chunks.pop()
    grad_qkv = jnp.transpose(jnp.concatenate(chunks, axis=-1), (1, 0, 2))
    return kv, grad_qkv, grad_out


def solution(mesh):
    in_specs = (
        P(("groups", "tm"), None),
        P(None, None, "mp"),
        P("mp", None),
        P("tm", "mp"),
        P("mp"),
        P(("mp", "tm"), None),
        P(),
        P(),
        P(("groups", "tm"), "mp"),
    )
    out_specs = (
        P(("groups", "tm"), "mp"),
        P(("groups", "tm"), None, "mp"),
        P(("groups", "mp", "tm"), None),
    )
    return jax.shard_map(
        on_device, mesh=mesh, in_specs=in_specs, out_specs=out_specs, check_vma=False
    )
```

```python
import functools

import jax
import jax.numpy as jnp
import numpy as np
from jax import lax
from jax.experimental import pallas as pl
from jax.experimental.pallas import tpu as pltpu
from jax.sharding import PartitionSpec as P

HEAD = 64
WINDOW = 256
POOL = 4
LLM_D = 8192
BF = jnp.bfloat16
F32 = jnp.float32
VMEM_LIMIT = 48 << 20
SPLIT = 1
CHUNK = 512
LANES = 128


def dot(a, b):
    return jnp.dot(a, b, preferred_element_type=F32)


def dot_nt(a, b):
    return lax.dot_general(a, b, (((1,), (1,)), ((), ())), preferred_element_type=F32)


def dot_tn(a, b):
    return lax.dot_general(a, b, (((0,), (0,)), ((), ())), preferred_element_type=F32)


def swap_tm(block, mask):
    n = lax.axis_size("tm")
    return lax.ppermute(block, "tm", [(i, i ^ mask) for i in range(n)])


def swap_mp(block):
    n = lax.axis_size("mp")
    return lax.ppermute(block, "mp", [(i, n - 1 - i) for i in range(n)])


def to_tm(block, step, cross):
    n, m = lax.axis_size("tm"), lax.axis_size("mp")
    pairs = []
    for i in range(n):
        for c in range(m):
            pairs.append((i * m + c, (i + step) % n * m + (m - 1 - c if cross else c)))
    return lax.ppermute(block, ("tm", "mp"), pairs)


def offsets(masks):
    order = [0]
    for mask in reversed(masks):
        order = order + [k | mask for k in order]
    return order


def tm_bits():
    n = lax.axis_size("tm")
    return [1 << i for i in range(n.bit_length() - 1)]


def group_bits():
    return [bit for bit in tm_bits() if bit != SPLIT]


def gather_doubling(block, masks):
    block = block[None]
    for mask in reversed(masks):
        block = jnp.concatenate([block, swap_tm(block, mask)], axis=0)
    return block


def scatter_halving(blocks, masks, kind):
    total = blocks
    for mask in masks:
        low = total.astype(kind)
        half = low.shape[0] // 2
        total = low[:half].astype(F32) + swap_tm(low[half:], mask).astype(F32)
    return total[0]


def in_turn(got, last):
    return got if last is None else lax.optimization_barrier((got, last))[0]


def scatter_last(parts, masks):
    lows, pairs, last = list(parts), [], None
    for mask in masks:
        for i, low in enumerate(lows):
            half = low.shape[0] // 2
            got = in_turn(swap_tm(low[half:], mask), last)
            if mask == masks[-1]:
                pairs.append((low[0], got[0]))
                last = got
                continue
            lows[i] = last = (low[:half].astype(F32) + got.astype(F32)).astype(BF)
    return pairs


def gather_parts(parts, masks):
    parts, last = [part[None] for part in parts], None
    for mask in reversed(masks):
        for i, part in enumerate(parts):
            got = in_turn(swap_tm(part, mask), last)
            parts[i] = last = jnp.concatenate([part, got], axis=0)
    return parts


def scatter_chunks(chunks, steps, last):
    sums = [lower for lower, _, _ in chunks]
    sends = [upper for _, upper, _ in chunks]
    stage = [0] * len(chunks)
    for i in steps:
        got = in_turn(swap_tm(sends[i], chunks[i][2][stage[i]]), last)
        stage[i] += 1
        total = sums[i].astype(F32) + got.astype(F32)
        if total.shape[0] == 1:
            sums[i] = total[0]
            continue
        low = last = total.astype(BF)
        half = low.shape[0] // 2
        sums[i], sends[i] = low[:half], low[half:]
    return sums


def head_mask(shape, head):
    return lax.broadcasted_iota(jnp.int32, shape, 1) // HEAD == head


def forward_kernel(at, x_ref, wq_ref, wk_ref, wv_ref, wo_ref, *refs):
    normed, qkv, probs, pooled, own_near, own_far, tail_near, tail_far, attn, out = refs
    shift, border, core = at[0], at[1], at[3]
    rows = x_ref.shape[0]
    cols = wq_ref.shape[0]

    @pl.when(pl.program_id(0) == 0)
    def _():
        x = x_ref[...].astype(F32)
        scale = lax.rsqrt(jnp.mean(x * x, axis=-1, keepdims=True) + 1e-05)
        normed[...] = (x * scale).astype(BF)
        out[...] = jnp.zeros_like(out)

    base = normed[...]
    for i, w_ref in enumerate((wq_ref, wk_ref, wv_ref)):
        qkv[i] = dot_nt(base, w_ref[...]).astype(BF)
    windows, heads = range(rows // WINDOW), range(cols // HEAD)
    spans = [pl.ds(w * WINDOW, WINDOW) for w in windows]
    own = [head_mask((WINDOW, cols), h) for h in heads]
    scores = []
    for w in windows:
        q, k = qkv[0, spans[w], :], qkv[1, spans[w], :]
        for h in heads:
            scores.append(dot_nt(jnp.where(own[h], k, jnp.zeros_like(k)), q))
    square = (WINDOW, WINDOW)
    key_at = lax.broadcasted_iota(jnp.int32, square, 0)
    query_at = lax.broadcasted_iota(jnp.int32, square, 1)
    lows = []
    for w in windows:
        edge = border - w * WINDOW
        allowed = (key_at >= edge) == (query_at >= edge)
        for h in heads:
            score = jnp.where(allowed, scores[w * len(heads) + h] * HEAD ** (-0.5), -1e30)
            terms = jnp.exp(score - jnp.max(score, axis=0, keepdims=True))
            low = (terms * (1.0 / jnp.sum(terms, axis=0, keepdims=True))).astype(BF)
            probs[0, w, h] = low
            lows.append(low)
    for w in windows:
        v = qkv[2, spans[w], :]
        attended = None
        for h in heads:
            part = dot_tn(lows[w * len(heads) + h], v)
            attended = part if attended is None else jnp.where(own[h], part, attended)
        attn[spans[w], :] = attended.astype(BF)
    tok_shape = (pooled.shape[0], rows)
    tok_of = (lax.broadcasted_iota(jnp.int32, tok_shape, 1) + shift) // POOL
    member = tok_of == lax.broadcasted_iota(jnp.int32, tok_shape, 0)
    pool = jnp.where(member, 1.0 / POOL, 0.0).astype(BF)
    low = dot(pool, attn[...]).astype(BF)
    pooled[...] = low
    out[...] += dot(low, wo_ref[...])

    @pl.when(pl.program_id(0) == pl.num_programs(0) - 1)
    def _():
        count, half = own_near.shape
        near = pl.ds(pl.multiple_of(core * half, half), half)
        far = pl.ds(pl.multiple_of((1 - core) * half, half), half)
        own_near[...] = out[:count, near]
        own_far[...] = out[:count, far].astype(BF)
        tail_near[...] = out[count:, near].astype(BF)
        tail_far[...] = out[count:, far].astype(BF)


def encoder_forward(x_roll, w_t, weight_out, at, ext_tok):
    rows, width = x_roll.shape
    heads_w = weight_out.shape[0]
    cols = 2 * HEAD
    pairs = heads_w // cols
    windows = rows // WINDOW
    weight = lambda i: pl.BlockSpec((cols, width), lambda p, at: (i * pairs + p, 0))
    own_tok = rows // POOL
    piece = lambda count: pl.BlockSpec((count, width // 2), lambda p, at: (0, 0))
    return pl.pallas_call(
        forward_kernel,
        grid_spec=pltpu.PrefetchScalarGridSpec(
            num_scalar_prefetch=1,
            grid=(pairs,),
            in_specs=[
                pl.BlockSpec((rows, width), lambda p, at: (0, 0)),
                weight(0),
                weight(1),
                weight(2),
                weight(0),
            ],
            out_specs=[
                pl.BlockSpec((rows, width), lambda p, at: (0, 0)),
                pl.BlockSpec((3, rows, cols), lambda p, at: (0, 0, p)),
                pl.BlockSpec((1, windows, 2, WINDOW, WINDOW), lambda p, at: (p, 0, 0, 0, 0)),
                pl.BlockSpec((ext_tok, cols), lambda p, at: (0, p)),
                piece(own_tok),
                piece(own_tok),
                piece(ext_tok - own_tok),
                piece(ext_tok - own_tok),
            ],
            scratch_shapes=[pltpu.VMEM((rows, cols), BF), pltpu.VMEM((ext_tok, width), F32)],
        ),
        out_shape=[
            pltpu.HBM((rows, width), BF),
            pltpu.HBM((3, rows, heads_w), BF),
            pltpu.HBM((pairs, windows, 2, WINDOW, WINDOW), BF),
            pltpu.HBM((ext_tok, heads_w), BF),
            jax.ShapeDtypeStruct((own_tok, width // 2), F32),
            jax.ShapeDtypeStruct((own_tok, width // 2), BF),
            jax.ShapeDtypeStruct((ext_tok - own_tok, width // 2), BF),
            jax.ShapeDtypeStruct((ext_tok - own_tok, width // 2), BF),
        ],
        compiler_params=pltpu.CompilerParams(vmem_limit_bytes=VMEM_LIMIT),
        name="encoder_forward",
    )(at, x_roll, w_t, w_t, w_t, weight_out)


def out_grad_kernel(masks, at, d_ref, wo_ref, pa_ref, d_attn, even, odd, turned):
    me = at[2]
    block = even.shape[1]
    d_ext = d_ref[...]
    d_attn[...] = (dot_nt(d_ext, wo_ref[...]) * (1.0 / POOL)).astype(BF)
    turned[...] = pa_ref[...].T
    for bit, ref in ((0, even), (masks[0], odd)):
        for j, k in enumerate(offsets(masks[1:])):
            start = pl.multiple_of((me ^ (k | bit)) * block, block)
            ref[j] = dot(turned[pl.ds(start, block), :], d_ext).astype(BF)


def out_grad(d_ext, weight_out, pooled_attn, at, masks):
    heads_w, width = weight_out.shape
    n = 2 ** len(masks)
    blocks = jax.ShapeDtypeStruct((n // 2, heads_w // n, width), BF)
    whole = pl.BlockSpec(memory_space=pltpu.VMEM)
    return pl.pallas_call(
        functools.partial(out_grad_kernel, masks),
        in_specs=[pl.BlockSpec(memory_space=pltpu.SMEM), whole, whole, whole],
        out_specs=[whole] * 3,
        out_shape=[jax.ShapeDtypeStruct(pooled_attn.shape, BF), blocks, blocks],
        scratch_shapes=[pltpu.VMEM((heads_w, pooled_attn.shape[0]), BF)],
        compiler_params=pltpu.CompilerParams(vmem_limit_bytes=VMEM_LIMIT),
        name="out_grad",
    )(at, d_ext, weight_out, pooled_attn)


def backward_kernel(masks, at, turned, qkv, probs, d_ref, even, odd, grads):
    shift, me = at[0], at[2]
    rows = turned.shape[1]
    cols = d_ref.shape[1]
    block = even.shape[2]
    tok_shape = (rows, d_ref.shape[0])
    tok_of = (lax.broadcasted_iota(jnp.int32, tok_shape, 0) + shift) // POOL
    member = tok_of == lax.broadcasted_iota(jnp.int32, tok_shape, 1)
    d_rows = dot(jnp.where(member, 1.0, 0.0).astype(BF), d_ref[...]).astype(BF)
    for w in range(rows // WINDOW):
        span = pl.ds(w * WINDOW, WINDOW)
        q, k, v = qkv[0, span, :], qkv[1, span, :], qkv[2, span, :]
        d_out = d_rows[w * WINDOW : (w + 1) * WINDOW]
        none = jnp.zeros_like(q)
        sums = [0.0, 0.0, 0.0]
        for h in range(cols // HEAD):
            own = head_mask(q.shape, h)
            low = probs[0, w, h]
            weight = low.astype(F32)
            d_weight = dot_nt(jnp.where(own, v, none), d_out)
            centre = jnp.sum(weight * d_weight, axis=0, keepdims=True)
            d_score = (weight * (d_weight - centre) * HEAD ** (-0.5)).astype(BF)
            sums[0] += dot_tn(d_score, jnp.where(own, k, none))
            sums[1] += dot(d_score, jnp.where(own, q, none))
            sums[2] += dot(low, jnp.where(own, d_out, none))
        for i in range(3):
            grads[span, i * cols : (i + 1) * cols] = sums[i].astype(BF)
    d_all = grads[...]
    for bit, ref in ((0, even), (masks[0], odd)):
        for j, k in enumerate(offsets(masks[1:])):
            start = pl.multiple_of((me ^ (k | bit)) * block, block)
            term = dot(turned[pl.ds(start, block), :], d_all).astype(BF)
            for i in range(3):
                ref[j, i] = term[:, i * cols : (i + 1) * cols]


def encoder_backward(turned, qkv, probs, d_attn, at, masks, first, count):
    width, rows = turned.shape
    n = 2 ** len(masks)
    cols = 2 * HEAD
    windows = rows // WINDOW
    block = width // n
    out = pl.BlockSpec((n // 2, 3, block, cols), lambda p, at: (0, 0, 0, p))
    shape = jax.ShapeDtypeStruct((n // 2, 3, block, cols * count), BF)
    return pl.pallas_call(
        functools.partial(backward_kernel, masks),
        grid_spec=pltpu.PrefetchScalarGridSpec(
            num_scalar_prefetch=1,
            grid=(count,),
            in_specs=[
                pl.BlockSpec((width, rows), lambda p, at: (0, 0)),
                pl.BlockSpec((3, rows, cols), lambda p, at: (0, 0, p + first)),
                pl.BlockSpec(
                    (1, windows, 2, WINDOW, WINDOW), lambda p, at: (p + first, 0, 0, 0, 0)
                ),
                pl.BlockSpec((d_attn.shape[0], cols), lambda p, at: (0, p + first)),
            ],
            out_specs=[out, out],
            scratch_shapes=[pltpu.VMEM((rows, 3 * cols), BF)],
        ),
        out_shape=[shape, shape],
        compiler_params=pltpu.CompilerParams(vmem_limit_bytes=VMEM_LIMIT),
        name="encoder_backward",
    )(at, turned, qkv, probs, d_attn)


def moves(order, piece):
    count = len(order)
    for e, offset in enumerate(order):
        for b in range(2):
            for i, step in enumerate(order):
                owner = order.index(offset ^ step)
                source_row = ((e * 2 + b) * count + i) * piece
                owner_row = ((owner * count + i) * 2 + b) * piece
                yield source_row, owner_row


def chunks_of(rows):
    return [slice(r, min(r + CHUNK, rows)) for r in range(0, rows, CHUNK)]


def column_starts(order, at, block):
    if order is None:
        return None
    offset = [k | bit for bit in (0, SPLIT) for k in order]
    return [pl.multiple_of((at[2] ^ k) * block, block) for k in offset]


def weight_rows(blocks):
    return jnp.concatenate([block[...] for block in blocks], axis=0)


def both(index, size):
    return (
        pl.ds(pl.multiple_of(index * size, size), size),
        pl.ds(pl.multiple_of((1 - index) * size, size), size),
    )


def kv_columns(low, at, kva, near, far, side, rows, out):
    feats, cols = kva.shape[0], near.shape[1]
    mine, across = both(at[2] % 2, feats)
    span = pl.ds(pl.multiple_of(side * cols, cols), cols)
    for place, part in enumerate((near, far)):

        @pl.when(side ^ at[4] == place)
        def _():
            total = dot(low[rows, mine], kva[:, span]) + dot(low[rows, across], part[...])
            out[rows] = total.astype(BF)


def lift_kernel(table, order, at, ta, tb, gain, kva, kv_near, kv_far, *refs):
    blocks, (lifted, squares, low, send, tok) = refs[:-5], refs[-5:]
    core = at[3]
    near, far = both(core, ta.shape[1])
    piece = ta.shape[0] // len(table) if table else 0
    for source_row, owner_row in table:
        tok[owner_row : owner_row + piece, near] = ta[source_row : source_row + piece]
        tok[owner_row : owner_row + piece, far] = tb[source_row : source_row + piece]
    if not table:
        tok[:, near] = ta[...]
        tok[:, far] = tb[...]
    block = blocks[0].shape[0]
    starts = column_starts(order, at, block)
    weight = weight_rows(blocks)
    group_rows = squares.shape[1]
    for rows in chunks_of(tok.shape[0]):
        x = tok[rows]
        if starts:
            x = jnp.concatenate([tok[rows, pl.ds(start, block)] for start in starts], axis=1)
        product = dot(x, weight)
        lifted[rows] = product.astype(BF)
        low[rows] = (product * gain[...]).astype(BF)
        sums = jnp.sum(product * product, axis=1, keepdims=True)
        for first in range(0, rows.stop - rows.start, group_rows):
            column = sums[first : first + group_rows]
            owner = (rows.start + first) // group_rows
            squares[owner : owner + 1] = jnp.broadcast_to(column, (group_rows,) * 2).T[:1]
        kv_columns(low, at, kva, kv_near, kv_far, 1 - core, rows, send)


def lift(table, order, at, own_tok, ta, tb, gain, kvs, blocks):
    rows, half = ta.shape
    feats, cols = kvs[0].shape[0], kvs[0].shape[1] // 2
    whole = pl.BlockSpec(memory_space=pltpu.VMEM)
    return pl.pallas_call(
        functools.partial(lift_kernel, table, order),
        in_specs=[pl.BlockSpec(memory_space=pltpu.SMEM)] + [whole] * (6 + len(blocks)),
        out_specs=[whole] * 4,
        out_shape=[
            jax.ShapeDtypeStruct((rows, 2 * feats), BF),
            jax.ShapeDtypeStruct((rows // own_tok, own_tok), F32),
            jax.ShapeDtypeStruct((rows, 2 * feats), BF),
            jax.ShapeDtypeStruct((rows, cols), BF),
        ],
        scratch_shapes=[pltpu.VMEM((rows, 2 * half), BF)],
        compiler_params=pltpu.CompilerParams(vmem_limit_bytes=VMEM_LIMIT),
        name="lift",
    )(at, ta, tb, gain, *kvs, *blocks)


def keep_kernel(at, low, kva, kv_near, kv_far, keep):
    for rows in chunks_of(low.shape[0]):
        kv_columns(low, at, kva, kv_near, kv_far, at[3], rows, keep)


def keep_columns(at, low, kvs):
    whole = pl.BlockSpec(memory_space=pltpu.VMEM)
    return pl.pallas_call(
        keep_kernel,
        in_specs=[pl.BlockSpec(memory_space=pltpu.SMEM)] + [whole] * 4,
        out_specs=whole,
        out_shape=jax.ShapeDtypeStruct((low.shape[0], kvs[0].shape[1] // 2), BF),
        compiler_params=pltpu.CompilerParams(vmem_limit_bytes=VMEM_LIMIT),
        name="keep_columns",
    )(at, low, *kvs)


def two_parts(column):
    high = column.astype(BF)
    return high, (column - high.astype(F32)).astype(BF)


def finish_kernel(mine, got, squares, d_kv, *refs):
    rows, cols = mine.shape
    kv, load, inner = refs[-3:]
    total = mine[...].astype(F32) + got[...].astype(F32)
    mean = jnp.broadcast_to(squares[...], (rows, rows)).T[:, :1] * (1.0 / LLM_D)
    inv = lax.rsqrt(mean + 1e-05)
    low = (total * inv).astype(BF)
    kv[...] = low
    cot = (low.astype(F32) + d_kv[...].astype(F32)).astype(BF)
    load[:, :cols] = cot
    pull = jnp.sum(cot.astype(F32) * total, axis=1, keepdims=True)
    if len(refs) == 4:
        pull += refs[0][...]
        lane = lax.broadcasted_iota(jnp.int32, (rows, load.shape[1] - cols), 1)
        extra = jnp.zeros(lane.shape, F32)
        for i, part in enumerate(two_parts(inv) + two_parts(pull)):
            extra = jnp.where(lane == i, part.astype(F32), extra)
        load[:, cols:] = extra.astype(BF)
    inner[...] = pull


def finish(mine, got, squares, d_kv, *inner):
    rows, cols = mine.shape
    return pl.pallas_call(
        finish_kernel,
        out_shape=[
            jax.ShapeDtypeStruct((rows, cols), BF),
            jax.ShapeDtypeStruct((rows, cols + LANES * len(inner)), BF),
            jax.ShapeDtypeStruct((rows, 1), F32),
        ],
        compiler_params=pltpu.CompilerParams(vmem_limit_bytes=VMEM_LIMIT),
        name="finish",
    )(mine, got, squares, d_kv, *inner)


def lower_kernel(table, order, at, ca0, ca1, cb0, cb1, gain, lifted, kva, kv_near, kv_far, *refs):
    blocks, (send, keep, nat, low) = refs[:-4], refs[-4:]
    core, group = at[3], at[4]
    feats, half = kva.shape[0], send.shape[1]
    cols = kva.shape[1] // 2
    near, far = both(core, half)
    mine, across = both(at[2] % 2, feats)
    block = blocks[0].shape[0]
    starts = column_starts(order, at, block)
    weight = weight_rows(blocks)
    part_cols = ca0.shape[1]
    piece = ca0.shape[0] // len(table) if table else 0
    for rows in chunks_of(ca0.shape[0]):
        extra = ca1[rows, part_cols:].astype(F32)
        extra_b = cb1[rows, part_cols:].astype(F32)
        inv = extra[:, 0:1] + extra[:, 1:2]
        inner = extra[:, 2:3] + extra[:, 3:4] + extra_b[:, 2:3] + extra_b[:, 3:4]
        pull = inv * inv * inv * inner * (1.0 / LLM_D)
        cot_a = lambda: jnp.concatenate([ca0[rows], ca1[rows, :part_cols]], axis=1)
        cot_b = lambda: jnp.concatenate([cb0[rows], cb1[rows, :part_cols]], axis=1)

        def put(span, weight_a, weight_b):
            d_normed = dot_nt(cot_a(), weight_a) + dot_nt(cot_b(), weight_b)
            scaled = inv * gain[:, span] * d_normed
            low[rows, span] = (scaled - lifted[rows, span].astype(F32) * pull).astype(BF)

        own_cols, other_cols = both(core, cols)
        put(mine, kva[:, own_cols], kva[:, other_cols])
        for place, pair in enumerate(((kv_near, kv_far), (kv_far, kv_near))):

            @pl.when(core ^ group == place)
            def _():
                put(across, pair[0][...], pair[1][...])

        d_tok = dot_nt(low[rows], weight).astype(BF)
        if not starts:
            nat[rows] = d_tok
        for i, start in enumerate(starts or ()):
            nat[rows, pl.ds(start, block)] = d_tok[:, i * block : (i + 1) * block]
    for source_row, owner_row in table:
        send[source_row : source_row + piece] = nat[owner_row : owner_row + piece, far]
        keep[source_row : source_row + piece] = nat[owner_row : owner_row + piece, near]
    if not table:
        send[...] = nat[:, far]
        keep[...] = nat[:, near]


def lower(table, order, at, cots, gain, lifted, kvs, blocks):
    rows, width = cots[0].shape[0], lifted.shape[1]
    tok_width = len(blocks) * blocks[0].shape[0]
    whole = pl.BlockSpec(memory_space=pltpu.VMEM)
    out = jax.ShapeDtypeStruct((rows, tok_width // 2), BF)
    return pl.pallas_call(
        functools.partial(lower_kernel, table, order),
        in_specs=[pl.BlockSpec(memory_space=pltpu.SMEM)] + [whole] * (9 + len(blocks)),
        out_specs=[whole] * 2,
        out_shape=[out] * 2,
        scratch_shapes=[pltpu.VMEM((rows, tok_width), BF), pltpu.VMEM((rows, width), BF)],
        compiler_params=pltpu.CompilerParams(vmem_limit_bytes=VMEM_LIMIT),
        name="lower",
    )(at, *cots, gain, lifted, *kvs, *blocks)


def on_device(frames, weight_qkv, weight_out, proj_in, norm_gain, proj_kv, shifts, route, d_kv):
    n = lax.axis_size("tm")
    me = lax.axis_index("tm")
    core = lax.axis_index("mp")
    rows, width = frames.shape
    half_w = width // 2
    shift = shifts[0]
    own_tok = rows // POOL
    tail_tok = WINDOW // POOL
    ext_tok = own_tok + tail_tok
    feats = proj_kv.shape[0]
    kv_half = proj_kv.shape[1] // 2
    piece = own_tok // n

    part = lax.dynamic_slice_in_dim(frames, core * (WINDOW // 2), WINDOW // 2, 0)
    mine = to_tm(part, -1, False)
    w_t = jnp.transpose(weight_qkv, (1, 2, 0)).reshape(-1, width)
    group = lax.axis_index("groups")
    two_groups = lax.axis_size("groups") == 2
    if not two_groups:
        group = group * 0
    proj_kv, part = lax.optimization_barrier((proj_kv, part))
    kv_near = swap_tm(lax.dynamic_slice_in_dim(proj_kv, group * kv_half, kv_half, 1), SPLIT)
    proj_in, w_t = lax.optimization_barrier((proj_in, w_t))

    masks = group_bits()
    order = offsets(masks)
    members = order + [k | SPLIT for k in order]
    count = n // 2
    blocks = []
    for k in order:
        pair = lax.dynamic_slice_in_dim(proj_in, (me ^ k) // 2 * 2 * feats, 2 * feats, 1)
        blocks.append(swap_tm(pair, k) if k else pair)
    across = [swap_tm(blocks[0], SPLIT)]

    other = swap_mp(mine)
    halo = jnp.where(
        core == 0, jnp.concatenate([mine, other], 0), jnp.concatenate([other, mine], 0)
    )
    x_roll = lax.dynamic_slice_in_dim(jnp.concatenate([frames, halo], 0), shift, rows, 0)

    at = jnp.stack([shift, rows * n - shift - me * rows, me, core, group]).astype(jnp.int32)
    normed, qkv, probs, pooled_attn, own_near, own_far, tail_near, tail_far = encoder_forward(
        x_roll, w_t, weight_out, at, ext_tok
    )
    own_far, kv_near, across, blocks[1:-1] = lax.optimization_barrier(
        (own_far, kv_near, across, blocks[1:-1])
    )
    across += [swap_tm(block, SPLIT) for block in blocks[1:-1]]
    swap_groups = lambda block: lax.ppermute(block, "groups", [(0, 1), (1, 0)])
    if two_groups:
        kv_far = swap_groups(kv_near)
    else:
        kv_far = swap_tm(proj_kv[:, kv_half:], SPLIT)
    turned = normed.T
    route, norm_gain, d_kv, pooled_attn = lax.optimization_barrier(
        (route, norm_gain, d_kv, pooled_attn)
    )
    gain = lax.dynamic_slice_in_dim(norm_gain, me // 2 * 2 * feats, 2 * feats, 0)
    gain = gain.reshape(1, -1)
    owner_at = (lax.dynamic_index_in_dim(route, me, 0, keepdims=False) ^ me)[None, :]
    sort = owner_at == jnp.array(members, jnp.int32)[:, None]
    sort = jnp.kron(sort.astype(BF), jnp.eye(piece, dtype=BF))
    source_at = jnp.arange(n, dtype=jnp.int32) ^ me
    spread = source_at[:, None] == jnp.array(
        [k | bit for k in order for bit in (0, SPLIT)], jnp.int32
    )
    spread = jnp.kron(spread.astype(BF), jnp.eye(piece, dtype=BF))
    d_kv = dot_tn(spread, d_kv).astype(BF)

    from_core = swap_mp(own_far)
    tail_a = to_tm(tail_near, 1, False)
    tail_b = to_tm(tail_far, 1, True)
    own_pool = (
        jnp.arange(rows, dtype=jnp.int32)[None, :] // POOL
        == jnp.arange(own_tok, dtype=jnp.int32)[:, None]
    ).astype(BF) * (1.0 / POOL)
    x_mean = dot(own_pool, lax.dynamic_slice_in_dim(frames, core * half_w, half_w, 1))
    pooled = x_mean + own_near + from_core.astype(F32)
    tail = tail_a.astype(F32) + tail_b.astype(F32)
    pooled = jnp.concatenate([pooled[:tail_tok] + tail, pooled[tail_tok:]], 0).astype(BF)

    sorted_tok = dot(sort, pooled).astype(BF).reshape(2, count * piece, half_w)
    handed = swap_tm(sorted_tok[1], SPLIT)
    handed, across, blocks[-1] = lax.optimization_barrier((handed, across, blocks[-1]))
    last_across = swap_tm(blocks[-1], SPLIT)
    pair_tok = jnp.stack([sorted_tok[0], handed])
    tok_half = gather_doubling(pair_tok, masks[-1:])
    tok_half, turned, d_kv, last_across = lax.optimization_barrier(
        (tok_half, turned, d_kv, last_across)
    )
    blocks += across + [last_across]
    at_rows = order
    if width // n % LANES:
        source = jnp.arange(n, dtype=jnp.int32) ^ me
        found = source[:, None] == jnp.array(members, jnp.int32)[None, :]
        place = jnp.sum(found * jnp.arange(n, dtype=jnp.int32)[None, :], axis=1)
        blocks = list(jnp.take(jnp.stack(blocks), place, axis=0))
        at_rows = None
    for mask in reversed(masks[:-1]):
        tok_half = jnp.concatenate([tok_half, swap_tm(tok_half, mask)], axis=0)
    tok_half, kv_far = lax.optimization_barrier((tok_half.reshape(-1, half_w), kv_far))
    kvs = (proj_kv, kv_near, kv_far)
    tok_other = swap_mp(tok_half)
    table = list(moves(order, piece))
    source_rows = np.concatenate([np.arange(r, r + piece) for r, _ in table])
    owner_rows = np.concatenate([np.arange(r, r + piece) for _, r in table])
    by_xla = piece % 16 != 0
    if by_xla:
        at_owner = source_rows[np.argsort(owner_rows)]
        tok_half, tok_other = tok_half[at_owner], tok_other[at_owner]
        table = []
    lifted, squares, scaled, kv_send = lift(
        table, at_rows, at, own_tok, tok_half, tok_other, gain, kvs, blocks
    )
    kv_got = swap_mp(kv_send)
    kv_keep = keep_columns(at, scaled, kvs)
    square_sum = scatter_halving(squares + swap_mp(squares), masks, F32)
    kv_part = (kv_keep.astype(F32) + kv_got.astype(F32)).astype(BF)
    kv_parts = jnp.split(kv_part.reshape(count, own_tok, kv_half), 2, axis=2)
    (mine_a, got_a), (mine_b, got_b) = scatter_last(kv_parts, masks)
    square_sum = square_sum.reshape(1, own_tok)
    d_kv_a, d_kv_b = jnp.split(d_kv, 2, axis=1)
    kv_a, load_a, inner = finish(mine_a, got_a, square_sum, d_kv_a)
    kv_b, load_b, _ = finish(mine_b, got_b, square_sum, d_kv_b, inner)
    kv = dot(spread, jnp.concatenate([kv_a, kv_b], axis=1)).astype(BF)
    loads = gather_parts([load_a, load_b], masks)
    loads = [load.reshape(count * own_tok, -1) for load in loads]
    cots = loads + [swap_mp(load) for load in loads]
    d_send, d_keep = lower(table, at_rows, at, cots, gain, lifted, kvs, blocks)
    if by_xla:
        at_source = owner_rows[np.argsort(source_rows)]
        d_send, d_keep = d_send[at_source], d_keep[at_source]
    d_part = d_keep.astype(F32) + swap_mp(d_send).astype(F32)
    d_pair = scatter_halving(d_part.reshape(count, 2, count * piece, half_w), masks, BF)
    d_sorted = jnp.concatenate([d_pair[0].astype(BF), swap_tm(d_pair[1].astype(BF), SPLIT)], 0)
    d_half = dot_tn(sort, d_sorted).astype(BF)

    d_other = swap_mp(d_half)
    next_a = to_tm(d_half[:tail_tok], -1, False)
    next_b = to_tm(d_half[:tail_tok], -1, True)
    left = jnp.concatenate([d_half, next_a], 0)
    right = jnp.concatenate([d_other, next_b], 0)
    d_ext = jnp.where(
        core == 0, jnp.concatenate([left, right], 1), jnp.concatenate([right, left], 1)
    )
    bits = tm_bits()
    crossed = [bits[1], bits[0]] + bits[2:]
    d_attn, out_even, out_odd = out_grad(d_ext, weight_out, pooled_attn, at, bits)
    chunks = []
    for pair, path in enumerate((bits, bits, bits, crossed)):
        even, odd = encoder_backward(turned, qkv, probs, d_attn, at, path, pair, 1)
        even, odd, at = lax.optimization_barrier((even, odd, at))
        chunks.append((even, odd, path))
    chunks.append((out_even, out_odd, bits))
    steps = list(range(len(chunks))) * len(bits)
    if len(bits) == 3:
        steps = [0, 0, 1, 3, 0, 1, 4, 2, 1, 4, 3, 2, 4, 3, 2]
    chunks = scatter_chunks(chunks, steps, even)
    grad_out = chunks.pop()
    grad_qkv = jnp.transpose(jnp.concatenate(chunks, axis=-1), (1, 0, 2))
    return kv, grad_qkv, grad_out


def solution(mesh):
    in_specs = (
        P(("groups", "tm"), None),
        P(None, None, "mp"),
        P("mp", None),
        P("tm", "mp"),
        P("mp"),
        P(("mp", "tm"), None),
        P(),
        P(),
        P(("groups", "tm"), "mp"),
    )
    out_specs = (
        P(("groups", "tm"), "mp"),
        P(("groups", "tm"), None, "mp"),
        P(("groups", "mp", "tm"), None),
    )
    return jax.shard_map(
        on_device, mesh=mesh, in_specs=in_specs, out_specs=out_specs, check_vma=False
    )
```

```python
import functools

import jax
import jax.numpy as jnp
import numpy as np
from jax import lax
from jax.experimental import pallas as pl
from jax.experimental.pallas import tpu as pltpu
from jax.sharding import PartitionSpec as P

HEAD = 64
WINDOW = 256
POOL = 4
LLM_D = 8192
BF = jnp.bfloat16
F32 = jnp.float32
VMEM_LIMIT = 48 << 20
SPLIT = 1
CHUNK = 512
LANES = 128


def dot(a, b):
    return jnp.dot(a, b, preferred_element_type=F32)


def dot_nt(a, b):
    return lax.dot_general(a, b, (((1,), (1,)), ((), ())), preferred_element_type=F32)


def dot_tn(a, b):
    return lax.dot_general(a, b, (((0,), (0,)), ((), ())), preferred_element_type=F32)


def swap_tm(block, mask):
    n = lax.axis_size("tm")
    return lax.ppermute(block, "tm", [(i, i ^ mask) for i in range(n)])


def swap_mp(block):
    n = lax.axis_size("mp")
    return lax.ppermute(block, "mp", [(i, n - 1 - i) for i in range(n)])


def to_tm(block, step, cross):
    n, m = lax.axis_size("tm"), lax.axis_size("mp")
    pairs = []
    for i in range(n):
        for c in range(m):
            pairs.append((i * m + c, (i + step) % n * m + (m - 1 - c if cross else c)))
    return lax.ppermute(block, ("tm", "mp"), pairs)


def offsets(masks):
    order = [0]
    for mask in reversed(masks):
        order = order + [k | mask for k in order]
    return order


def tm_bits():
    n = lax.axis_size("tm")
    return [1 << i for i in range(n.bit_length() - 1)]


def group_bits():
    return [bit for bit in tm_bits() if bit != SPLIT]


def gather_doubling(block, masks):
    block = block[None]
    for mask in reversed(masks):
        block = jnp.concatenate([block, swap_tm(block, mask)], axis=0)
    return block


def scatter_halving(blocks, masks, kind):
    total = blocks
    for mask in masks:
        low = total.astype(kind)
        half = low.shape[0] // 2
        total = low[:half].astype(F32) + swap_tm(low[half:], mask).astype(F32)
    return total[0]


def in_turn(got, last):
    return got if last is None else lax.optimization_barrier((got, last))[0]


def scatter_last(parts, masks):
    lows, pairs, last = list(parts), [], None
    for mask in masks:
        for i, low in enumerate(lows):
            half = low.shape[0] // 2
            got = in_turn(swap_tm(low[half:], mask), last)
            if mask == masks[-1]:
                pairs.append((low[0], got[0]))
                last = got
                continue
            lows[i] = last = (low[:half].astype(F32) + got.astype(F32)).astype(BF)
    return pairs


def gather_parts(parts, masks):
    parts, last = [part[None] for part in parts], None
    for mask in reversed(masks):
        for i, part in enumerate(parts):
            got = in_turn(swap_tm(part, mask), last)
            parts[i] = last = jnp.concatenate([part, got], axis=0)
    return parts


def scatter_chunks(chunks, steps, last):
    sums = [lower for lower, _, _ in chunks]
    sends = [upper for _, upper, _ in chunks]
    stage = [0] * len(chunks)
    for i in steps:
        got = in_turn(swap_tm(sends[i], chunks[i][2][stage[i]]), last)
        stage[i] += 1
        total = sums[i].astype(F32) + got.astype(F32)
        if total.shape[0] == 1:
            sums[i] = total[0]
            continue
        low = last = total.astype(BF)
        half = low.shape[0] // 2
        sums[i], sends[i] = low[:half], low[half:]
    return sums


def head_mask(shape, head):
    return lax.broadcasted_iota(jnp.int32, shape, 1) // HEAD == head


def forward_kernel(at, x_ref, wq_ref, wk_ref, wv_ref, wo_ref, *refs):
    normed, qkv, probs, pooled, own_near, own_far, tail_near, tail_far, attn, out = refs
    shift, border, core = at[0], at[1], at[3]
    rows = x_ref.shape[0]
    cols = wq_ref.shape[0]

    @pl.when(pl.program_id(0) == 0)
    def _():
        x = x_ref[...].astype(F32)
        scale = lax.rsqrt(jnp.mean(x * x, axis=-1, keepdims=True) + 1e-05)
        normed[...] = (x * scale).astype(BF)
        out[...] = jnp.zeros_like(out)

    base = normed[...]
    for i, w_ref in enumerate((wq_ref, wk_ref, wv_ref)):
        qkv[i] = dot_nt(base, w_ref[...]).astype(BF)
    windows, heads = range(rows // WINDOW), range(cols // HEAD)
    spans = [pl.ds(w * WINDOW, WINDOW) for w in windows]
    own = [head_mask((WINDOW, cols), h) for h in heads]
    scores = []
    for w in windows:
        q, k = qkv[0, spans[w], :], qkv[1, spans[w], :]
        for h in heads:
            scores.append(dot_nt(jnp.where(own[h], k, jnp.zeros_like(k)), q))
    square = (WINDOW, WINDOW)
    key_at = lax.broadcasted_iota(jnp.int32, square, 0)
    query_at = lax.broadcasted_iota(jnp.int32, square, 1)
    lows = []
    for w in windows:
        edge = border - w * WINDOW
        allowed = (key_at >= edge) == (query_at >= edge)
        for h in heads:
            score = jnp.where(allowed, scores[w * len(heads) + h] * HEAD ** (-0.5), -1e30)
            terms = jnp.exp(score - jnp.max(score, axis=0, keepdims=True))
            low = (terms * (1.0 / jnp.sum(terms, axis=0, keepdims=True))).astype(BF)
            probs[0, w, h] = low
            lows.append(low)
    for w in windows:
        v = qkv[2, spans[w], :]
        attended = None
        for h in heads:
            part = dot_tn(lows[w * len(heads) + h], v)
            attended = part if attended is None else jnp.where(own[h], part, attended)
        attn[spans[w], :] = attended.astype(BF)
    tok_shape = (pooled.shape[0], rows)
    tok_of = (lax.broadcasted_iota(jnp.int32, tok_shape, 1) + shift) // POOL
    member = tok_of == lax.broadcasted_iota(jnp.int32, tok_shape, 0)
    pool = jnp.where(member, 1.0 / POOL, 0.0).astype(BF)
    low = dot(pool, attn[...]).astype(BF)
    pooled[...] = low
    out[...] += dot(low, wo_ref[...])

    @pl.when(pl.program_id(0) == pl.num_programs(0) - 1)
    def _():
        count, half = own_near.shape
        near = pl.ds(pl.multiple_of(core * half, half), half)
        far = pl.ds(pl.multiple_of((1 - core) * half, half), half)
        own_near[...] = out[:count, near]
        own_far[...] = out[:count, far].astype(BF)
        tail_near[...] = out[count:, near].astype(BF)
        tail_far[...] = out[count:, far].astype(BF)


def encoder_forward(x_roll, w_t, weight_out, at, ext_tok):
    rows, width = x_roll.shape
    heads_w = weight_out.shape[0]
    cols = 2 * HEAD
    pairs = heads_w // cols
    windows = rows // WINDOW
    weight = lambda i: pl.BlockSpec((cols, width), lambda p, at: (i * pairs + p, 0))
    own_tok = rows // POOL
    piece = lambda count: pl.BlockSpec((count, width // 2), lambda p, at: (0, 0))
    return pl.pallas_call(
        forward_kernel,
        grid_spec=pltpu.PrefetchScalarGridSpec(
            num_scalar_prefetch=1,
            grid=(pairs,),
            in_specs=[
                pl.BlockSpec((rows, width), lambda p, at: (0, 0)),
                weight(0),
                weight(1),
                weight(2),
                weight(0),
            ],
            out_specs=[
                pl.BlockSpec((rows, width), lambda p, at: (0, 0)),
                pl.BlockSpec((3, rows, cols), lambda p, at: (0, 0, p)),
                pl.BlockSpec((1, windows, 2, WINDOW, WINDOW), lambda p, at: (p, 0, 0, 0, 0)),
                pl.BlockSpec((ext_tok, cols), lambda p, at: (0, p)),
                piece(own_tok),
                piece(own_tok),
                piece(ext_tok - own_tok),
                piece(ext_tok - own_tok),
            ],
            scratch_shapes=[pltpu.VMEM((rows, cols), BF), pltpu.VMEM((ext_tok, width), F32)],
        ),
        out_shape=[
            pltpu.HBM((rows, width), BF),
            pltpu.HBM((3, rows, heads_w), BF),
            pltpu.HBM((pairs, windows, 2, WINDOW, WINDOW), BF),
            pltpu.HBM((ext_tok, heads_w), BF),
            jax.ShapeDtypeStruct((own_tok, width // 2), F32),
            jax.ShapeDtypeStruct((own_tok, width // 2), BF),
            jax.ShapeDtypeStruct((ext_tok - own_tok, width // 2), BF),
            jax.ShapeDtypeStruct((ext_tok - own_tok, width // 2), BF),
        ],
        compiler_params=pltpu.CompilerParams(vmem_limit_bytes=VMEM_LIMIT),
        name="encoder_forward",
    )(at, x_roll, w_t, w_t, w_t, weight_out)


def out_grad_kernel(masks, at, d_ref, wo_ref, pa_ref, d_attn, even, odd, turned):
    me = at[2]
    block = even.shape[1]
    d_ext = d_ref[...]
    d_attn[...] = (dot_nt(d_ext, wo_ref[...]) * (1.0 / POOL)).astype(BF)
    turned[...] = pa_ref[...].T
    for bit, ref in ((0, even), (masks[0], odd)):
        for j, k in enumerate(offsets(masks[1:])):
            start = pl.multiple_of((me ^ (k | bit)) * block, block)
            ref[j] = dot(turned[pl.ds(start, block), :], d_ext).astype(BF)


def out_grad(d_ext, weight_out, pooled_attn, at, masks):
    heads_w, width = weight_out.shape
    n = 2 ** len(masks)
    blocks = jax.ShapeDtypeStruct((n // 2, heads_w // n, width), BF)
    whole = pl.BlockSpec(memory_space=pltpu.VMEM)
    return pl.pallas_call(
        functools.partial(out_grad_kernel, masks),
        in_specs=[pl.BlockSpec(memory_space=pltpu.SMEM), whole, whole, whole],
        out_specs=[whole] * 3,
        out_shape=[jax.ShapeDtypeStruct(pooled_attn.shape, BF), blocks, blocks],
        scratch_shapes=[pltpu.VMEM((heads_w, pooled_attn.shape[0]), BF)],
        compiler_params=pltpu.CompilerParams(vmem_limit_bytes=VMEM_LIMIT),
        name="out_grad",
    )(at, d_ext, weight_out, pooled_attn)


def backward_kernel(masks, at, turned, qkv, probs, d_ref, even, odd, grads):
    shift, me = at[0], at[2]
    rows = turned.shape[1]
    cols = d_ref.shape[1]
    block = even.shape[2]
    tok_shape = (rows, d_ref.shape[0])
    tok_of = (lax.broadcasted_iota(jnp.int32, tok_shape, 0) + shift) // POOL
    member = tok_of == lax.broadcasted_iota(jnp.int32, tok_shape, 1)
    d_rows = dot(jnp.where(member, 1.0, 0.0).astype(BF), d_ref[...]).astype(BF)
    for w in range(rows // WINDOW):
        span = pl.ds(w * WINDOW, WINDOW)
        q, k, v = qkv[0, span, :], qkv[1, span, :], qkv[2, span, :]
        d_out = d_rows[w * WINDOW : (w + 1) * WINDOW]
        none = jnp.zeros_like(q)
        sums = [0.0, 0.0, 0.0]
        for h in range(cols // HEAD):
            own = head_mask(q.shape, h)
            low = probs[0, w, h]
            weight = low.astype(F32)
            d_weight = dot_nt(jnp.where(own, v, none), d_out)
            centre = jnp.sum(weight * d_weight, axis=0, keepdims=True)
            d_score = (weight * (d_weight - centre) * HEAD ** (-0.5)).astype(BF)
            sums[0] += dot_tn(d_score, jnp.where(own, k, none))
            sums[1] += dot(d_score, jnp.where(own, q, none))
            sums[2] += dot(low, jnp.where(own, d_out, none))
        for i in range(3):
            grads[span, i * cols : (i + 1) * cols] = sums[i].astype(BF)
    d_all = grads[...]
    for bit, ref in ((0, even), (masks[0], odd)):
        for j, k in enumerate(offsets(masks[1:])):
            start = pl.multiple_of((me ^ (k | bit)) * block, block)
            term = dot(turned[pl.ds(start, block), :], d_all).astype(BF)
            for i in range(3):
                ref[j, i] = term[:, i * cols : (i + 1) * cols]


def encoder_backward(turned, qkv, probs, d_attn, at, masks, first, count):
    width, rows = turned.shape
    n = 2 ** len(masks)
    cols = 2 * HEAD
    windows = rows // WINDOW
    block = width // n
    out = pl.BlockSpec((n // 2, 3, block, cols), lambda p, at: (0, 0, 0, p))
    shape = jax.ShapeDtypeStruct((n // 2, 3, block, cols * count), BF)
    return pl.pallas_call(
        functools.partial(backward_kernel, masks),
        grid_spec=pltpu.PrefetchScalarGridSpec(
            num_scalar_prefetch=1,
            grid=(count,),
            in_specs=[
                pl.BlockSpec((width, rows), lambda p, at: (0, 0)),
                pl.BlockSpec((3, rows, cols), lambda p, at: (0, 0, p + first)),
                pl.BlockSpec(
                    (1, windows, 2, WINDOW, WINDOW), lambda p, at: (p + first, 0, 0, 0, 0)
                ),
                pl.BlockSpec((d_attn.shape[0], cols), lambda p, at: (0, p + first)),
            ],
            out_specs=[out, out],
            scratch_shapes=[pltpu.VMEM((rows, 3 * cols), BF)],
        ),
        out_shape=[shape, shape],
        compiler_params=pltpu.CompilerParams(vmem_limit_bytes=VMEM_LIMIT),
        name="encoder_backward",
    )(at, turned, qkv, probs, d_attn)


def moves(order, piece):
    count = len(order)
    for e, offset in enumerate(order):
        for b in range(2):
            for i, step in enumerate(order):
                owner = order.index(offset ^ step)
                source_row = ((e * 2 + b) * count + i) * piece
                owner_row = ((owner * count + i) * 2 + b) * piece
                yield source_row, owner_row


def chunks_of(rows):
    return [slice(r, min(r + CHUNK, rows)) for r in range(0, rows, CHUNK)]


def column_starts(order, at, block):
    if order is None:
        return None
    offset = [k | bit for bit in (0, SPLIT) for k in order]
    return [pl.multiple_of((at[2] ^ k) * block, block) for k in offset]


def weight_rows(blocks):
    return jnp.concatenate([b[...].reshape(-1, b.shape[-1]) for b in blocks], axis=0)


def both(index, size):
    return (
        pl.ds(pl.multiple_of(index * size, size), size),
        pl.ds(pl.multiple_of((1 - index) * size, size), size),
    )


def kv_columns(low, at, kva, near, far, side, rows, out):
    feats, cols = kva.shape[0], near.shape[1]
    mine, across = both(at[2] % 2, feats)
    span = pl.ds(pl.multiple_of(side * cols, cols), cols)
    for place, part in enumerate((near, far)):

        @pl.when(side ^ at[4] == place)
        def _():
            total = dot(low[rows, mine], kva[:, span]) + dot(low[rows, across], part[...])
            out[rows] = total.astype(BF)


def lift_kernel(table, order, at, ta, tb, gain, kva, kv_near, kv_far, *refs):
    blocks, (lifted, squares, low, send, tok) = refs[:-5], refs[-5:]
    core = at[3]
    near, far = both(core, ta.shape[1])
    piece = ta.shape[0] // len(table) if table else 0
    for source_row, owner_row in table:
        tok[owner_row : owner_row + piece, near] = ta[source_row : source_row + piece]
        tok[owner_row : owner_row + piece, far] = tb[source_row : source_row + piece]
    if not table:
        tok[:, near] = ta[...]
        tok[:, far] = tb[...]
    block = blocks[0].shape[0]
    starts = column_starts(order, at, block)
    weight = weight_rows(blocks)
    group_rows = squares.shape[1]
    for rows in chunks_of(tok.shape[0]):
        x = tok[rows]
        if starts:
            x = jnp.concatenate([tok[rows, pl.ds(start, block)] for start in starts], axis=1)
        product = dot(x, weight)
        lifted[rows] = product.astype(BF)
        low[rows] = (product * gain[...]).astype(BF)
        sums = jnp.sum(product * product, axis=1, keepdims=True)
        for first in range(0, rows.stop - rows.start, group_rows):
            column = sums[first : first + group_rows]
            owner = (rows.start + first) // group_rows
            squares[owner : owner + 1] = jnp.broadcast_to(column, (group_rows,) * 2).T[:1]
        kv_columns(low, at, kva, kv_near, kv_far, 1 - core, rows, send)


def lift(table, order, at, own_tok, ta, tb, gain, kvs, blocks):
    rows, half = ta.shape
    feats, cols = kvs[0].shape[0], kvs[0].shape[1] // 2
    whole = pl.BlockSpec(memory_space=pltpu.VMEM)
    return pl.pallas_call(
        functools.partial(lift_kernel, table, order),
        in_specs=[pl.BlockSpec(memory_space=pltpu.SMEM)] + [whole] * (6 + len(blocks)),
        out_specs=[whole] * 4,
        out_shape=[
            jax.ShapeDtypeStruct((rows, 2 * feats), BF),
            jax.ShapeDtypeStruct((rows // own_tok, own_tok), F32),
            jax.ShapeDtypeStruct((rows, 2 * feats), BF),
            jax.ShapeDtypeStruct((rows, cols), BF),
        ],
        scratch_shapes=[pltpu.VMEM((rows, 2 * half), BF)],
        compiler_params=pltpu.CompilerParams(vmem_limit_bytes=VMEM_LIMIT),
        name="lift",
    )(at, ta, tb, gain, *kvs, *blocks)


def keep_kernel(at, low, kva, kv_near, kv_far, keep):
    for rows in chunks_of(low.shape[0]):
        kv_columns(low, at, kva, kv_near, kv_far, at[3], rows, keep)


def keep_columns(at, low, kvs):
    whole = pl.BlockSpec(memory_space=pltpu.VMEM)
    return pl.pallas_call(
        keep_kernel,
        in_specs=[pl.BlockSpec(memory_space=pltpu.SMEM)] + [whole] * 4,
        out_specs=whole,
        out_shape=jax.ShapeDtypeStruct((low.shape[0], kvs[0].shape[1] // 2), BF),
        compiler_params=pltpu.CompilerParams(vmem_limit_bytes=VMEM_LIMIT),
        name="keep_columns",
    )(at, low, *kvs)


def two_parts(column):
    high = column.astype(BF)
    return high, (column - high.astype(F32)).astype(BF)


def finish_kernel(mine, got, squares, d_kv, *refs):
    rows, cols = mine.shape
    kv, load, inner = refs[-3:]
    total = mine[...].astype(F32) + got[...].astype(F32)
    mean = jnp.broadcast_to(squares[...], (rows, rows)).T[:, :1] * (1.0 / LLM_D)
    inv = lax.rsqrt(mean + 1e-05)
    low = (total * inv).astype(BF)
    kv[...] = low
    cot = (low.astype(F32) + d_kv[...].astype(F32)).astype(BF)
    load[:, :cols] = cot
    pull = jnp.sum(cot.astype(F32) * total, axis=1, keepdims=True)
    if len(refs) == 4:
        pull += refs[0][...]
        lane = lax.broadcasted_iota(jnp.int32, (rows, load.shape[1] - cols), 1)
        extra = jnp.zeros(lane.shape, F32)
        for i, part in enumerate(two_parts(inv) + two_parts(pull)):
            extra = jnp.where(lane == i, part.astype(F32), extra)
        load[:, cols:] = extra.astype(BF)
    inner[...] = pull


def finish(mine, got, squares, d_kv, *inner):
    rows, cols = mine.shape
    return pl.pallas_call(
        finish_kernel,
        out_shape=[
            jax.ShapeDtypeStruct((rows, cols), BF),
            jax.ShapeDtypeStruct((rows, cols + LANES * len(inner)), BF),
            jax.ShapeDtypeStruct((rows, 1), F32),
        ],
        compiler_params=pltpu.CompilerParams(vmem_limit_bytes=VMEM_LIMIT),
        name="finish",
    )(mine, got, squares, d_kv, *inner)


def lower_kernel(table, order, at, ca0, ca1, cb0, cb1, gain, lifted, kva, kv_near, kv_far, *refs):
    blocks, (send, keep, nat, low) = refs[:-4], refs[-4:]
    core, group = at[3], at[4]
    feats, half = kva.shape[0], send.shape[1]
    cols = kva.shape[1] // 2
    near, far = both(core, half)
    mine, across = both(at[2] % 2, feats)
    block = blocks[0].shape[0]
    starts = column_starts(order, at, block)
    weight = weight_rows(blocks)
    part_cols = ca0.shape[1]
    piece = ca0.shape[0] // len(table) if table else 0
    for rows in chunks_of(ca0.shape[0]):
        extra = ca1[rows, part_cols:].astype(F32)
        extra_b = cb1[rows, part_cols:].astype(F32)
        inv = extra[:, 0:1] + extra[:, 1:2]
        inner = extra[:, 2:3] + extra[:, 3:4] + extra_b[:, 2:3] + extra_b[:, 3:4]
        pull = inv * inv * inv * inner * (1.0 / LLM_D)
        cot_a = lambda: jnp.concatenate([ca0[rows], ca1[rows, :part_cols]], axis=1)
        cot_b = lambda: jnp.concatenate([cb0[rows], cb1[rows, :part_cols]], axis=1)

        def put(span, weight_a, weight_b):
            d_normed = dot_nt(cot_a(), weight_a) + dot_nt(cot_b(), weight_b)
            scaled = inv * gain[:, span] * d_normed
            low[rows, span] = (scaled - lifted[rows, span].astype(F32) * pull).astype(BF)

        own_cols, other_cols = both(core, cols)
        put(mine, kva[:, own_cols], kva[:, other_cols])
        for place, pair in enumerate(((kv_near, kv_far), (kv_far, kv_near))):

            @pl.when(core ^ group == place)
            def _():
                put(across, pair[0][...], pair[1][...])

        d_tok = dot_nt(low[rows], weight).astype(BF)
        if not starts:
            nat[rows] = d_tok
        for i, start in enumerate(starts or ()):
            nat[rows, pl.ds(start, block)] = d_tok[:, i * block : (i + 1) * block]
    for source_row, owner_row in table:
        send[source_row : source_row + piece] = nat[owner_row : owner_row + piece, far]
        keep[source_row : source_row + piece] = nat[owner_row : owner_row + piece, near]
    if not table:
        send[...] = nat[:, far]
        keep[...] = nat[:, near]


def lower(table, order, at, cots, gain, lifted, kvs, blocks):
    rows, width = cots[0].shape[0], lifted.shape[1]
    tok_width = sum(block.size for block in blocks) // width
    whole = pl.BlockSpec(memory_space=pltpu.VMEM)
    out = jax.ShapeDtypeStruct((rows, tok_width // 2), BF)
    return pl.pallas_call(
        functools.partial(lower_kernel, table, order),
        in_specs=[pl.BlockSpec(memory_space=pltpu.SMEM)] + [whole] * (9 + len(blocks)),
        out_specs=[whole] * 2,
        out_shape=[out] * 2,
        scratch_shapes=[pltpu.VMEM((rows, tok_width), BF), pltpu.VMEM((rows, width), BF)],
        compiler_params=pltpu.CompilerParams(vmem_limit_bytes=VMEM_LIMIT),
        name="lower",
    )(at, *cots, gain, lifted, *kvs, *blocks)


def on_device(frames, weight_qkv, weight_out, proj_in, norm_gain, proj_kv, shifts, route, d_kv):
    n = lax.axis_size("tm")
    me = lax.axis_index("tm")
    core = lax.axis_index("mp")
    rows, width = frames.shape
    half_w = width // 2
    shift = shifts[0]
    own_tok = rows // POOL
    tail_tok = WINDOW // POOL
    ext_tok = own_tok + tail_tok
    feats = proj_kv.shape[0]
    kv_half = proj_kv.shape[1] // 2
    piece = own_tok // n

    part = lax.dynamic_slice_in_dim(frames, core * (WINDOW // 2), WINDOW // 2, 0)
    mine = to_tm(part, -1, False)
    w_t = jnp.transpose(weight_qkv, (1, 2, 0)).reshape(-1, width)
    group = lax.axis_index("groups")
    two_groups = lax.axis_size("groups") == 2
    if not two_groups:
        group = group * 0
    proj_kv, part = lax.optimization_barrier((proj_kv, part))
    kv_near = swap_tm(lax.dynamic_slice_in_dim(proj_kv, group * kv_half, kv_half, 1), SPLIT)
    proj_in, w_t = lax.optimization_barrier((proj_in, w_t))

    masks = group_bits()
    order = offsets(masks)
    members = order + [k | SPLIT for k in order]
    count = n // 2
    blocks = []
    for k in order:
        pair = lax.dynamic_slice_in_dim(proj_in, (me ^ k) // 2 * 2 * feats, 2 * feats, 1)
        blocks.append(swap_tm(pair, k) if k else pair)

    other = swap_mp(mine)
    halo = jnp.where(
        core == 0, jnp.concatenate([mine, other], 0), jnp.concatenate([other, mine], 0)
    )
    x_roll = lax.dynamic_slice_in_dim(jnp.concatenate([frames, halo], 0), shift, rows, 0)

    at = jnp.stack([shift, rows * n - shift - me * rows, me, core, group]).astype(jnp.int32)
    normed, qkv, probs, pooled_attn, own_near, own_far, tail_near, tail_far = encoder_forward(
        x_roll, w_t, weight_out, at, ext_tok
    )
    own_far, kv_near, blocks[0] = lax.optimization_barrier((own_far, kv_near, blocks[0]))
    across = [swap_tm(blocks[0], SPLIT)]
    swap_groups = lambda block: lax.ppermute(block, "groups", [(0, 1), (1, 0)])
    if two_groups:
        kv_far = swap_groups(kv_near)
    else:
        kv_far = swap_tm(proj_kv[:, kv_half:], SPLIT)
    turned = normed.T
    route, norm_gain, d_kv, pooled_attn = lax.optimization_barrier(
        (route, norm_gain, d_kv, pooled_attn)
    )
    gain = lax.dynamic_slice_in_dim(norm_gain, me // 2 * 2 * feats, 2 * feats, 0)
    gain = gain.reshape(1, -1)
    owner_at = (lax.dynamic_index_in_dim(route, me, 0, keepdims=False) ^ me)[None, :]
    sort = owner_at == jnp.array(members, jnp.int32)[:, None]
    sort = jnp.kron(sort.astype(BF), jnp.eye(piece, dtype=BF))
    source_at = jnp.arange(n, dtype=jnp.int32) ^ me
    spread = source_at[:, None] == jnp.array(
        [k | bit for k in order for bit in (0, SPLIT)], jnp.int32
    )
    spread = jnp.kron(spread.astype(BF), jnp.eye(piece, dtype=BF))
    d_kv = dot_tn(spread, d_kv).astype(BF)

    from_core = swap_mp(own_far)
    tail_a = to_tm(tail_near, 1, False)
    tail_b = to_tm(tail_far, 1, True)
    own_pool = (
        jnp.arange(rows, dtype=jnp.int32)[None, :] // POOL
        == jnp.arange(own_tok, dtype=jnp.int32)[:, None]
    ).astype(BF) * (1.0 / POOL)
    x_mean = dot(own_pool, lax.dynamic_slice_in_dim(frames, core * half_w, half_w, 1))
    pooled = x_mean + own_near + from_core.astype(F32)
    tail = tail_a.astype(F32) + tail_b.astype(F32)
    pooled = jnp.concatenate([pooled[:tail_tok] + tail, pooled[tail_tok:]], 0).astype(BF)

    sorted_tok = dot(sort, pooled).astype(BF).reshape(2, count * piece, half_w)
    handed = swap_tm(sorted_tok[1], SPLIT)
    handed, across, blocks[1:] = lax.optimization_barrier((handed, across, blocks[1:]))
    across.append(swap_tm(jnp.stack(blocks[1:]), SPLIT))
    pair_tok = jnp.stack([sorted_tok[0], handed])
    tok_half = gather_doubling(pair_tok, masks[-1:])
    tok_half, turned, d_kv = lax.optimization_barrier((tok_half, turned, d_kv))
    for mask in reversed(masks[:-1]):
        tok_half = jnp.concatenate([tok_half, swap_tm(tok_half, mask)], axis=0)
    tok_half, kv_far = lax.optimization_barrier((tok_half.reshape(-1, half_w), kv_far))
    kvs = (proj_kv, kv_near, kv_far)
    tok_other = swap_mp(tok_half)
    blocks += across
    at_rows = order
    if width // n % LANES:
        source = jnp.arange(n, dtype=jnp.int32) ^ me
        found = source[:, None] == jnp.array(members, jnp.int32)[None, :]
        place = jnp.sum(found * jnp.arange(n, dtype=jnp.int32)[None, :], axis=1)
        stacked = jnp.concatenate([b.reshape((-1,) + blocks[0].shape) for b in blocks])
        blocks = list(jnp.take(stacked, place, axis=0))
        at_rows = None
    table = list(moves(order, piece))
    source_rows = np.concatenate([np.arange(r, r + piece) for r, _ in table])
    owner_rows = np.concatenate([np.arange(r, r + piece) for _, r in table])
    by_xla = piece % 16 != 0
    if by_xla:
        at_owner = source_rows[np.argsort(owner_rows)]
        tok_half, tok_other = tok_half[at_owner], tok_other[at_owner]
        table = []
    lifted, squares, scaled, kv_send = lift(
        table, at_rows, at, own_tok, tok_half, tok_other, gain, kvs, blocks
    )
    kv_got = swap_mp(kv_send)
    kv_keep = keep_columns(at, scaled, kvs)
    square_sum = scatter_halving(squares + swap_mp(squares), masks, F32)
    kv_part = (kv_keep.astype(F32) + kv_got.astype(F32)).astype(BF)
    kv_parts = jnp.split(kv_part.reshape(count, own_tok, kv_half), 2, axis=2)
    (mine_a, got_a), (mine_b, got_b) = scatter_last(kv_parts, masks)
    square_sum = square_sum.reshape(1, own_tok)
    d_kv_a, d_kv_b = jnp.split(d_kv, 2, axis=1)
    kv_a, load_a, inner = finish(mine_a, got_a, square_sum, d_kv_a)
    kv_b, load_b, _ = finish(mine_b, got_b, square_sum, d_kv_b, inner)
    kv = dot(spread, jnp.concatenate([kv_a, kv_b], axis=1)).astype(BF)
    loads = gather_parts([load_a, load_b], masks)
    loads = [load.reshape(count * own_tok, -1) for load in loads]
    cots = loads + [swap_mp(load) for load in loads]
    d_send, d_keep = lower(table, at_rows, at, cots, gain, lifted, kvs, blocks)
    if by_xla:
        at_source = owner_rows[np.argsort(source_rows)]
        d_send, d_keep = d_send[at_source], d_keep[at_source]
    d_part = d_keep.astype(F32) + swap_mp(d_send).astype(F32)
    d_pair = scatter_halving(d_part.reshape(count, 2, count * piece, half_w), masks, BF)
    d_sorted = jnp.concatenate([d_pair[0].astype(BF), swap_tm(d_pair[1].astype(BF), SPLIT)], 0)
    d_half = dot_tn(sort, d_sorted).astype(BF)

    d_other = swap_mp(d_half)
    next_a = to_tm(d_half[:tail_tok], -1, False)
    next_b = to_tm(d_half[:tail_tok], -1, True)
    left = jnp.concatenate([d_half, next_a], 0)
    right = jnp.concatenate([d_other, next_b], 0)
    d_ext = jnp.where(
        core == 0, jnp.concatenate([left, right], 1), jnp.concatenate([right, left], 1)
    )
    bits = tm_bits()
    crossed = [bits[1], bits[0]] + bits[2:]
    d_attn, out_even, out_odd = out_grad(d_ext, weight_out, pooled_attn, at, bits)
    chunks = []
    out_got = swap_tm(out_odd, bits[0])
    for pair, path in enumerate((bits, bits, bits, crossed)):
        if pair == 3:
            at, out_got = lax.optimization_barrier((at, out_got))
        even, odd = encoder_backward(turned, qkv, probs, d_attn, at, path, pair, 1)
        even, odd, at = lax.optimization_barrier((even, odd, at))
        chunks.append((even, odd, path))
    out_low = (out_even.astype(F32) + out_got.astype(F32)).astype(BF)
    out_half = out_low.shape[0] // 2
    chunks.append((out_low[:out_half], out_low[out_half:], bits[1:]))
    steps = [i for t in range(len(bits)) for i, c in enumerate(chunks) if t < len(c[2])]
    if len(bits) == 3:
        steps = [0, 4, 3, 1, 0, 4, 0, 2, 1, 1, 3, 2, 3, 2]
    chunks = scatter_chunks(chunks, steps, even)
    grad_out = chunks.pop()
    grad_qkv = jnp.transpose(jnp.concatenate(chunks, axis=-1), (1, 0, 2))
    return kv, grad_qkv, grad_out


def solution(mesh):
    in_specs = (
        P(("groups", "tm"), None),
        P(None, None, "mp"),
        P("mp", None),
        P("tm", "mp"),
        P("mp"),
        P(("mp", "tm"), None),
        P(),
        P(),
        P(("groups", "tm"), "mp"),
    )
    out_specs = (
        P(("groups", "tm"), "mp"),
        P(("groups", "tm"), None, "mp"),
        P(("groups", "mp", "tm"), None),
    )
    return jax.shard_map(
        on_device, mesh=mesh, in_specs=in_specs, out_specs=out_specs, check_vma=False
    )
```

```python
import functools

import jax
import jax.numpy as jnp
import numpy as np
from jax import lax
from jax.experimental import pallas as pl
from jax.experimental.pallas import tpu as pltpu
from jax.sharding import PartitionSpec as P

HEAD = 64
WINDOW = 256
POOL = 4
LLM_D = 8192
BF = jnp.bfloat16
F32 = jnp.float32
VMEM_LIMIT = 48 << 20
SPLIT = 1
CHUNK = 512
LANES = 128


def dot(a, b):
    return jnp.dot(a, b, preferred_element_type=F32)


def dot_nt(a, b):
    return lax.dot_general(a, b, (((1,), (1,)), ((), ())), preferred_element_type=F32)


def dot_tn(a, b):
    return lax.dot_general(a, b, (((0,), (0,)), ((), ())), preferred_element_type=F32)


def swap_tm(block, mask):
    n = lax.axis_size("tm")
    return lax.ppermute(block, "tm", [(i, i ^ mask) for i in range(n)])


def swap_mp(block):
    n = lax.axis_size("mp")
    return lax.ppermute(block, "mp", [(i, n - 1 - i) for i in range(n)])


def to_tm(block, step, cross):
    n, m = lax.axis_size("tm"), lax.axis_size("mp")
    pairs = []
    for i in range(n):
        for c in range(m):
            pairs.append((i * m + c, (i + step) % n * m + (m - 1 - c if cross else c)))
    return lax.ppermute(block, ("tm", "mp"), pairs)


def offsets(masks):
    order = [0]
    for mask in reversed(masks):
        order = order + [k | mask for k in order]
    return order


def tm_bits():
    n = lax.axis_size("tm")
    return [1 << i for i in range(n.bit_length() - 1)]


def group_bits():
    return [bit for bit in tm_bits() if bit != SPLIT]


def gather_doubling(block, masks):
    block = block[None]
    for mask in reversed(masks):
        block = jnp.concatenate([block, swap_tm(block, mask)], axis=0)
    return block


def scatter_halving(blocks, masks, kind):
    total = blocks
    for mask in masks:
        low = total.astype(kind)
        half = low.shape[0] // 2
        total = low[:half].astype(F32) + swap_tm(low[half:], mask).astype(F32)
    return total[0]


def in_turn(got, last):
    return got if last is None else lax.optimization_barrier((got, last))[0]


def scatter_last(parts, masks):
    lows, pairs, last = list(parts), [], None
    for mask in masks:
        for i, low in enumerate(lows):
            half = low.shape[0] // 2
            got = in_turn(swap_tm(low[half:], mask), last)
            if mask == masks[-1]:
                pairs.append((low[0], got[0]))
                last = got
                continue
            lows[i] = last = (low[:half].astype(F32) + got.astype(F32)).astype(BF)
    return pairs


def gather_parts(parts, masks):
    parts, last = [part[None] for part in parts], None
    for mask in reversed(masks):
        for i, part in enumerate(parts):
            got = in_turn(swap_tm(part, mask), last)
            parts[i] = last = jnp.concatenate([part, got], axis=0)
    return parts


def scatter_chunks(chunks, steps, last):
    sums = [lower for lower, _, _ in chunks]
    sends = [upper for _, upper, _ in chunks]
    stage = [0] * len(chunks)
    for i in steps:
        got = in_turn(swap_tm(sends[i], chunks[i][2][stage[i]]), last)
        stage[i] += 1
        total = sums[i].astype(F32) + got.astype(F32)
        if total.shape[0] == 1:
            sums[i] = total[0]
            continue
        low = last = total.astype(BF)
        half = low.shape[0] // 2
        sums[i], sends[i] = low[:half], low[half:]
    return sums


def head_mask(shape, head):
    return lax.broadcasted_iota(jnp.int32, shape, 1) // HEAD == head


def forward_kernel(at, x_ref, wq_ref, wk_ref, wv_ref, wo_ref, *refs):
    normed, qkv, probs, pooled, own_near, own_far, tail_near, tail_far, attn, out = refs
    shift, border, core = at[0], at[1], at[3]
    rows = x_ref.shape[0]
    cols = wq_ref.shape[0]

    @pl.when(pl.program_id(0) == 0)
    def _():
        x = x_ref[...].astype(F32)
        scale = lax.rsqrt(jnp.mean(x * x, axis=-1, keepdims=True) + 1e-05)
        normed[...] = (x * scale).astype(BF)
        out[...] = jnp.zeros_like(out)

    base = normed[...]
    for i, w_ref in enumerate((wq_ref, wk_ref, wv_ref)):
        qkv[i] = dot_nt(base, w_ref[...]).astype(BF)
    windows, heads = range(rows // WINDOW), range(cols // HEAD)
    spans = [pl.ds(w * WINDOW, WINDOW) for w in windows]
    own = [head_mask((WINDOW, cols), h) for h in heads]
    scores = []
    for w in windows:
        q, k = qkv[0, spans[w], :], qkv[1, spans[w], :]
        for h in heads:
            scores.append(dot_nt(jnp.where(own[h], k, jnp.zeros_like(k)), q))
    square = (WINDOW, WINDOW)
    key_at = lax.broadcasted_iota(jnp.int32, square, 0)
    query_at = lax.broadcasted_iota(jnp.int32, square, 1)
    lows = []
    for w in windows:
        edge = border - w * WINDOW
        allowed = (key_at >= edge) == (query_at >= edge)
        for h in heads:
            score = jnp.where(allowed, scores[w * len(heads) + h] * HEAD ** (-0.5), -1e30)
            terms = jnp.exp(score - jnp.max(score, axis=0, keepdims=True))
            low = (terms * (1.0 / jnp.sum(terms, axis=0, keepdims=True))).astype(BF)
            probs[0, w, h] = low
            lows.append(low)
    for w in windows:
        v = qkv[2, spans[w], :]
        attended = None
        for h in heads:
            part = dot_tn(lows[w * len(heads) + h], v)
            attended = part if attended is None else jnp.where(own[h], part, attended)
        attn[spans[w], :] = attended.astype(BF)
    tok_shape = (pooled.shape[0], rows)
    tok_of = (lax.broadcasted_iota(jnp.int32, tok_shape, 1) + shift) // POOL
    member = tok_of == lax.broadcasted_iota(jnp.int32, tok_shape, 0)
    pool = jnp.where(member, 1.0 / POOL, 0.0).astype(BF)
    low = dot(pool, attn[...]).astype(BF)
    pooled[...] = low
    out[...] += dot(low, wo_ref[...])

    @pl.when(pl.program_id(0) == pl.num_programs(0) - 1)
    def _():
        count, half = own_near.shape
        near = pl.ds(pl.multiple_of(core * half, half), half)
        far = pl.ds(pl.multiple_of((1 - core) * half, half), half)
        own_near[...] = out[:count, near]
        own_far[...] = out[:count, far].astype(BF)
        tail_near[...] = out[count:, near].astype(BF)
        tail_far[...] = out[count:, far].astype(BF)


def encoder_forward(x_roll, w_t, weight_out, at, ext_tok):
    rows, width = x_roll.shape
    heads_w = weight_out.shape[0]
    cols = 2 * HEAD
    pairs = heads_w // cols
    windows = rows // WINDOW
    weight = lambda i: pl.BlockSpec((cols, width), lambda p, at: (i * pairs + p, 0))
    own_tok = rows // POOL
    piece = lambda count: pl.BlockSpec((count, width // 2), lambda p, at: (0, 0))
    return pl.pallas_call(
        forward_kernel,
        grid_spec=pltpu.PrefetchScalarGridSpec(
            num_scalar_prefetch=1,
            grid=(pairs,),
            in_specs=[
                pl.BlockSpec((rows, width), lambda p, at: (0, 0)),
                weight(0),
                weight(1),
                weight(2),
                weight(0),
            ],
            out_specs=[
                pl.BlockSpec((rows, width), lambda p, at: (0, 0)),
                pl.BlockSpec((3, rows, cols), lambda p, at: (0, 0, p)),
                pl.BlockSpec((1, windows, 2, WINDOW, WINDOW), lambda p, at: (p, 0, 0, 0, 0)),
                pl.BlockSpec((ext_tok, cols), lambda p, at: (0, p)),
                piece(own_tok),
                piece(own_tok),
                piece(ext_tok - own_tok),
                piece(ext_tok - own_tok),
            ],
            scratch_shapes=[pltpu.VMEM((rows, cols), BF), pltpu.VMEM((ext_tok, width), F32)],
        ),
        out_shape=[
            pltpu.HBM((rows, width), BF),
            pltpu.HBM((3, rows, heads_w), BF),
            pltpu.HBM((pairs, windows, 2, WINDOW, WINDOW), BF),
            pltpu.HBM((ext_tok, heads_w), BF),
            jax.ShapeDtypeStruct((own_tok, width // 2), F32),
            jax.ShapeDtypeStruct((own_tok, width // 2), BF),
            jax.ShapeDtypeStruct((ext_tok - own_tok, width // 2), BF),
            jax.ShapeDtypeStruct((ext_tok - own_tok, width // 2), BF),
        ],
        compiler_params=pltpu.CompilerParams(vmem_limit_bytes=VMEM_LIMIT),
        name="encoder_forward",
    )(at, x_roll, w_t, w_t, w_t, weight_out)


def out_grad_kernel(masks, at, d_ref, wo_ref, pa_ref, d_attn, even, odd, turned):
    me = at[2]
    block = even.shape[1]
    d_ext = d_ref[...]
    d_attn[...] = (dot_nt(d_ext, wo_ref[...]) * (1.0 / POOL)).astype(BF)
    turned[...] = pa_ref[...].T
    for bit, ref in ((0, even), (masks[0], odd)):
        for j, k in enumerate(offsets(masks[1:])):
            start = pl.multiple_of((me ^ (k | bit)) * block, block)
            ref[j] = dot(turned[pl.ds(start, block), :], d_ext).astype(BF)


def out_grad(d_ext, weight_out, pooled_attn, at, masks):
    heads_w, width = weight_out.shape
    n = 2 ** len(masks)
    blocks = jax.ShapeDtypeStruct((n // 2, heads_w // n, width), BF)
    whole = pl.BlockSpec(memory_space=pltpu.VMEM)
    return pl.pallas_call(
        functools.partial(out_grad_kernel, masks),
        in_specs=[pl.BlockSpec(memory_space=pltpu.SMEM), whole, whole, whole],
        out_specs=[whole] * 3,
        out_shape=[jax.ShapeDtypeStruct(pooled_attn.shape, BF), blocks, blocks],
        scratch_shapes=[pltpu.VMEM((heads_w, pooled_attn.shape[0]), BF)],
        compiler_params=pltpu.CompilerParams(vmem_limit_bytes=VMEM_LIMIT),
        name="out_grad",
    )(at, d_ext, weight_out, pooled_attn)


def backward_kernel(masks, at, turned, qkv, probs, d_ref, even, odd, grads):
    shift, me = at[0], at[2]
    rows = turned.shape[1]
    cols = d_ref.shape[1]
    block = even.shape[2]
    tok_shape = (rows, d_ref.shape[0])
    tok_of = (lax.broadcasted_iota(jnp.int32, tok_shape, 0) + shift) // POOL
    member = tok_of == lax.broadcasted_iota(jnp.int32, tok_shape, 1)
    d_rows = dot(jnp.where(member, 1.0, 0.0).astype(BF), d_ref[...]).astype(BF)
    for w in range(rows // WINDOW):
        span = pl.ds(w * WINDOW, WINDOW)
        q, k, v = qkv[0, span, :], qkv[1, span, :], qkv[2, span, :]
        d_out = d_rows[w * WINDOW : (w + 1) * WINDOW]
        none = jnp.zeros_like(q)
        sums = [0.0, 0.0, 0.0]
        for h in range(cols // HEAD):
            own = head_mask(q.shape, h)
            low = probs[0, w, h]
            weight = low.astype(F32)
            d_weight = dot_nt(jnp.where(own, v, none), d_out)
            centre = jnp.sum(weight * d_weight, axis=0, keepdims=True)
            d_score = (weight * (d_weight - centre) * HEAD ** (-0.5)).astype(BF)
            sums[0] += dot_tn(d_score, jnp.where(own, k, none))
            sums[1] += dot(d_score, jnp.where(own, q, none))
            sums[2] += dot(low, jnp.where(own, d_out, none))
        for i in range(3):
            grads[span, i * cols : (i + 1) * cols] = sums[i].astype(BF)
    d_all = grads[...]
    for bit, ref in ((0, even), (masks[0], odd)):
        for j, k in enumerate(offsets(masks[1:])):
            start = pl.multiple_of((me ^ (k | bit)) * block, block)
            term = dot(turned[pl.ds(start, block), :], d_all).astype(BF)
            for i in range(3):
                ref[j, i] = term[:, i * cols : (i + 1) * cols]


def encoder_backward(turned, qkv, probs, d_attn, at, masks, first, count):
    width, rows = turned.shape
    n = 2 ** len(masks)
    cols = 2 * HEAD
    windows = rows // WINDOW
    block = width // n
    out = pl.BlockSpec((n // 2, 3, block, cols), lambda p, at: (0, 0, 0, p))
    shape = jax.ShapeDtypeStruct((n // 2, 3, block, cols * count), BF)
    return pl.pallas_call(
        functools.partial(backward_kernel, masks),
        grid_spec=pltpu.PrefetchScalarGridSpec(
            num_scalar_prefetch=1,
            grid=(count,),
            in_specs=[
                pl.BlockSpec((width, rows), lambda p, at: (0, 0)),
                pl.BlockSpec((3, rows, cols), lambda p, at: (0, 0, p + first)),
                pl.BlockSpec(
                    (1, windows, 2, WINDOW, WINDOW), lambda p, at: (p + first, 0, 0, 0, 0)
                ),
                pl.BlockSpec((d_attn.shape[0], cols), lambda p, at: (0, p + first)),
            ],
            out_specs=[out, out],
            scratch_shapes=[pltpu.VMEM((rows, 3 * cols), BF)],
        ),
        out_shape=[shape, shape],
        compiler_params=pltpu.CompilerParams(vmem_limit_bytes=VMEM_LIMIT),
        name="encoder_backward",
    )(at, turned, qkv, probs, d_attn)


def moves(order, piece):
    count = len(order)
    for e, offset in enumerate(order):
        for b in range(2):
            for i, step in enumerate(order):
                owner = order.index(offset ^ step)
                source_row = ((e * 2 + b) * count + i) * piece
                owner_row = ((owner * count + i) * 2 + b) * piece
                yield source_row, owner_row


def chunks_of(rows):
    return [slice(r, min(r + CHUNK, rows)) for r in range(0, rows, CHUNK)]


def column_starts(order, at, block):
    if order is None:
        return None
    offset = [k | bit for bit in (0, SPLIT) for k in order]
    return [pl.multiple_of((at[2] ^ k) * block, block) for k in offset]


def weight_rows(here, there):
    return jnp.concatenate([w[...].reshape(-1, w.shape[-1]) for w in (here, there)], axis=0)


def both(index, size):
    return (
        pl.ds(pl.multiple_of(index * size, size), size),
        pl.ds(pl.multiple_of((1 - index) * size, size), size),
    )


def kv_columns(low, at, kva, kvb, side, rows):
    feats, cols = kva.shape[0], kvb.shape[2]
    mine, across = both(at[2] % 2, feats)
    span = pl.ds(pl.multiple_of(side * cols, cols), cols)
    part = dot(low[rows, mine], kva[:, span]) + dot(low[rows, across], kvb[side ^ at[4]])
    return part.astype(BF)


def lift_kernel(table, order, at, ta, tb, here, there, gain, kva, kvb, *refs):
    lifted, squares, low, send, tok = refs
    core = at[3]
    near, far = both(core, ta.shape[1])
    piece = ta.shape[0] // len(table) if table else 0
    for source_row, owner_row in table:
        tok[owner_row : owner_row + piece, near] = ta[source_row : source_row + piece]
        tok[owner_row : owner_row + piece, far] = tb[source_row : source_row + piece]
    if not table:
        tok[:, near] = ta[...]
        tok[:, far] = tb[...]
    block = here.shape[1]
    starts = column_starts(order, at, block)
    weight = weight_rows(here, there)
    group_rows = squares.shape[1]
    for rows in chunks_of(tok.shape[0]):
        x = tok[rows]
        if starts:
            x = jnp.concatenate([tok[rows, pl.ds(start, block)] for start in starts], axis=1)
        product = dot(x, weight)
        lifted[rows] = product.astype(BF)
        low[rows] = (product * gain[...]).astype(BF)
        sums = jnp.sum(product * product, axis=1, keepdims=True)
        for first in range(0, rows.stop - rows.start, group_rows):
            column = sums[first : first + group_rows]
            owner = (rows.start + first) // group_rows
            squares[owner : owner + 1] = jnp.broadcast_to(column, (group_rows,) * 2).T[:1]
        send[rows] = kv_columns(low, at, kva, kvb, 1 - core, rows)


def lift(table, order, at, own_tok, ta, tb, here, there, gain, kva, kvb):
    rows, half = ta.shape
    feats, cols = kva.shape[0], kva.shape[1] // 2
    whole = pl.BlockSpec(memory_space=pltpu.VMEM)
    return pl.pallas_call(
        functools.partial(lift_kernel, table, order),
        in_specs=[pl.BlockSpec(memory_space=pltpu.SMEM)] + [whole] * 7,
        out_specs=[whole] * 4,
        out_shape=[
            jax.ShapeDtypeStruct((rows, 2 * feats), BF),
            jax.ShapeDtypeStruct((rows // own_tok, own_tok), F32),
            jax.ShapeDtypeStruct((rows, 2 * feats), BF),
            jax.ShapeDtypeStruct((rows, cols), BF),
        ],
        scratch_shapes=[pltpu.VMEM((rows, 2 * half), BF)],
        compiler_params=pltpu.CompilerParams(vmem_limit_bytes=VMEM_LIMIT),
        name="lift",
    )(at, ta, tb, here, there, gain, kva, kvb)


def keep_kernel(at, low, kva, kvb, keep):
    for rows in chunks_of(low.shape[0]):
        keep[rows] = kv_columns(low, at, kva, kvb, at[3], rows)


def keep_columns(at, low, kva, kvb):
    whole = pl.BlockSpec(memory_space=pltpu.VMEM)
    return pl.pallas_call(
        keep_kernel,
        in_specs=[pl.BlockSpec(memory_space=pltpu.SMEM)] + [whole] * 3,
        out_specs=whole,
        out_shape=jax.ShapeDtypeStruct((low.shape[0], kva.shape[1] // 2), BF),
        compiler_params=pltpu.CompilerParams(vmem_limit_bytes=VMEM_LIMIT),
        name="keep_columns",
    )(at, low, kva, kvb)


def two_parts(column):
    high = column.astype(BF)
    return high, (column - high.astype(F32)).astype(BF)


def finish_kernel(mine, got, squares, d_kv, *refs):
    rows, cols = mine.shape
    kv, load, inner = refs[-3:]
    total = mine[...].astype(F32) + got[...].astype(F32)
    mean = jnp.broadcast_to(squares[...], (rows, rows)).T[:, :1] * (1.0 / LLM_D)
    inv = lax.rsqrt(mean + 1e-05)
    low = (total * inv).astype(BF)
    kv[...] = low
    cot = (low.astype(F32) + d_kv[...].astype(F32)).astype(BF)
    load[:, :cols] = cot
    pull = jnp.sum(cot.astype(F32) * total, axis=1, keepdims=True)
    if len(refs) == 4:
        pull += refs[0][...]
        lane = lax.broadcasted_iota(jnp.int32, (rows, load.shape[1] - cols), 1)
        extra = jnp.zeros(lane.shape, F32)
        for i, part in enumerate(two_parts(inv) + two_parts(pull)):
            extra = jnp.where(lane == i, part.astype(F32), extra)
        load[:, cols:] = extra.astype(BF)
    inner[...] = pull


def finish(mine, got, squares, d_kv, *inner):
    rows, cols = mine.shape
    return pl.pallas_call(
        finish_kernel,
        out_shape=[
            jax.ShapeDtypeStruct((rows, cols), BF),
            jax.ShapeDtypeStruct((rows, cols + LANES * len(inner)), BF),
            jax.ShapeDtypeStruct((rows, 1), F32),
        ],
        compiler_params=pltpu.CompilerParams(vmem_limit_bytes=VMEM_LIMIT),
        name="finish",
    )(mine, got, squares, d_kv, *inner)


def lower_kernel(table, order, at, ca0, ca1, cb0, cb1, here, there, gain, kva, kvb, *refs):
    lifted, send, keep, nat, low = refs
    core, group = at[3], at[4]
    feats, half = kva.shape[0], send.shape[1]
    cols = kva.shape[1] // 2
    near, far = both(core, half)
    mine, across = both(at[2] % 2, feats)
    block = here.shape[1]
    starts = column_starts(order, at, block)
    weight = weight_rows(here, there)
    part_cols = ca0.shape[1]
    piece = ca0.shape[0] // len(table) if table else 0
    for rows in chunks_of(ca0.shape[0]):
        extra = ca1[rows, part_cols:].astype(F32)
        extra_b = cb1[rows, part_cols:].astype(F32)
        inv = extra[:, 0:1] + extra[:, 1:2]
        inner = extra[:, 2:3] + extra[:, 3:4] + extra_b[:, 2:3] + extra_b[:, 3:4]
        pull = inv * inv * inv * inner * (1.0 / LLM_D)
        cots = [
            (jnp.concatenate([c0[rows], c1[rows, :part_cols]], axis=1), side)
            for c0, c1, side in ((ca0, ca1, core), (cb0, cb1, 1 - core))
        ]
        for is_mine, span in ((True, mine), (False, across)):
            d_normed = None
            for cot, side in cots:
                at_side = pl.ds(pl.multiple_of(side * cols, cols), cols)
                part = dot_nt(cot, kva[:, at_side] if is_mine else kvb[side ^ group])
                d_normed = part if d_normed is None else d_normed + part
            low[rows, span] = (
                inv * gain[:, span] * d_normed - lifted[rows, span].astype(F32) * pull
            ).astype(BF)
        d_tok = dot_nt(low[rows], weight).astype(BF)
        if not starts:
            nat[rows] = d_tok
        for i, start in enumerate(starts or ()):
            nat[rows, pl.ds(start, block)] = d_tok[:, i * block : (i + 1) * block]
    for source_row, owner_row in table:
        send[source_row : source_row + piece] = nat[owner_row : owner_row + piece, far]
        keep[source_row : source_row + piece] = nat[owner_row : owner_row + piece, near]
    if not table:
        send[...] = nat[:, far]
        keep[...] = nat[:, near]


def lower(table, order, at, cots, here, there, gain, kva, kvb, lifted):
    rows, width = cots[0].shape[0], lifted.shape[1]
    tok_width = 2 * here.shape[0] * here.shape[1]
    whole = pl.BlockSpec(memory_space=pltpu.VMEM)
    out = jax.ShapeDtypeStruct((rows, tok_width // 2), BF)
    return pl.pallas_call(
        functools.partial(lower_kernel, table, order),
        in_specs=[pl.BlockSpec(memory_space=pltpu.SMEM)] + [whole] * 10,
        out_specs=[whole] * 2,
        out_shape=[out] * 2,
        scratch_shapes=[pltpu.VMEM((rows, tok_width), BF), pltpu.VMEM((rows, width), BF)],
        compiler_params=pltpu.CompilerParams(vmem_limit_bytes=VMEM_LIMIT),
        name="lower",
    )(at, *cots, here, there, gain, kva, kvb, lifted)


def on_device(frames, weight_qkv, weight_out, proj_in, norm_gain, proj_kv, shifts, route, d_kv):
    n = lax.axis_size("tm")
    me = lax.axis_index("tm")
    core = lax.axis_index("mp")
    rows, width = frames.shape
    half_w = width // 2
    shift = shifts[0]
    own_tok = rows // POOL
    tail_tok = WINDOW // POOL
    ext_tok = own_tok + tail_tok
    feats = proj_kv.shape[0]
    kv_half = proj_kv.shape[1] // 2
    piece = own_tok // n

    part = lax.dynamic_slice_in_dim(frames, core * (WINDOW // 2), WINDOW // 2, 0)
    mine = to_tm(part, -1, False)
    w_t = jnp.transpose(weight_qkv, (1, 2, 0)).reshape(-1, width)
    group = lax.axis_index("groups")
    two_groups = lax.axis_size("groups") == 2
    if not two_groups:
        group = group * 0
    proj_kv, part = lax.optimization_barrier((proj_kv, part))
    kv_near = swap_tm(lax.dynamic_slice_in_dim(proj_kv, group * kv_half, kv_half, 1), SPLIT)
    proj_in, w_t = lax.optimization_barrier((proj_in, w_t))

    masks = group_bits()
    order = offsets(masks)
    members = order + [k | SPLIT for k in order]
    count = n // 2
    blocks = []
    for k in order:
        pair = lax.dynamic_slice_in_dim(proj_in, (me ^ k) // 2 * 2 * feats, 2 * feats, 1)
        blocks.append(swap_tm(pair, k) if k else pair)

    other = swap_mp(mine)
    halo = jnp.where(
        core == 0, jnp.concatenate([mine, other], 0), jnp.concatenate([other, mine], 0)
    )
    x_roll = lax.dynamic_slice_in_dim(jnp.concatenate([frames, halo], 0), shift, rows, 0)

    at = jnp.stack([shift, rows * n - shift - me * rows, me, core, group]).astype(jnp.int32)
    normed, qkv, probs, pooled_attn, own_near, own_far, tail_near, tail_far = encoder_forward(
        x_roll, w_t, weight_out, at, ext_tok
    )
    own_far, kv_near = lax.optimization_barrier((own_far, kv_near))
    swap_groups = lambda block: lax.ppermute(block, "groups", [(0, 1), (1, 0)])
    if two_groups:
        kv_far = swap_groups(kv_near)
    else:
        kv_far = swap_tm(proj_kv[:, kv_half:], SPLIT)
    turned = normed.T
    route, norm_gain, d_kv, pooled_attn = lax.optimization_barrier(
        (route, norm_gain, d_kv, pooled_attn)
    )
    gain = lax.dynamic_slice_in_dim(norm_gain, me // 2 * 2 * feats, 2 * feats, 0)
    gain = gain.reshape(1, -1)
    owner_at = (lax.dynamic_index_in_dim(route, me, 0, keepdims=False) ^ me)[None, :]
    sort = owner_at == jnp.array(members, jnp.int32)[:, None]
    sort = jnp.kron(sort.astype(BF), jnp.eye(piece, dtype=BF))
    source_at = jnp.arange(n, dtype=jnp.int32) ^ me
    spread = source_at[:, None] == jnp.array(
        [k | bit for k in order for bit in (0, SPLIT)], jnp.int32
    )
    spread = jnp.kron(spread.astype(BF), jnp.eye(piece, dtype=BF))
    d_kv = dot_tn(spread, d_kv).astype(BF)

    from_core = swap_mp(own_far)
    tail_a = to_tm(tail_near, 1, False)
    tail_b = to_tm(tail_far, 1, True)
    tail_a, tail_b, from_core, blocks = lax.optimization_barrier(
        (tail_a, tail_b, from_core, blocks)
    )
    own_pool = (
        jnp.arange(rows, dtype=jnp.int32)[None, :] // POOL
        == jnp.arange(own_tok, dtype=jnp.int32)[:, None]
    ).astype(BF) * (1.0 / POOL)
    x_mean = dot(own_pool, lax.dynamic_slice_in_dim(frames, core * half_w, half_w, 1))
    pooled = x_mean + own_near + from_core.astype(F32)
    tail = tail_a.astype(F32) + tail_b.astype(F32)
    pooled = jnp.concatenate([pooled[:tail_tok] + tail, pooled[tail_tok:]], 0).astype(BF)

    sorted_tok = dot(sort, pooled).astype(BF).reshape(2, count * piece, half_w)
    handed = swap_tm(sorted_tok[1], SPLIT)
    here = jnp.stack(blocks)
    handed, here = lax.optimization_barrier((handed, here))
    there = swap_tm(here, SPLIT)
    pair_tok = jnp.stack([sorted_tok[0], handed])
    tok_half = gather_doubling(pair_tok, masks[-1:])
    tok_half, turned, d_kv = lax.optimization_barrier((tok_half, turned, d_kv))
    kva, kvb = proj_kv, jnp.stack([kv_near, kv_far])
    at_rows = order
    if width // n % LANES:
        stacked = jnp.concatenate([here, there])
        source = jnp.arange(n, dtype=jnp.int32) ^ me
        found = source[:, None] == jnp.array(members, jnp.int32)[None, :]
        place = jnp.sum(found * jnp.arange(n, dtype=jnp.int32)[None, :], axis=1)
        stacked = jnp.take(stacked, place, axis=0)
        here, there = jnp.split(stacked, 2)
        at_rows = None
    for mask in reversed(masks[:-1]):
        tok_half = jnp.concatenate([tok_half, swap_tm(tok_half, mask)], axis=0)
    tok_half = tok_half.reshape(-1, half_w)
    tok_other = swap_mp(tok_half)
    table = list(moves(order, piece))
    source_rows = np.concatenate([np.arange(r, r + piece) for r, _ in table])
    owner_rows = np.concatenate([np.arange(r, r + piece) for _, r in table])
    by_xla = piece % 16 != 0
    if by_xla:
        at_owner = source_rows[np.argsort(owner_rows)]
        tok_half, tok_other = tok_half[at_owner], tok_other[at_owner]
        table = []
    lifted, squares, scaled, kv_send = lift(
        table, at_rows, at, own_tok, tok_half, tok_other, here, there, gain, kva, kvb
    )
    kv_got = swap_mp(kv_send)
    kv_keep = keep_columns(at, scaled, kva, kvb)
    square_sum = scatter_halving(squares + swap_mp(squares), masks, F32)
    kv_part = (kv_keep.astype(F32) + kv_got.astype(F32)).astype(BF)
    kv_parts = jnp.split(kv_part.reshape(count, own_tok, kv_half), 2, axis=2)
    (mine_a, got_a), (mine_b, got_b) = scatter_last(kv_parts, masks)
    square_sum = square_sum.reshape(1, own_tok)
    d_kv_a, d_kv_b = jnp.split(d_kv, 2, axis=1)
    kv_a, load_a, inner = finish(mine_a, got_a, square_sum, d_kv_a)
    kv_b, load_b, _ = finish(mine_b, got_b, square_sum, d_kv_b, inner)
    kv = dot(spread, jnp.concatenate([kv_a, kv_b], axis=1)).astype(BF)
    loads = gather_parts([load_a, load_b], masks)
    loads = [load.reshape(count * own_tok, -1) for load in loads]
    cots = loads + [swap_mp(load) for load in loads]
    d_send, d_keep = lower(
        table, at_rows, at, cots, here, there, gain, kva, kvb, lifted
    )
    if by_xla:
        at_source = owner_rows[np.argsort(source_rows)]
        d_send, d_keep = d_send[at_source], d_keep[at_source]
    d_part = d_keep.astype(F32) + swap_mp(d_send).astype(F32)
    d_pair = scatter_halving(d_part.reshape(count, 2, count * piece, half_w), masks, BF)
    d_sorted = jnp.concatenate([d_pair[0].astype(BF), swap_tm(d_pair[1].astype(BF), SPLIT)], 0)
    d_half = dot_tn(sort, d_sorted).astype(BF)

    d_other = swap_mp(d_half)
    next_a = to_tm(d_half[:tail_tok], -1, False)
    next_b = to_tm(d_half[:tail_tok], -1, True)
    left = jnp.concatenate([d_half, next_a], 0)
    right = jnp.concatenate([d_other, next_b], 0)
    d_ext = jnp.where(
        core == 0, jnp.concatenate([left, right], 1), jnp.concatenate([right, left], 1)
    )
    bits = tm_bits()
    crossed = [bits[1], bits[0]] + bits[2:]
    d_attn, out_even, out_odd = out_grad(d_ext, weight_out, pooled_attn, at, bits)
    chunks = []
    out_got = swap_tm(out_odd, bits[0])
    for pair, path in enumerate((bits, bits, bits, crossed)):
        if pair == 3:
            at, out_got = lax.optimization_barrier((at, out_got))
        even, odd = encoder_backward(turned, qkv, probs, d_attn, at, path, pair, 1)
        even, odd, at = lax.optimization_barrier((even, odd, at))
        chunks.append((even, odd, path))
    out_low = (out_even.astype(F32) + out_got.astype(F32)).astype(BF)
    out_half = out_low.shape[0] // 2
    chunks.append((out_low[:out_half], out_low[out_half:], bits[1:]))
    steps = [i for t in range(len(bits)) for i, c in enumerate(chunks) if t < len(c[2])]
    if len(bits) == 3:
        steps = [0, 4, 1, 0, 4, 3, 2, 0, 1, 3, 2, 1, 3, 2]
    chunks = scatter_chunks(chunks, steps, even)
    grad_out = chunks.pop()
    grad_qkv = jnp.transpose(jnp.concatenate(chunks, axis=-1), (1, 0, 2))
    return kv, grad_qkv, grad_out


def solution(mesh):
    in_specs = (
        P(("groups", "tm"), None),
        P(None, None, "mp"),
        P("mp", None),
        P("tm", "mp"),
        P("mp"),
        P(("mp", "tm"), None),
        P(),
        P(),
        P(("groups", "tm"), "mp"),
    )
    out_specs = (
        P(("groups", "tm"), "mp"),
        P(("groups", "tm"), None, "mp"),
        P(("groups", "mp", "tm"), None),
    )
    return jax.shard_map(
        on_device, mesh=mesh, in_specs=in_specs, out_specs=out_specs, check_vma=False
    )
```

```python
import functools

import jax
import jax.numpy as jnp
import numpy as np
from jax import lax
from jax.experimental import pallas as pl
from jax.experimental.pallas import tpu as pltpu
from jax.sharding import PartitionSpec as P

HEAD = 64
WINDOW = 256
POOL = 4
LLM_D = 8192
BF = jnp.bfloat16
F32 = jnp.float32
VMEM_LIMIT = 48 << 20
SPLIT = 1
CHUNK = 512
LANES = 128


def dot(a, b):
    return jnp.dot(a, b, preferred_element_type=F32)


def dot_nt(a, b):
    return lax.dot_general(a, b, (((1,), (1,)), ((), ())), preferred_element_type=F32)


def dot_tn(a, b):
    return lax.dot_general(a, b, (((0,), (0,)), ((), ())), preferred_element_type=F32)


def swap_tm(block, mask):
    n = lax.axis_size("tm")
    return lax.ppermute(block, "tm", [(i, i ^ mask) for i in range(n)])


def swap_mp(block):
    n = lax.axis_size("mp")
    return lax.ppermute(block, "mp", [(i, n - 1 - i) for i in range(n)])


def to_tm(block, step, cross):
    n, m = lax.axis_size("tm"), lax.axis_size("mp")
    pairs = []
    for i in range(n):
        for c in range(m):
            pairs.append((i * m + c, (i + step) % n * m + (m - 1 - c if cross else c)))
    return lax.ppermute(block, ("tm", "mp"), pairs)


def offsets(masks):
    order = [0]
    for mask in reversed(masks):
        order = order + [k | mask for k in order]
    return order


def tm_bits():
    n = lax.axis_size("tm")
    return [1 << i for i in range(n.bit_length() - 1)]


def group_bits():
    return [bit for bit in tm_bits() if bit != SPLIT]


def gather_doubling(block, masks):
    block = block[None]
    for mask in reversed(masks):
        block = jnp.concatenate([block, swap_tm(block, mask)], axis=0)
    return block


def scatter_halving(blocks, masks, kind):
    total = blocks
    for mask in masks:
        low = total.astype(kind)
        half = low.shape[0] // 2
        total = low[:half].astype(F32) + swap_tm(low[half:], mask).astype(F32)
    return total[0]


def in_turn(got, last):
    return got if last is None else lax.optimization_barrier((got, last))[0]


def scatter_last(parts, masks):
    lows, pairs, last = list(parts), [], None
    for mask in masks:
        for i, low in enumerate(lows):
            half = low.shape[0] // 2
            got = in_turn(swap_tm(low[half:], mask), last)
            if mask == masks[-1]:
                pairs.append((low[0], got[0]))
                last = got
                continue
            lows[i] = last = (low[:half].astype(F32) + got.astype(F32)).astype(BF)
    return pairs


def gather_parts(parts, masks):
    parts, last = [part[None] for part in parts], None
    for mask in reversed(masks):
        for i, part in enumerate(parts):
            got = in_turn(swap_tm(part, mask), last)
            parts[i] = last = jnp.concatenate([part, got], axis=0)
    return parts


def scatter_chunks(chunks, steps, last):
    sums = [lower for lower, _, _ in chunks]
    sends = [upper for _, upper, _ in chunks]
    stage = [0] * len(chunks)
    for i in steps:
        got = in_turn(swap_tm(sends[i], chunks[i][2][stage[i]]), last)
        stage[i] += 1
        total = sums[i].astype(F32) + got.astype(F32)
        if total.shape[0] == 1:
            sums[i] = total[0]
            continue
        low = last = total.astype(BF)
        half = low.shape[0] // 2
        sums[i], sends[i] = low[:half], low[half:]
    return sums


def head_mask(shape, head):
    return lax.broadcasted_iota(jnp.int32, shape, 1) // HEAD == head


def forward_kernel(at, x_ref, wq_ref, wk_ref, wv_ref, wo_ref, *refs):
    normed, qkv, probs, pooled, own_near, own_far, tail_near, tail_far, attn, out = refs
    shift, border, core = at[0], at[1], at[3]
    rows = x_ref.shape[0]
    cols = wq_ref.shape[0]

    @pl.when(pl.program_id(0) == 0)
    def _():
        x = x_ref[...].astype(F32)
        scale = lax.rsqrt(jnp.mean(x * x, axis=-1, keepdims=True) + 1e-05)
        normed[...] = (x * scale).astype(BF)
        out[...] = jnp.zeros_like(out)

    base = normed[...]
    for i, w_ref in enumerate((wq_ref, wk_ref, wv_ref)):
        qkv[i] = dot_nt(base, w_ref[...]).astype(BF)
    windows, heads = range(rows // WINDOW), range(cols // HEAD)
    spans = [pl.ds(w * WINDOW, WINDOW) for w in windows]
    own = [head_mask((WINDOW, cols), h) for h in heads]
    scores = []
    for w in windows:
        q, k = qkv[0, spans[w], :], qkv[1, spans[w], :]
        for h in heads:
            scores.append(dot_nt(jnp.where(own[h], k, jnp.zeros_like(k)), q))
    square = (WINDOW, WINDOW)
    key_at = lax.broadcasted_iota(jnp.int32, square, 0)
    query_at = lax.broadcasted_iota(jnp.int32, square, 1)
    lows = []
    for w in windows:
        edge = border - w * WINDOW
        allowed = (key_at >= edge) == (query_at >= edge)
        for h in heads:
            score = jnp.where(allowed, scores[w * len(heads) + h] * HEAD ** (-0.5), -1e30)
            terms = jnp.exp(score - jnp.max(score, axis=0, keepdims=True))
            low = (terms * (1.0 / jnp.sum(terms, axis=0, keepdims=True))).astype(BF)
            probs[0, w, h] = low
            lows.append(low)
    for w in windows:
        v = qkv[2, spans[w], :]
        attended = None
        for h in heads:
            part = dot_tn(lows[w * len(heads) + h], v)
            attended = part if attended is None else jnp.where(own[h], part, attended)
        attn[spans[w], :] = attended.astype(BF)
    tok_shape = (pooled.shape[0], rows)
    tok_of = (lax.broadcasted_iota(jnp.int32, tok_shape, 1) + shift) // POOL
    member = tok_of == lax.broadcasted_iota(jnp.int32, tok_shape, 0)
    pool = jnp.where(member, 1.0 / POOL, 0.0).astype(BF)
    low = dot(pool, attn[...]).astype(BF)
    pooled[...] = low
    out[...] += dot(low, wo_ref[...])

    @pl.when(pl.program_id(0) == pl.num_programs(0) - 1)
    def _():
        count, half = own_near.shape
        near = pl.ds(pl.multiple_of(core * half, half), half)
        far = pl.ds(pl.multiple_of((1 - core) * half, half), half)
        own_near[...] = out[:count, near]
        own_far[...] = out[:count, far].astype(BF)
        tail_near[...] = out[count:, near].astype(BF)
        tail_far[...] = out[count:, far].astype(BF)


def encoder_forward(x_roll, w_t, weight_out, at, ext_tok):
    rows, width = x_roll.shape
    heads_w = weight_out.shape[0]
    cols = 2 * HEAD
    pairs = heads_w // cols
    windows = rows // WINDOW
    weight = lambda i: pl.BlockSpec((cols, width), lambda p, at: (i * pairs + p, 0))
    own_tok = rows // POOL
    piece = lambda count: pl.BlockSpec((count, width // 2), lambda p, at: (0, 0))
    return pl.pallas_call(
        forward_kernel,
        grid_spec=pltpu.PrefetchScalarGridSpec(
            num_scalar_prefetch=1,
            grid=(pairs,),
            in_specs=[
                pl.BlockSpec((rows, width), lambda p, at: (0, 0)),
                weight(0),
                weight(1),
                weight(2),
                weight(0),
            ],
            out_specs=[
                pl.BlockSpec((rows, width), lambda p, at: (0, 0)),
                pl.BlockSpec((3, rows, cols), lambda p, at: (0, 0, p)),
                pl.BlockSpec((1, windows, 2, WINDOW, WINDOW), lambda p, at: (p, 0, 0, 0, 0)),
                pl.BlockSpec((ext_tok, cols), lambda p, at: (0, p)),
                piece(own_tok),
                piece(own_tok),
                piece(ext_tok - own_tok),
                piece(ext_tok - own_tok),
            ],
            scratch_shapes=[pltpu.VMEM((rows, cols), BF), pltpu.VMEM((ext_tok, width), F32)],
        ),
        out_shape=[
            pltpu.HBM((rows, width), BF),
            pltpu.HBM((3, rows, heads_w), BF),
            pltpu.HBM((pairs, windows, 2, WINDOW, WINDOW), BF),
            pltpu.HBM((ext_tok, heads_w), BF),
            jax.ShapeDtypeStruct((own_tok, width // 2), F32),
            jax.ShapeDtypeStruct((own_tok, width // 2), BF),
            jax.ShapeDtypeStruct((ext_tok - own_tok, width // 2), BF),
            jax.ShapeDtypeStruct((ext_tok - own_tok, width // 2), BF),
        ],
        compiler_params=pltpu.CompilerParams(vmem_limit_bytes=VMEM_LIMIT),
        name="encoder_forward",
    )(at, x_roll, w_t, w_t, w_t, weight_out)


def out_grad_kernel(masks, at, d_ref, wo_ref, pa_ref, d_attn, even, odd, turned):
    me = at[2]
    block = even.shape[1]
    d_ext = d_ref[...]
    d_attn[...] = (dot_nt(d_ext, wo_ref[...]) * (1.0 / POOL)).astype(BF)
    turned[...] = pa_ref[...].T
    for bit, ref in ((0, even), (masks[0], odd)):
        for j, k in enumerate(offsets(masks[1:])):
            start = pl.multiple_of((me ^ (k | bit)) * block, block)
            ref[j] = dot(turned[pl.ds(start, block), :], d_ext).astype(BF)


def out_grad(d_ext, weight_out, pooled_attn, at, masks):
    heads_w, width = weight_out.shape
    n = 2 ** len(masks)
    blocks = jax.ShapeDtypeStruct((n // 2, heads_w // n, width), BF)
    whole = pl.BlockSpec(memory_space=pltpu.VMEM)
    return pl.pallas_call(
        functools.partial(out_grad_kernel, masks),
        in_specs=[pl.BlockSpec(memory_space=pltpu.SMEM), whole, whole, whole],
        out_specs=[whole] * 3,
        out_shape=[jax.ShapeDtypeStruct(pooled_attn.shape, BF), blocks, blocks],
        scratch_shapes=[pltpu.VMEM((heads_w, pooled_attn.shape[0]), BF)],
        compiler_params=pltpu.CompilerParams(vmem_limit_bytes=VMEM_LIMIT),
        name="out_grad",
    )(at, d_ext, weight_out, pooled_attn)


def backward_kernel(masks, at, turned, qkv, probs, d_ref, even, odd, grads):
    shift, me = at[0], at[2]
    rows = turned.shape[1]
    cols = d_ref.shape[1]
    block = even.shape[2]
    tok_shape = (rows, d_ref.shape[0])
    tok_of = (lax.broadcasted_iota(jnp.int32, tok_shape, 0) + shift) // POOL
    member = tok_of == lax.broadcasted_iota(jnp.int32, tok_shape, 1)
    d_rows = dot(jnp.where(member, 1.0, 0.0).astype(BF), d_ref[...]).astype(BF)
    for w in range(rows // WINDOW):
        span = pl.ds(w * WINDOW, WINDOW)
        q, k, v = qkv[0, span, :], qkv[1, span, :], qkv[2, span, :]
        d_out = d_rows[w * WINDOW : (w + 1) * WINDOW]
        none = jnp.zeros_like(q)
        sums = [0.0, 0.0, 0.0]
        for h in range(cols // HEAD):
            own = head_mask(q.shape, h)
            low = probs[0, w, h]
            weight = low.astype(F32)
            d_weight = dot_nt(jnp.where(own, v, none), d_out)
            centre = jnp.sum(weight * d_weight, axis=0, keepdims=True)
            d_score = (weight * (d_weight - centre) * HEAD ** (-0.5)).astype(BF)
            sums[0] += dot_tn(d_score, jnp.where(own, k, none))
            sums[1] += dot(d_score, jnp.where(own, q, none))
            sums[2] += dot(low, jnp.where(own, d_out, none))
        for i in range(3):
            grads[span, i * cols : (i + 1) * cols] = sums[i].astype(BF)
    d_all = grads[...]
    for bit, ref in ((0, even), (masks[0], odd)):
        for j, k in enumerate(offsets(masks[1:])):
            start = pl.multiple_of((me ^ (k | bit)) * block, block)
            term = dot(turned[pl.ds(start, block), :], d_all).astype(BF)
            for i in range(3):
                ref[j, i] = term[:, i * cols : (i + 1) * cols]


def encoder_backward(turned, qkv, probs, d_attn, at, masks, first, count):
    width, rows = turned.shape
    n = 2 ** len(masks)
    cols = 2 * HEAD
    windows = rows // WINDOW
    block = width // n
    out = pl.BlockSpec((n // 2, 3, block, cols), lambda p, at: (0, 0, 0, p))
    shape = jax.ShapeDtypeStruct((n // 2, 3, block, cols * count), BF)
    return pl.pallas_call(
        functools.partial(backward_kernel, masks),
        grid_spec=pltpu.PrefetchScalarGridSpec(
            num_scalar_prefetch=1,
            grid=(count,),
            in_specs=[
                pl.BlockSpec((width, rows), lambda p, at: (0, 0)),
                pl.BlockSpec((3, rows, cols), lambda p, at: (0, 0, p + first)),
                pl.BlockSpec(
                    (1, windows, 2, WINDOW, WINDOW), lambda p, at: (p + first, 0, 0, 0, 0)
                ),
                pl.BlockSpec((d_attn.shape[0], cols), lambda p, at: (0, p + first)),
            ],
            out_specs=[out, out],
            scratch_shapes=[pltpu.VMEM((rows, 3 * cols), BF)],
        ),
        out_shape=[shape, shape],
        compiler_params=pltpu.CompilerParams(vmem_limit_bytes=VMEM_LIMIT),
        name="encoder_backward",
    )(at, turned, qkv, probs, d_attn)


def moves(order, piece):
    count = len(order)
    for e, offset in enumerate(order):
        for b in range(2):
            for i, step in enumerate(order):
                owner = order.index(offset ^ step)
                source_row = ((e * 2 + b) * count + i) * piece
                owner_row = ((owner * count + i) * 2 + b) * piece
                yield source_row, owner_row


def chunks_of(rows):
    return [slice(r, min(r + CHUNK, rows)) for r in range(0, rows, CHUNK)]


def column_starts(order, at, block):
    if order is None:
        return None
    offset = [k | bit for bit in (0, SPLIT) for k in order]
    return [pl.multiple_of((at[2] ^ k) * block, block) for k in offset]


def weight_rows(here, there):
    return jnp.concatenate([w[...].reshape(-1, w.shape[-1]) for w in (here, there)], axis=0)


def both(index, size):
    return (
        pl.ds(pl.multiple_of(index * size, size), size),
        pl.ds(pl.multiple_of((1 - index) * size, size), size),
    )


def kv_columns(low, at, kva, kvb, side, rows):
    feats, cols = kva.shape[0], kvb.shape[2]
    mine, across = both(at[2] % 2, feats)
    span = pl.ds(pl.multiple_of(side * cols, cols), cols)
    part = dot(low[rows, mine], kva[:, span]) + dot(low[rows, across], kvb[side ^ at[4]])
    return part.astype(BF)


def lift_kernel(table, order, at, ta, tb, here, there, gain, kva, kvb, *refs):
    lifted, squares, low, send, tok = refs
    core = at[3]
    near, far = both(core, ta.shape[1])
    piece = ta.shape[0] // len(table) if table else 0
    for source_row, owner_row in table:
        tok[owner_row : owner_row + piece, near] = ta[source_row : source_row + piece]
        tok[owner_row : owner_row + piece, far] = tb[source_row : source_row + piece]
    if not table:
        tok[:, near] = ta[...]
        tok[:, far] = tb[...]
    block = here.shape[1]
    starts = column_starts(order, at, block)
    weight = weight_rows(here, there)
    group_rows = squares.shape[1]
    for rows in chunks_of(tok.shape[0]):
        x = tok[rows]
        if starts:
            x = jnp.concatenate([tok[rows, pl.ds(start, block)] for start in starts], axis=1)
        product = dot(x, weight)
        lifted[rows] = product.astype(BF)
        low[rows] = (product * gain[...]).astype(BF)
        sums = jnp.sum(product * product, axis=1, keepdims=True)
        for first in range(0, rows.stop - rows.start, group_rows):
            column = sums[first : first + group_rows]
            owner = (rows.start + first) // group_rows
            squares[owner : owner + 1] = jnp.broadcast_to(column, (group_rows,) * 2).T[:1]
        send[rows] = kv_columns(low, at, kva, kvb, 1 - core, rows)


def lift(table, order, at, own_tok, ta, tb, here, there, gain, kva, kvb):
    rows, half = ta.shape
    feats, cols = kva.shape[0], kva.shape[1] // 2
    whole = pl.BlockSpec(memory_space=pltpu.VMEM)
    return pl.pallas_call(
        functools.partial(lift_kernel, table, order),
        in_specs=[pl.BlockSpec(memory_space=pltpu.SMEM)] + [whole] * 7,
        out_specs=[whole] * 4,
        out_shape=[
            jax.ShapeDtypeStruct((rows, 2 * feats), BF),
            jax.ShapeDtypeStruct((rows // own_tok, own_tok), F32),
            jax.ShapeDtypeStruct((rows, 2 * feats), BF),
            jax.ShapeDtypeStruct((rows, cols), BF),
        ],
        scratch_shapes=[pltpu.VMEM((rows, 2 * half), BF)],
        compiler_params=pltpu.CompilerParams(vmem_limit_bytes=VMEM_LIMIT),
        name="lift",
    )(at, ta, tb, here, there, gain, kva, kvb)


def keep_kernel(at, low, kva, kvb, keep):
    for rows in chunks_of(low.shape[0]):
        keep[rows] = kv_columns(low, at, kva, kvb, at[3], rows)


def keep_columns(at, low, kva, kvb):
    whole = pl.BlockSpec(memory_space=pltpu.VMEM)
    return pl.pallas_call(
        keep_kernel,
        in_specs=[pl.BlockSpec(memory_space=pltpu.SMEM)] + [whole] * 3,
        out_specs=whole,
        out_shape=jax.ShapeDtypeStruct((low.shape[0], kva.shape[1] // 2), BF),
        compiler_params=pltpu.CompilerParams(vmem_limit_bytes=VMEM_LIMIT),
        name="keep_columns",
    )(at, low, kva, kvb)


def two_parts(column):
    high = column.astype(BF)
    return high, (column - high.astype(F32)).astype(BF)


def finish_kernel(mine, got, squares, d_kv, *refs):
    rows, cols = mine.shape
    kv, load, inner = refs[-3:]
    total = mine[...].astype(F32) + got[...].astype(F32)
    mean = jnp.broadcast_to(squares[...], (rows, rows)).T[:, :1] * (1.0 / LLM_D)
    inv = lax.rsqrt(mean + 1e-05)
    low = (total * inv).astype(BF)
    kv[...] = low
    cot = (low.astype(F32) + d_kv[...].astype(F32)).astype(BF)
    load[:, :cols] = cot
    pull = jnp.sum(cot.astype(F32) * total, axis=1, keepdims=True)
    if len(refs) == 4:
        pull += refs[0][...]
        lane = lax.broadcasted_iota(jnp.int32, (rows, load.shape[1] - cols), 1)
        extra = jnp.zeros(lane.shape, F32)
        for i, part in enumerate(two_parts(inv) + two_parts(pull)):
            extra = jnp.where(lane == i, part.astype(F32), extra)
        load[:, cols:] = extra.astype(BF)
    inner[...] = pull


def finish(mine, got, squares, d_kv, *inner):
    rows, cols = mine.shape
    return pl.pallas_call(
        finish_kernel,
        out_shape=[
            jax.ShapeDtypeStruct((rows, cols), BF),
            jax.ShapeDtypeStruct((rows, cols + LANES * len(inner)), BF),
            jax.ShapeDtypeStruct((rows, 1), F32),
        ],
        compiler_params=pltpu.CompilerParams(vmem_limit_bytes=VMEM_LIMIT),
        name="finish",
    )(mine, got, squares, d_kv, *inner)


def lower_kernel(table, order, at, ca0, ca1, cb0, cb1, here, there, gain, kva, kvb, *refs):
    lifted, send, keep, nat, low = refs
    core, group = at[3], at[4]
    feats, half = kva.shape[0], send.shape[1]
    cols = kva.shape[1] // 2
    near, far = both(core, half)
    mine, across = both(at[2] % 2, feats)
    block = here.shape[1]
    starts = column_starts(order, at, block)
    weight = weight_rows(here, there)
    part_cols = ca0.shape[1]
    piece = ca0.shape[0] // len(table) if table else 0
    for rows in chunks_of(ca0.shape[0]):
        extra = ca1[rows, part_cols:].astype(F32)
        extra_b = cb1[rows, part_cols:].astype(F32)
        inv = extra[:, 0:1] + extra[:, 1:2]
        inner = extra[:, 2:3] + extra[:, 3:4] + extra_b[:, 2:3] + extra_b[:, 3:4]
        pull = inv * inv * inv * inner * (1.0 / LLM_D)
        cots = [
            (jnp.concatenate([c0[rows], c1[rows, :part_cols]], axis=1), side)
            for c0, c1, side in ((ca0, ca1, core), (cb0, cb1, 1 - core))
        ]
        for is_mine, span in ((True, mine), (False, across)):
            d_normed = None
            for cot, side in cots:
                at_side = pl.ds(pl.multiple_of(side * cols, cols), cols)
                part = dot_nt(cot, kva[:, at_side] if is_mine else kvb[side ^ group])
                d_normed = part if d_normed is None else d_normed + part
            low[rows, span] = (
                inv * gain[:, span] * d_normed - lifted[rows, span].astype(F32) * pull
            ).astype(BF)
        d_tok = dot_nt(low[rows], weight).astype(BF)
        if not starts:
            nat[rows] = d_tok
        for i, start in enumerate(starts or ()):
            nat[rows, pl.ds(start, block)] = d_tok[:, i * block : (i + 1) * block]
    for source_row, owner_row in table:
        send[source_row : source_row + piece] = nat[owner_row : owner_row + piece, far]
        keep[source_row : source_row + piece] = nat[owner_row : owner_row + piece, near]
    if not table:
        send[...] = nat[:, far]
        keep[...] = nat[:, near]


def lower(table, order, at, cots, here, there, gain, kva, kvb, lifted):
    rows, width = cots[0].shape[0], lifted.shape[1]
    tok_width = 2 * here.shape[0] * here.shape[1]
    whole = pl.BlockSpec(memory_space=pltpu.VMEM)
    out = jax.ShapeDtypeStruct((rows, tok_width // 2), BF)
    return pl.pallas_call(
        functools.partial(lower_kernel, table, order),
        in_specs=[pl.BlockSpec(memory_space=pltpu.SMEM)] + [whole] * 10,
        out_specs=[whole] * 2,
        out_shape=[out] * 2,
        scratch_shapes=[pltpu.VMEM((rows, tok_width), BF), pltpu.VMEM((rows, width), BF)],
        compiler_params=pltpu.CompilerParams(vmem_limit_bytes=VMEM_LIMIT),
        name="lower",
    )(at, *cots, here, there, gain, kva, kvb, lifted)


def on_device(frames, weight_qkv, weight_out, proj_in, norm_gain, proj_kv, shifts, route, d_kv):
    n = lax.axis_size("tm")
    me = lax.axis_index("tm")
    core = lax.axis_index("mp")
    rows, width = frames.shape
    half_w = width // 2
    shift = shifts[0]
    own_tok = rows // POOL
    tail_tok = WINDOW // POOL
    ext_tok = own_tok + tail_tok
    feats = proj_kv.shape[0]
    kv_half = proj_kv.shape[1] // 2
    piece = own_tok // n

    part = lax.dynamic_slice_in_dim(frames, core * (WINDOW // 2), WINDOW // 2, 0)
    mine = to_tm(part, -1, False)
    w_t = jnp.transpose(weight_qkv, (1, 2, 0)).reshape(-1, width)
    group = lax.axis_index("groups")
    two_groups = lax.axis_size("groups") == 2
    if not two_groups:
        group = group * 0
    proj_kv, part = lax.optimization_barrier((proj_kv, part))
    kv_near = swap_tm(lax.dynamic_slice_in_dim(proj_kv, group * kv_half, kv_half, 1), SPLIT)
    proj_in, w_t = lax.optimization_barrier((proj_in, w_t))

    masks = group_bits()
    order = offsets(masks)
    members = order + [k | SPLIT for k in order]
    count = n // 2
    blocks = []
    for k in order:
        pair = lax.dynamic_slice_in_dim(proj_in, (me ^ k) // 2 * 2 * feats, 2 * feats, 1)
        blocks.append(swap_tm(pair, k) if k else pair)

    other = swap_mp(mine)
    halo = jnp.where(
        core == 0, jnp.concatenate([mine, other], 0), jnp.concatenate([other, mine], 0)
    )
    x_roll = lax.dynamic_slice_in_dim(jnp.concatenate([frames, halo], 0), shift, rows, 0)

    at = jnp.stack([shift, rows * n - shift - me * rows, me, core, group]).astype(jnp.int32)
    normed, qkv, probs, pooled_attn, own_near, own_far, tail_near, tail_far = encoder_forward(
        x_roll, w_t, weight_out, at, ext_tok
    )
    own_far, kv_near = lax.optimization_barrier((own_far, kv_near))
    swap_groups = lambda block: lax.ppermute(block, "groups", [(0, 1), (1, 0)])
    if two_groups:
        kv_far = swap_groups(kv_near)
    else:
        kv_far = swap_tm(proj_kv[:, kv_half:], SPLIT)
    turned = normed.T
    route, norm_gain, d_kv, pooled_attn = lax.optimization_barrier(
        (route, norm_gain, d_kv, pooled_attn)
    )
    gain = lax.dynamic_slice_in_dim(norm_gain, me // 2 * 2 * feats, 2 * feats, 0)
    gain = gain.reshape(1, -1)
    owner_at = (lax.dynamic_index_in_dim(route, me, 0, keepdims=False) ^ me)[None, :]
    sort = owner_at == jnp.array(members, jnp.int32)[:, None]
    sort = jnp.kron(sort.astype(BF), jnp.eye(piece, dtype=BF))
    source_at = jnp.arange(n, dtype=jnp.int32) ^ me
    spread = source_at[:, None] == jnp.array(
        [k | bit for k in order for bit in (0, SPLIT)], jnp.int32
    )
    spread = jnp.kron(spread.astype(BF), jnp.eye(piece, dtype=BF))
    d_kv = dot_tn(spread, d_kv).astype(BF)

    from_core = swap_mp(own_far)
    tail_a = to_tm(tail_near, 1, False)
    tail_b = to_tm(tail_far, 1, True)
    tail_a, tail_b, from_core, blocks = lax.optimization_barrier(
        (tail_a, tail_b, from_core, blocks)
    )
    own_pool = (
        jnp.arange(rows, dtype=jnp.int32)[None, :] // POOL
        == jnp.arange(own_tok, dtype=jnp.int32)[:, None]
    ).astype(BF) * (1.0 / POOL)
    x_mean = dot(own_pool, lax.dynamic_slice_in_dim(frames, core * half_w, half_w, 1))
    pooled = x_mean + own_near + from_core.astype(F32)
    tail = tail_a.astype(F32) + tail_b.astype(F32)
    pooled = jnp.concatenate([pooled[:tail_tok] + tail, pooled[tail_tok:]], 0).astype(BF)

    sorted_tok = dot(sort, pooled).astype(BF).reshape(2, count * piece, half_w)
    handed = swap_tm(sorted_tok[1], SPLIT)
    here = jnp.stack(blocks)
    handed, here = lax.optimization_barrier((handed, here))
    there = swap_tm(here, SPLIT)
    pair_tok = jnp.stack([sorted_tok[0], handed])
    tok_half = gather_doubling(pair_tok, masks[-1:])
    tok_half, turned, d_kv = lax.optimization_barrier((tok_half, turned, d_kv))
    kva, kvb = proj_kv, jnp.stack([kv_near, kv_far])
    at_rows = order
    if width // n % LANES:
        stacked = jnp.concatenate([here, there])
        source = jnp.arange(n, dtype=jnp.int32) ^ me
        found = source[:, None] == jnp.array(members, jnp.int32)[None, :]
        place = jnp.sum(found * jnp.arange(n, dtype=jnp.int32)[None, :], axis=1)
        stacked = jnp.take(stacked, place, axis=0)
        here, there = jnp.split(stacked, 2)
        at_rows = None
    for mask in reversed(masks[:-1]):
        tok_half = jnp.concatenate([tok_half, swap_tm(tok_half, mask)], axis=0)
    tok_half = tok_half.reshape(-1, half_w)
    tok_other = swap_mp(tok_half)
    table = list(moves(order, piece))
    source_rows = np.concatenate([np.arange(r, r + piece) for r, _ in table])
    owner_rows = np.concatenate([np.arange(r, r + piece) for _, r in table])
    by_xla = piece % 16 != 0
    if by_xla:
        at_owner = source_rows[np.argsort(owner_rows)]
        tok_half, tok_other = tok_half[at_owner], tok_other[at_owner]
        table = []
    lifted, squares, scaled, kv_send = lift(
        table, at_rows, at, own_tok, tok_half, tok_other, here, there, gain, kva, kvb
    )
    kv_got = swap_mp(kv_send)
    kv_keep = keep_columns(at, scaled, kva, kvb)
    square_sum = scatter_halving(squares + swap_mp(squares), masks, F32)
    kv_part = (kv_keep.astype(F32) + kv_got.astype(F32)).astype(BF)
    kv_parts = jnp.split(kv_part.reshape(count, own_tok, kv_half), 2, axis=2)
    (mine_a, got_a), (mine_b, got_b) = scatter_last(kv_parts, masks)
    square_sum = square_sum.reshape(1, own_tok)
    d_kv_a, d_kv_b = jnp.split(d_kv, 2, axis=1)
    kv_a, load_a, inner = finish(mine_a, got_a, square_sum, d_kv_a)
    kv_b, load_b, _ = finish(mine_b, got_b, square_sum, d_kv_b, inner)
    kv = dot(spread, jnp.concatenate([kv_a, kv_b], axis=1)).astype(BF)
    loads = gather_parts([load_a, load_b], masks)
    loads = [load.reshape(count * own_tok, -1) for load in loads]
    cots = loads + [swap_mp(load) for load in loads]
    d_send, d_keep = lower(
        table, at_rows, at, cots, here, there, gain, kva, kvb, lifted
    )
    if by_xla:
        at_source = owner_rows[np.argsort(source_rows)]
        d_send, d_keep = d_send[at_source], d_keep[at_source]
    d_part = d_keep.astype(F32) + swap_mp(d_send).astype(F32)
    d_pair = scatter_halving(d_part.reshape(count, 2, count * piece, half_w), masks, BF)
    d_sorted = jnp.concatenate([d_pair[0].astype(BF), swap_tm(d_pair[1].astype(BF), SPLIT)], 0)
    d_half = dot_tn(sort, d_sorted).astype(BF)

    d_other = swap_mp(d_half)
    next_a = to_tm(d_half[:tail_tok], -1, False)
    next_b = to_tm(d_half[:tail_tok], -1, True)
    left = jnp.concatenate([d_half, next_a], 0)
    right = jnp.concatenate([d_other, next_b], 0)
    d_ext = jnp.where(
        core == 0, jnp.concatenate([left, right], 1), jnp.concatenate([right, left], 1)
    )
    bits = tm_bits()
    crossed = [bits[1], bits[0]] + bits[2:]
    d_attn, out_even, out_odd = out_grad(d_ext, weight_out, pooled_attn, at, bits)
    chunks = []
    out_got = swap_tm(out_odd, bits[0])
    for pair, path in enumerate((bits, bits, bits, crossed)):
        if pair == 3:
            at, out_got = lax.optimization_barrier((at, out_got))
        even, odd = encoder_backward(turned, qkv, probs, d_attn, at, path, pair, 1)
        even, odd, at = lax.optimization_barrier((even, odd, at))
        chunks.append((even, odd, path))
    out_low = (out_even.astype(F32) + out_got.astype(F32)).astype(BF)
    out_half = out_low.shape[0] // 2
    chunks.append((out_low[:out_half], out_low[out_half:], bits[1:]))
    steps = [i for t in range(len(bits)) for i, c in enumerate(chunks) if t < len(c[2])]
    if len(bits) == 3:
        steps = [0, 4, 1, 0, 4, 2, 3, 0, 1, 2, 3, 1, 2, 3]
    chunks = scatter_chunks(chunks, steps, even)
    grad_out = chunks.pop()
    grad_qkv = jnp.transpose(jnp.concatenate(chunks, axis=-1), (1, 0, 2))
    return kv, grad_qkv, grad_out


def solution(mesh):
    in_specs = (
        P(("groups", "tm"), None),
        P(None, None, "mp"),
        P("mp", None),
        P("tm", "mp"),
        P("mp"),
        P(("mp", "tm"), None),
        P(),
        P(),
        P(("groups", "tm"), "mp"),
    )
    out_specs = (
        P(("groups", "tm"), "mp"),
        P(("groups", "tm"), None, "mp"),
        P(("groups", "mp", "tm"), None),
    )
    return jax.shard_map(
        on_device, mesh=mesh, in_specs=in_specs, out_specs=out_specs, check_vma=False
    )
```

```python
import functools

import jax
import jax.numpy as jnp
import numpy as np
from jax import lax
from jax.experimental import pallas as pl
from jax.experimental.pallas import tpu as pltpu
from jax.sharding import PartitionSpec as P

HEAD = 64
WINDOW = 256
POOL = 4
LLM_D = 8192
BF = jnp.bfloat16
F32 = jnp.float32
VMEM_LIMIT = 48 << 20
SPLIT = 1
CHUNK = 512
LANES = 128


def dot(a, b):
    return jnp.dot(a, b, preferred_element_type=F32)


def dot_nt(a, b):
    return lax.dot_general(a, b, (((1,), (1,)), ((), ())), preferred_element_type=F32)


def dot_tn(a, b):
    return lax.dot_general(a, b, (((0,), (0,)), ((), ())), preferred_element_type=F32)


def swap_tm(block, mask):
    n = lax.axis_size("tm")
    return lax.ppermute(block, "tm", [(i, i ^ mask) for i in range(n)])


def swap_mp(block):
    n = lax.axis_size("mp")
    return lax.ppermute(block, "mp", [(i, n - 1 - i) for i in range(n)])


def to_tm(block, step, cross):
    n, m = lax.axis_size("tm"), lax.axis_size("mp")
    pairs = []
    for i in range(n):
        for c in range(m):
            pairs.append((i * m + c, (i + step) % n * m + (m - 1 - c if cross else c)))
    return lax.ppermute(block, ("tm", "mp"), pairs)


def offsets(masks):
    order = [0]
    for mask in reversed(masks):
        order = order + [k | mask for k in order]
    return order


def tm_bits():
    n = lax.axis_size("tm")
    return [1 << i for i in range(n.bit_length() - 1)]


def group_bits():
    return [bit for bit in tm_bits() if bit != SPLIT]


def gather_doubling(block, masks):
    block = block[None]
    for mask in reversed(masks):
        block = jnp.concatenate([block, swap_tm(block, mask)], axis=0)
    return block


def scatter_halving(blocks, masks, kind):
    total = blocks
    for mask in masks:
        low = total.astype(kind)
        half = low.shape[0] // 2
        total = low[:half].astype(F32) + swap_tm(low[half:], mask).astype(F32)
    return total[0]


def in_turn(got, last):
    return got if last is None else lax.optimization_barrier((got, last))[0]


def scatter_last(parts, masks):
    lows, pairs, last = list(parts), [], None
    for mask in masks:
        for i, low in enumerate(lows):
            half = low.shape[0] // 2
            got = in_turn(swap_tm(low[half:], mask), last)
            if mask == masks[-1]:
                pairs.append((low[0], got[0]))
                last = got
                continue
            lows[i] = last = (low[:half].astype(F32) + got.astype(F32)).astype(BF)
    return pairs


def gather_parts(parts, masks):
    parts, last = [part[None] for part in parts], None
    for mask in reversed(masks):
        for i, part in enumerate(parts):
            got = in_turn(swap_tm(part, mask), last)
            parts[i] = last = jnp.concatenate([part, got], axis=0)
    return parts


def scatter_chunks(chunks, steps, last):
    sums = [lower for lower, _, _ in chunks]
    sends = [upper for _, upper, _ in chunks]
    stage = [0] * len(chunks)
    for i in steps:
        got = in_turn(swap_tm(sends[i], chunks[i][2][stage[i]]), last)
        stage[i] += 1
        total = sums[i].astype(F32) + got.astype(F32)
        if total.shape[0] == 1:
            sums[i] = total[0]
            continue
        low = last = total.astype(BF)
        half = low.shape[0] // 2
        sums[i], sends[i] = low[:half], low[half:]
    return sums


def head_mask(shape, head):
    return lax.broadcasted_iota(jnp.int32, shape, 1) // HEAD == head


def forward_kernel(at, x_ref, wq_ref, wk_ref, wv_ref, wo_ref, *refs):
    normed, qkv, probs, pooled, own_near, own_far, tail_near, tail_far, attn, out = refs
    shift, border, core = at[0], at[1], at[3]
    rows = x_ref.shape[0]
    cols = wq_ref.shape[0]

    @pl.when(pl.program_id(0) == 0)
    def _():
        x = x_ref[...].astype(F32)
        scale = lax.rsqrt(jnp.mean(x * x, axis=-1, keepdims=True) + 1e-05)
        normed[...] = (x * scale).astype(BF)
        out[...] = jnp.zeros_like(out)

    base = normed[...]
    for i, w_ref in enumerate((wq_ref, wk_ref, wv_ref)):
        qkv[i] = dot_nt(base, w_ref[...]).astype(BF)
    windows, heads = range(rows // WINDOW), range(cols // HEAD)
    spans = [pl.ds(w * WINDOW, WINDOW) for w in windows]
    own = [head_mask((WINDOW, cols), h) for h in heads]
    scores = []
    for w in windows:
        q, k = qkv[0, spans[w], :], qkv[1, spans[w], :]
        for h in heads:
            scores.append(dot_nt(jnp.where(own[h], k, jnp.zeros_like(k)), q))
    square = (WINDOW, WINDOW)
    key_at = lax.broadcasted_iota(jnp.int32, square, 0)
    query_at = lax.broadcasted_iota(jnp.int32, square, 1)
    lows = []
    for w in windows:
        edge = border - w * WINDOW
        allowed = (key_at >= edge) == (query_at >= edge)
        for h in heads:
            score = jnp.where(allowed, scores[w * len(heads) + h] * HEAD ** (-0.5), -1e30)
            terms = jnp.exp(score - jnp.max(score, axis=0, keepdims=True))
            low = (terms * (1.0 / jnp.sum(terms, axis=0, keepdims=True))).astype(BF)
            probs[0, w, h] = low
            lows.append(low)
    for w in windows:
        v = qkv[2, spans[w], :]
        attended = None
        for h in heads:
            part = dot_tn(lows[w * len(heads) + h], v)
            attended = part if attended is None else jnp.where(own[h], part, attended)
        attn[spans[w], :] = attended.astype(BF)
    tok_shape = (pooled.shape[0], rows)
    tok_of = (lax.broadcasted_iota(jnp.int32, tok_shape, 1) + shift) // POOL
    member = tok_of == lax.broadcasted_iota(jnp.int32, tok_shape, 0)
    pool = jnp.where(member, 1.0 / POOL, 0.0).astype(BF)
    low = dot(pool, attn[...]).astype(BF)
    pooled[...] = low
    out[...] += dot(low, wo_ref[...])

    @pl.when(pl.program_id(0) == pl.num_programs(0) - 1)
    def _():
        count, half = own_near.shape
        near = pl.ds(pl.multiple_of(core * half, half), half)
        far = pl.ds(pl.multiple_of((1 - core) * half, half), half)
        own_near[...] = out[:count, near]
        own_far[...] = out[:count, far].astype(BF)
        tail_near[...] = out[count:, near].astype(BF)
        tail_far[...] = out[count:, far].astype(BF)


def encoder_forward(x_roll, w_t, weight_out, at, ext_tok):
    rows, width = x_roll.shape
    heads_w = weight_out.shape[0]
    cols = 2 * HEAD
    pairs = heads_w // cols
    windows = rows // WINDOW
    weight = lambda i: pl.BlockSpec((cols, width), lambda p, at: (i * pairs + p, 0))
    own_tok = rows // POOL
    piece = lambda count: pl.BlockSpec((count, width // 2), lambda p, at: (0, 0))
    return pl.pallas_call(
        forward_kernel,
        grid_spec=pltpu.PrefetchScalarGridSpec(
            num_scalar_prefetch=1,
            grid=(pairs,),
            in_specs=[
                pl.BlockSpec((rows, width), lambda p, at: (0, 0)),
                weight(0),
                weight(1),
                weight(2),
                weight(0),
            ],
            out_specs=[
                pl.BlockSpec((rows, width), lambda p, at: (0, 0)),
                pl.BlockSpec((3, rows, cols), lambda p, at: (0, 0, p)),
                pl.BlockSpec((1, windows, 2, WINDOW, WINDOW), lambda p, at: (p, 0, 0, 0, 0)),
                pl.BlockSpec((ext_tok, cols), lambda p, at: (0, p)),
                piece(own_tok),
                piece(own_tok),
                piece(ext_tok - own_tok),
                piece(ext_tok - own_tok),
            ],
            scratch_shapes=[pltpu.VMEM((rows, cols), BF), pltpu.VMEM((ext_tok, width), F32)],
        ),
        out_shape=[
            pltpu.HBM((rows, width), BF),
            pltpu.HBM((3, rows, heads_w), BF),
            pltpu.HBM((pairs, windows, 2, WINDOW, WINDOW), BF),
            pltpu.HBM((ext_tok, heads_w), BF),
            jax.ShapeDtypeStruct((own_tok, width // 2), F32),
            jax.ShapeDtypeStruct((own_tok, width // 2), BF),
            jax.ShapeDtypeStruct((ext_tok - own_tok, width // 2), BF),
            jax.ShapeDtypeStruct((ext_tok - own_tok, width // 2), BF),
        ],
        compiler_params=pltpu.CompilerParams(vmem_limit_bytes=VMEM_LIMIT),
        name="encoder_forward",
    )(at, x_roll, w_t, w_t, w_t, weight_out)


def out_grad_kernel(masks, at, d_ref, wo_ref, pa_ref, d_attn, even, odd, turned):
    me = at[2]
    block = even.shape[1]
    d_ext = d_ref[...]
    d_attn[...] = (dot_nt(d_ext, wo_ref[...]) * (1.0 / POOL)).astype(BF)
    turned[...] = pa_ref[...].T
    for bit, ref in ((0, even), (masks[0], odd)):
        for j, k in enumerate(offsets(masks[1:])):
            start = pl.multiple_of((me ^ (k | bit)) * block, block)
            ref[j] = dot(turned[pl.ds(start, block), :], d_ext).astype(BF)


def out_grad(d_ext, weight_out, pooled_attn, at, masks):
    heads_w, width = weight_out.shape
    n = 2 ** len(masks)
    blocks = jax.ShapeDtypeStruct((n // 2, heads_w // n, width), BF)
    whole = pl.BlockSpec(memory_space=pltpu.VMEM)
    return pl.pallas_call(
        functools.partial(out_grad_kernel, masks),
        in_specs=[pl.BlockSpec(memory_space=pltpu.SMEM), whole, whole, whole],
        out_specs=[whole] * 3,
        out_shape=[jax.ShapeDtypeStruct(pooled_attn.shape, BF), blocks, blocks],
        scratch_shapes=[pltpu.VMEM((heads_w, pooled_attn.shape[0]), BF)],
        compiler_params=pltpu.CompilerParams(vmem_limit_bytes=VMEM_LIMIT),
        name="out_grad",
    )(at, d_ext, weight_out, pooled_attn)


def backward_kernel(masks, at, turned, qkv, probs, d_ref, even, odd, grads):
    shift, me = at[0], at[2]
    rows = turned.shape[1]
    cols = d_ref.shape[1]
    block = even.shape[2]
    tok_shape = (rows, d_ref.shape[0])
    tok_of = (lax.broadcasted_iota(jnp.int32, tok_shape, 0) + shift) // POOL
    member = tok_of == lax.broadcasted_iota(jnp.int32, tok_shape, 1)
    d_rows = dot(jnp.where(member, 1.0, 0.0).astype(BF), d_ref[...]).astype(BF)
    for w in range(rows // WINDOW):
        span = pl.ds(w * WINDOW, WINDOW)
        q, k, v = qkv[0, span, :], qkv[1, span, :], qkv[2, span, :]
        d_out = d_rows[w * WINDOW : (w + 1) * WINDOW]
        none = jnp.zeros_like(q)
        sums = [0.0, 0.0, 0.0]
        for h in range(cols // HEAD):
            own = head_mask(q.shape, h)
            low = probs[0, w, h]
            weight = low.astype(F32)
            d_weight = dot_nt(jnp.where(own, v, none), d_out)
            centre = jnp.sum(weight * d_weight, axis=0, keepdims=True)
            d_score = (weight * (d_weight - centre) * HEAD ** (-0.5)).astype(BF)
            sums[0] += dot_tn(d_score, jnp.where(own, k, none))
            sums[1] += dot(d_score, jnp.where(own, q, none))
            sums[2] += dot(low, jnp.where(own, d_out, none))
        for i in range(3):
            grads[span, i * cols : (i + 1) * cols] = sums[i].astype(BF)
    d_all = grads[...]
    for bit, ref in ((0, even), (masks[0], odd)):
        for j, k in enumerate(offsets(masks[1:])):
            start = pl.multiple_of((me ^ (k | bit)) * block, block)
            term = dot(turned[pl.ds(start, block), :], d_all).astype(BF)
            for i in range(3):
                ref[j, i] = term[:, i * cols : (i + 1) * cols]


def encoder_backward(turned, qkv, probs, d_attn, at, masks, first, count):
    width, rows = turned.shape
    n = 2 ** len(masks)
    cols = 2 * HEAD
    windows = rows // WINDOW
    block = width // n
    out = pl.BlockSpec((n // 2, 3, block, cols), lambda p, at: (0, 0, 0, p))
    shape = jax.ShapeDtypeStruct((n // 2, 3, block, cols * count), BF)
    return pl.pallas_call(
        functools.partial(backward_kernel, masks),
        grid_spec=pltpu.PrefetchScalarGridSpec(
            num_scalar_prefetch=1,
            grid=(count,),
            in_specs=[
                pl.BlockSpec((width, rows), lambda p, at: (0, 0)),
                pl.BlockSpec((3, rows, cols), lambda p, at: (0, 0, p + first)),
                pl.BlockSpec(
                    (1, windows, 2, WINDOW, WINDOW), lambda p, at: (p + first, 0, 0, 0, 0)
                ),
                pl.BlockSpec((d_attn.shape[0], cols), lambda p, at: (0, p + first)),
            ],
            out_specs=[out, out],
            scratch_shapes=[pltpu.VMEM((rows, 3 * cols), BF)],
        ),
        out_shape=[shape, shape],
        compiler_params=pltpu.CompilerParams(vmem_limit_bytes=VMEM_LIMIT),
        name="encoder_backward",
    )(at, turned, qkv, probs, d_attn)


def moves(order, piece):
    count = len(order)
    for e, offset in enumerate(order):
        for b in range(2):
            for i, step in enumerate(order):
                owner = order.index(offset ^ step)
                source_row = ((e * 2 + b) * count + i) * piece
                owner_row = ((owner * count + i) * 2 + b) * piece
                yield source_row, owner_row


def chunks_of(rows):
    return [slice(r, min(r + CHUNK, rows)) for r in range(0, rows, CHUNK)]


def column_starts(order, at, block):
    if order is None:
        return None
    offset = [k | bit for bit in (0, SPLIT) for k in order]
    return [pl.multiple_of((at[2] ^ k) * block, block) for k in offset]


def weight_rows(here, there):
    return jnp.concatenate([w[...].reshape(-1, w.shape[-1]) for w in (here, there)], axis=0)


def both(index, size):
    return (
        pl.ds(pl.multiple_of(index * size, size), size),
        pl.ds(pl.multiple_of((1 - index) * size, size), size),
    )


def kv_columns(low, at, kva, kvb, side, rows):
    feats, cols = kva.shape[0], kvb.shape[2]
    mine, across = both(at[2] % 2, feats)
    span = pl.ds(pl.multiple_of(side * cols, cols), cols)
    part = dot(low[rows, mine], kva[:, span]) + dot(low[rows, across], kvb[side ^ at[4]])
    return part.astype(BF)


def lift_kernel(table, order, at, ta, tb, here, there, gain, kva, kvb, *refs):
    lifted, squares, low, send, tok = refs
    core = at[3]
    near, far = both(core, ta.shape[1])
    piece = ta.shape[0] // len(table) if table else 0
    for source_row, owner_row in table:
        tok[owner_row : owner_row + piece, near] = ta[source_row : source_row + piece]
        tok[owner_row : owner_row + piece, far] = tb[source_row : source_row + piece]
    if not table:
        tok[:, near] = ta[...]
        tok[:, far] = tb[...]
    block = here.shape[1]
    starts = column_starts(order, at, block)
    weight = weight_rows(here, there)
    group_rows = squares.shape[1]
    for rows in chunks_of(tok.shape[0]):
        x = tok[rows]
        if starts:
            x = jnp.concatenate([tok[rows, pl.ds(start, block)] for start in starts], axis=1)
        product = dot(x, weight)
        lifted[rows] = product.astype(BF)
        low[rows] = (product * gain[...]).astype(BF)
        sums = jnp.sum(product * product, axis=1, keepdims=True)
        for first in range(0, rows.stop - rows.start, group_rows):
            column = sums[first : first + group_rows]
            owner = (rows.start + first) // group_rows
            squares[owner : owner + 1] = jnp.broadcast_to(column, (group_rows,) * 2).T[:1]
        send[rows] = kv_columns(low, at, kva, kvb, 1 - core, rows)


def lift(table, order, at, own_tok, ta, tb, here, there, gain, kva, kvb):
    rows, half = ta.shape
    feats, cols = kva.shape[0], kva.shape[1] // 2
    whole = pl.BlockSpec(memory_space=pltpu.VMEM)
    return pl.pallas_call(
        functools.partial(lift_kernel, table, order),
        in_specs=[pl.BlockSpec(memory_space=pltpu.SMEM)] + [whole] * 7,
        out_specs=[whole] * 4,
        out_shape=[
            jax.ShapeDtypeStruct((rows, 2 * feats), BF),
            jax.ShapeDtypeStruct((rows // own_tok, own_tok), F32),
            jax.ShapeDtypeStruct((rows, 2 * feats), BF),
            jax.ShapeDtypeStruct((rows, cols), BF),
        ],
        scratch_shapes=[pltpu.VMEM((rows, 2 * half), BF)],
        compiler_params=pltpu.CompilerParams(vmem_limit_bytes=VMEM_LIMIT),
        name="lift",
    )(at, ta, tb, here, there, gain, kva, kvb)


def keep_kernel(at, low, kva, kvb, keep):
    for rows in chunks_of(low.shape[0]):
        keep[rows] = kv_columns(low, at, kva, kvb, at[3], rows)


def keep_columns(at, low, kva, kvb):
    whole = pl.BlockSpec(memory_space=pltpu.VMEM)
    return pl.pallas_call(
        keep_kernel,
        in_specs=[pl.BlockSpec(memory_space=pltpu.SMEM)] + [whole] * 3,
        out_specs=whole,
        out_shape=jax.ShapeDtypeStruct((low.shape[0], kva.shape[1] // 2), BF),
        compiler_params=pltpu.CompilerParams(vmem_limit_bytes=VMEM_LIMIT),
        name="keep_columns",
    )(at, low, kva, kvb)


def two_parts(column):
    high = column.astype(BF)
    return high, (column - high.astype(F32)).astype(BF)


def finish_kernel(mine, got, squares, d_kv, *refs):
    rows, cols = mine.shape
    kv, load, inner = refs[-3:]
    total = mine[...].astype(F32) + got[...].astype(F32)
    mean = jnp.broadcast_to(squares[...], (rows, rows)).T[:, :1] * (1.0 / LLM_D)
    inv = lax.rsqrt(mean + 1e-05)
    low = (total * inv).astype(BF)
    kv[...] = low
    cot = (low.astype(F32) + d_kv[...].astype(F32)).astype(BF)
    load[:, :cols] = cot
    pull = jnp.sum(cot.astype(F32) * total, axis=1, keepdims=True)
    if len(refs) == 4:
        pull += refs[0][...]
        lane = lax.broadcasted_iota(jnp.int32, (rows, load.shape[1] - cols), 1)
        extra = jnp.zeros(lane.shape, F32)
        for i, part in enumerate(two_parts(inv) + two_parts(pull)):
            extra = jnp.where(lane == i, part.astype(F32), extra)
        load[:, cols:] = extra.astype(BF)
    inner[...] = pull


def finish(mine, got, squares, d_kv, *inner):
    rows, cols = mine.shape
    return pl.pallas_call(
        finish_kernel,
        out_shape=[
            jax.ShapeDtypeStruct((rows, cols), BF),
            jax.ShapeDtypeStruct((rows, cols + LANES * len(inner)), BF),
            jax.ShapeDtypeStruct((rows, 1), F32),
        ],
        compiler_params=pltpu.CompilerParams(vmem_limit_bytes=VMEM_LIMIT),
        name="finish",
    )(mine, got, squares, d_kv, *inner)


def lower_kernel(table, order, at, ca0, ca1, cb0, cb1, here, there, gain, kva, kvb, *refs):
    lifted, send, keep, nat, low = refs
    core, group = at[3], at[4]
    feats, half = kva.shape[0], send.shape[1]
    cols = kva.shape[1] // 2
    near, far = both(core, half)
    mine, across = both(at[2] % 2, feats)
    block = here.shape[1]
    starts = column_starts(order, at, block)
    weight = weight_rows(here, there)
    part_cols = ca0.shape[1]
    piece = ca0.shape[0] // len(table) if table else 0
    for rows in chunks_of(ca0.shape[0]):
        extra = ca1[rows, part_cols:].astype(F32)
        extra_b = cb1[rows, part_cols:].astype(F32)
        inv = extra[:, 0:1] + extra[:, 1:2]
        inner = extra[:, 2:3] + extra[:, 3:4] + extra_b[:, 2:3] + extra_b[:, 3:4]
        pull = inv * inv * inv * inner * (1.0 / LLM_D)
        cots = [
            (jnp.concatenate([c0[rows], c1[rows, :part_cols]], axis=1), side)
            for c0, c1, side in ((ca0, ca1, core), (cb0, cb1, 1 - core))
        ]
        for is_mine, span in ((True, mine), (False, across)):
            d_normed = None
            for cot, side in cots:
                at_side = pl.ds(pl.multiple_of(side * cols, cols), cols)
                part = dot_nt(cot, kva[:, at_side] if is_mine else kvb[side ^ group])
                d_normed = part if d_normed is None else d_normed + part
            low[rows, span] = (
                inv * gain[:, span] * d_normed - lifted[rows, span].astype(F32) * pull
            ).astype(BF)
        d_tok = dot_nt(low[rows], weight).astype(BF)
        if not starts:
            nat[rows] = d_tok
        for i, start in enumerate(starts or ()):
            nat[rows, pl.ds(start, block)] = d_tok[:, i * block : (i + 1) * block]
    for source_row, owner_row in table:
        send[source_row : source_row + piece] = nat[owner_row : owner_row + piece, far]
        keep[source_row : source_row + piece] = nat[owner_row : owner_row + piece, near]
    if not table:
        send[...] = nat[:, far]
        keep[...] = nat[:, near]


def lower(table, order, at, cots, here, there, gain, kva, kvb, lifted):
    rows, width = cots[0].shape[0], lifted.shape[1]
    tok_width = 2 * here.shape[0] * here.shape[1]
    whole = pl.BlockSpec(memory_space=pltpu.VMEM)
    out = jax.ShapeDtypeStruct((rows, tok_width // 2), BF)
    return pl.pallas_call(
        functools.partial(lower_kernel, table, order),
        in_specs=[pl.BlockSpec(memory_space=pltpu.SMEM)] + [whole] * 10,
        out_specs=[whole] * 2,
        out_shape=[out] * 2,
        scratch_shapes=[pltpu.VMEM((rows, tok_width), BF), pltpu.VMEM((rows, width), BF)],
        compiler_params=pltpu.CompilerParams(vmem_limit_bytes=VMEM_LIMIT),
        name="lower",
    )(at, *cots, here, there, gain, kva, kvb, lifted)


def on_device(frames, weight_qkv, weight_out, proj_in, norm_gain, proj_kv, shifts, route, d_kv):
    n = lax.axis_size("tm")
    me = lax.axis_index("tm")
    core = lax.axis_index("mp")
    rows, width = frames.shape
    half_w = width // 2
    shift = shifts[0]
    own_tok = rows // POOL
    tail_tok = WINDOW // POOL
    ext_tok = own_tok + tail_tok
    feats = proj_kv.shape[0]
    kv_half = proj_kv.shape[1] // 2
    piece = own_tok // n

    part = lax.dynamic_slice_in_dim(frames, core * (WINDOW // 2), WINDOW // 2, 0)
    mine = to_tm(part, -1, False)
    w_t = jnp.transpose(weight_qkv, (1, 2, 0)).reshape(-1, width)
    group = lax.axis_index("groups")
    two_groups = lax.axis_size("groups") == 2
    if not two_groups:
        group = group * 0
    proj_kv, part = lax.optimization_barrier((proj_kv, part))
    kv_near = swap_tm(lax.dynamic_slice_in_dim(proj_kv, group * kv_half, kv_half, 1), SPLIT)
    proj_in, w_t = lax.optimization_barrier((proj_in, w_t))

    masks = group_bits()
    order = offsets(masks)
    members = order + [k | SPLIT for k in order]
    count = n // 2
    blocks = []
    for k in order:
        pair = lax.dynamic_slice_in_dim(proj_in, (me ^ k) // 2 * 2 * feats, 2 * feats, 1)
        blocks.append(swap_tm(pair, k) if k else pair)

    other = swap_mp(mine)
    halo = jnp.where(
        core == 0, jnp.concatenate([mine, other], 0), jnp.concatenate([other, mine], 0)
    )
    x_roll = lax.dynamic_slice_in_dim(jnp.concatenate([frames, halo], 0), shift, rows, 0)

    at = jnp.stack([shift, rows * n - shift - me * rows, me, core, group]).astype(jnp.int32)
    normed, qkv, probs, pooled_attn, own_near, own_far, tail_near, tail_far = encoder_forward(
        x_roll, w_t, weight_out, at, ext_tok
    )
    own_far, kv_near = lax.optimization_barrier((own_far, kv_near))
    swap_groups = lambda block: lax.ppermute(block, "groups", [(0, 1), (1, 0)])
    if two_groups:
        kv_far = swap_groups(kv_near)
    else:
        kv_far = swap_tm(proj_kv[:, kv_half:], SPLIT)
    turned = normed.T
    route, norm_gain, d_kv, pooled_attn = lax.optimization_barrier(
        (route, norm_gain, d_kv, pooled_attn)
    )
    gain = lax.dynamic_slice_in_dim(norm_gain, me // 2 * 2 * feats, 2 * feats, 0)
    gain = gain.reshape(1, -1)
    owner_at = (lax.dynamic_index_in_dim(route, me, 0, keepdims=False) ^ me)[None, :]
    sort = owner_at == jnp.array(members, jnp.int32)[:, None]
    sort = jnp.kron(sort.astype(BF), jnp.eye(piece, dtype=BF))
    source_at = jnp.arange(n, dtype=jnp.int32) ^ me
    spread = source_at[:, None] == jnp.array(
        [k | bit for k in order for bit in (0, SPLIT)], jnp.int32
    )
    spread = jnp.kron(spread.astype(BF), jnp.eye(piece, dtype=BF))
    d_kv = dot_tn(spread, d_kv).astype(BF)

    from_core = swap_mp(own_far)
    tail_a = to_tm(tail_near, 1, False)
    tail_b = to_tm(tail_far, 1, True)
    tail_a, tail_b, from_core, blocks = lax.optimization_barrier(
        (tail_a, tail_b, from_core, blocks)
    )
    own_pool = (
        jnp.arange(rows, dtype=jnp.int32)[None, :] // POOL
        == jnp.arange(own_tok, dtype=jnp.int32)[:, None]
    ).astype(BF) * (1.0 / POOL)
    x_mean = dot(own_pool, lax.dynamic_slice_in_dim(frames, core * half_w, half_w, 1))
    pooled = x_mean + own_near + from_core.astype(F32)
    tail = tail_a.astype(F32) + tail_b.astype(F32)
    pooled = jnp.concatenate([pooled[:tail_tok] + tail, pooled[tail_tok:]], 0).astype(BF)

    sorted_tok = dot(sort, pooled).astype(BF).reshape(2, count * piece, half_w)
    handed = swap_tm(sorted_tok[1], SPLIT)
    here = jnp.stack(blocks)
    handed, here = lax.optimization_barrier((handed, here))
    there = swap_tm(here, SPLIT)
    pair_tok = jnp.stack([sorted_tok[0], handed])
    tok_half = gather_doubling(pair_tok, masks[-1:])
    tok_half, turned, d_kv = lax.optimization_barrier((tok_half, turned, d_kv))
    kva, kvb = proj_kv, jnp.stack([kv_near, kv_far])
    at_rows = order
    if width // n % LANES:
        stacked = jnp.concatenate([here, there])
        source = jnp.arange(n, dtype=jnp.int32) ^ me
        found = source[:, None] == jnp.array(members, jnp.int32)[None, :]
        place = jnp.sum(found * jnp.arange(n, dtype=jnp.int32)[None, :], axis=1)
        stacked = jnp.take(stacked, place, axis=0)
        here, there = jnp.split(stacked, 2)
        at_rows = None
    for mask in reversed(masks[:-1]):
        tok_half = jnp.concatenate([tok_half, swap_tm(tok_half, mask)], axis=0)
    tok_half = tok_half.reshape(-1, half_w)
    tok_other = swap_mp(tok_half)
    table = list(moves(order, piece))
    source_rows = np.concatenate([np.arange(r, r + piece) for r, _ in table])
    owner_rows = np.concatenate([np.arange(r, r + piece) for _, r in table])
    by_xla = piece % 16 != 0
    if by_xla:
        at_owner = source_rows[np.argsort(owner_rows)]
        tok_half, tok_other = tok_half[at_owner], tok_other[at_owner]
        table = []
    lifted, squares, scaled, kv_send = lift(
        table, at_rows, at, own_tok, tok_half, tok_other, here, there, gain, kva, kvb
    )
    kv_got = swap_mp(kv_send)
    kv_keep = keep_columns(at, scaled, kva, kvb)
    square_sum = scatter_halving(squares + swap_mp(squares), masks, F32)
    kv_part = (kv_keep.astype(F32) + kv_got.astype(F32)).astype(BF)
    kv_parts = jnp.split(kv_part.reshape(count, own_tok, kv_half), 2, axis=2)
    (mine_a, got_a), (mine_b, got_b) = scatter_last(kv_parts, masks)
    square_sum = square_sum.reshape(1, own_tok)
    d_kv_a, d_kv_b = jnp.split(d_kv, 2, axis=1)
    kv_a, load_a, inner = finish(mine_a, got_a, square_sum, d_kv_a)
    kv_b, load_b, _ = finish(mine_b, got_b, square_sum, d_kv_b, inner)
    kv = dot(spread, jnp.concatenate([kv_a, kv_b], axis=1)).astype(BF)
    loads = gather_parts([load_a, load_b], masks)
    loads = [load.reshape(count * own_tok, -1) for load in loads]
    cots = loads + [swap_mp(load) for load in loads]
    d_send, d_keep = lower(
        table, at_rows, at, cots, here, there, gain, kva, kvb, lifted
    )
    if by_xla:
        at_source = owner_rows[np.argsort(source_rows)]
        d_send, d_keep = d_send[at_source], d_keep[at_source]
    d_part = d_keep.astype(F32) + swap_mp(d_send).astype(F32)
    d_pair = scatter_halving(d_part.reshape(count, 2, count * piece, half_w), masks, BF)
    d_sorted = jnp.concatenate([d_pair[0].astype(BF), swap_tm(d_pair[1].astype(BF), SPLIT)], 0)
    d_half = dot_tn(sort, d_sorted).astype(BF)

    d_other = swap_mp(d_half)
    next_a = to_tm(d_half[:tail_tok], -1, False)
    next_b = to_tm(d_half[:tail_tok], -1, True)
    left = jnp.concatenate([d_half, next_a], 0)
    right = jnp.concatenate([d_other, next_b], 0)
    d_ext = jnp.where(
        core == 0, jnp.concatenate([left, right], 1), jnp.concatenate([right, left], 1)
    )
    bits = tm_bits()
    crossed = [bits[1], bits[0]] + bits[2:]
    d_attn, out_even, out_odd = out_grad(d_ext, weight_out, pooled_attn, at, bits)
    chunks = []
    out_got = swap_tm(out_odd, bits[0])
    for pair, path in enumerate((bits, bits, bits, crossed)):
        even, odd = encoder_backward(turned, qkv, probs, d_attn, at, path, pair, 1)
        if pair == 3:
            even, out_got = lax.optimization_barrier((even, out_got))
        even, odd, at = lax.optimization_barrier((even, odd, at))
        chunks.append((even, odd, path))
    out_low = (out_even.astype(F32) + out_got.astype(F32)).astype(BF)
    out_half = out_low.shape[0] // 2
    chunks.append((out_low[:out_half], out_low[out_half:], bits[1:]))
    steps = [i for t in range(len(bits)) for i, c in enumerate(chunks) if t < len(c[2])]
    if len(bits) == 3:
        steps = [0, 4, 1, 0, 4, 3, 2, 0, 1, 3, 2, 1, 3, 2]
    chunks = scatter_chunks(chunks, steps, even)
    grad_out = chunks.pop()
    grad_qkv = jnp.transpose(jnp.concatenate(chunks, axis=-1), (1, 0, 2))
    return kv, grad_qkv, grad_out


def solution(mesh):
    in_specs = (
        P(("groups", "tm"), None),
        P(None, None, "mp"),
        P("mp", None),
        P("tm", "mp"),
        P("mp"),
        P(("mp", "tm"), None),
        P(),
        P(),
        P(("groups", "tm"), "mp"),
    )
    out_specs = (
        P(("groups", "tm"), "mp"),
        P(("groups", "tm"), None, "mp"),
        P(("groups", "mp", "tm"), None),
    )
    return jax.shard_map(
        on_device, mesh=mesh, in_specs=in_specs, out_specs=out_specs, check_vma=False
    )
```
